32 devices in a mesh: patch: 16 (over z, y, x), rep: 2 (over core).
Axes of the slice: x: 2, y: 2, z: 4, core: 2. Of those that a mesh axis runs over, the one named last changes fastest.
Arguments:
- tokens: bfloat16 [8192, 512], P(('patch', 'rep')), may hold values from -6 to 6
- cotangent: bfloat16 [8192, 512], P(('patch', 'rep')), may hold values from -6 to 6
- dest: int32 [8192], P(('patch', 'rep')), may hold values from 0 to 15, as said below
- neighbours: int32 [8192, 16], P(('patch', 'rep')), may hold values from 0 to 8191, as said below
- w_qkv: bfloat16 [512, 1536], replicated, may hold values from -0.25 to 0.25
- w_out: bfloat16 [512, 512], replicated, may hold values from -1 to 1
- w_up: bfloat16 [512, 2048], replicated, may hold values from -0.25 to 0.25
- w_down: bfloat16 [2048, 512], replicated, may hold values from -0.125 to 0.125
- ada_attn: float32 [32, 1024], replicated, may hold values from -0.5 to 0.5
- ada_mlp: float32 [32, 1024], replicated, may hold values from -0.5 to 0.5
- cond: float32 [32], replicated, may hold values from -4 to 4
Outputs:
- output: bfloat16 [8192, 512], P(('patch', 'rep'))
- grad_tokens: bfloat16 [8192, 512], P(('patch', 'rep'))
- grad_qkv: float32 [512, 1536], replicated
- grad_out: float32 [512, 512], replicated
- grad_up: float32 [512, 2048], replicated
- grad_down: float32 [2048, 512], replicated
- grad_ada_attn: float32 [32, 1024], replicated
- grad_ada_mlp: float32 [32, 1024], replicated
- grad_cond: float32 [32], replicated
The draws below stay inside these ranges and needn't reach their ends.
Inputs may be any that keep to these rules, and one draw needn't show every extreme that they name: `dest`: within each index of rep, every patch receives exactly 256 rows; one device sends at most 17 rows to one patch, and each device sends exactly 17 rows to some patch. neighbours[i, 0] = i; every other neighbour of a node in patch q lies in the rows of the same index of rep in patch q - 1, q or q + 1, counted cyclically over 16 patches; positions may repeat.
All inputs are finite; a program needn't handle non-finite values.
Results may differ from the reference program's by a relative error of at most 0.013.
Values may be sent and summed in bfloat16 or wider, within the bound.
A program may use at most 128 MiB of HBM per device.

```python
import jax
import jax.numpy as jnp
from jax import lax

D = 512
H = 4
HD = 128
FF = 2048
CD = 32
NEIGH = 16
TOK_DEV = 256
NODES = 8192
N_PATCH = 16
N_REP = 2


def group_counts(subkey):
    key_first, key_mixer, key_step = jax.random.split(subkey, 3)
    per_pair = TOK_DEV // N_PATCH
    patch_ids = jnp.arange(N_PATCH, dtype=jnp.int32)
    first_perm = jax.random.permutation(key_first, N_PATCH).astype(jnp.int32)
    mixer = jax.random.permutation(key_mixer, N_PATCH).astype(jnp.int32)
    step = jax.random.randint(key_step, (), 1, N_PATCH).astype(jnp.int32)
    inverse = jnp.zeros((N_PATCH,), jnp.int32).at[mixer].set(patch_ids)
    second_perm = first_perm[inverse[(mixer + step) % N_PATCH]]
    more = (first_perm[:, None] == patch_ids[None, :]).astype(jnp.int32)
    fewer = (second_perm[:, None] == patch_ids[None, :]).astype(jnp.int32)
    return per_pair + more - fewer


def draw_dest(key, part):
    key_bits, key_order = jax.random.split(key)
    device_count = N_PATCH * N_REP
    count_keys = jax.random.split(key_bits, N_REP)
    counts = jax.vmap(group_counts)(count_keys)
    bounds = jnp.cumsum(counts, axis=-1)
    positions = jnp.arange(TOK_DEV, dtype=jnp.int32)

    def spread_row(edges):
        return jnp.searchsorted(edges, positions, side='right').astype(jnp.int32)
    sorted_dest = jax.vmap(jax.vmap(spread_row))(bounds)
    arranged = jnp.transpose(sorted_dest, (1, 0, 2))
    subkeys = jax.random.split(key_order, device_count)
    shuffles = jax.vmap(lambda subkey: jax.random.permutation(subkey, TOK_DEV))(subkeys).reshape(N_PATCH, N_REP, TOK_DEV)
    picked = jnp.take_along_axis(arranged, shuffles.astype(jnp.int32), axis=-1)
    return picked.reshape(N_PATCH * N_REP * TOK_DEV).astype(jnp.int32)


def draw_neighbours(key, part):
    key_shift, key_local = jax.random.split(key)
    device_count = N_PATCH * N_REP
    patch_step = jax.random.randint(key_shift, (device_count, TOK_DEV, NEIGH - 1), -1, 2)
    local_row = jax.random.randint(key_local, (device_count, TOK_DEV, NEIGH - 1), 0, TOK_DEV)
    device_ids = jnp.arange(device_count, dtype=jnp.int32)
    patch_ids = device_ids // N_REP
    group_ids = device_ids % N_REP
    other_device = (patch_ids[:, None, None] + patch_step) % N_PATCH * N_REP + group_ids[:, None, None]
    picked = other_device * TOK_DEV + local_row
    itself = (device_ids[:, None] * TOK_DEV + jnp.arange(TOK_DEV, dtype=jnp.int32)[None, :])[..., None]
    return jnp.concatenate([itself, picked], axis=-1).reshape(device_count * TOK_DEV, NEIGH).astype(jnp.int32)


def block_scale(stream_key, extent, shards, smallest, largest):
    gain, own = 1.0, jax.random.fold_in(stream_key, 6)
    for position, shards_of in shards:
        draws = jnp.exp(jax.random.uniform(jax.random.fold_in(own, position), (shards_of,), jnp.float32, smallest / len(shards), largest / len(shards)))
        gain = gain * jnp.repeat(draws, extent[position] // shards_of).reshape([-1 if axis == position else 1 for axis in range(len(extent))])
    return gain


def gaussian(stream_key, dims, scale, limit, cuts=(), kind=jnp.bfloat16):
    values = scale * jax.random.normal(stream_key, dims, jnp.float32)
    if cuts:
        values = values * block_scale(stream_key, dims, cuts, -0.22, 0.18)
    return jnp.clip(values, -limit, limit).astype(kind)


def setup_inputs(seed: int = 0) -> dict:
    streams_of = jax.random.split(jax.random.key(seed), 12)
    tokens = gaussian(streams_of[0], (NODES, D), 1.0, 6.0, ((0, 32),))
    cotangent = gaussian(streams_of[1], (NODES, D), 1.0, 6.0, ((0, 32),))
    dest = draw_dest(jax.random.fold_in(streams_of[11], 71), 0)
    neighbours = draw_neighbours(jax.random.fold_in(streams_of[11], 71), 0)
    w_qkv = gaussian(streams_of[4], (D, 3 * D), D ** -0.5, 0.25)
    w_out = gaussian(streams_of[5], (D, D), (D // NEIGH) ** -0.5, 1.0)
    w_up = gaussian(streams_of[6], (D, FF), D ** -0.5, 0.25)
    w_down = gaussian(streams_of[7], (FF, D), FF ** -0.5, 0.125)
    ada_attn = gaussian(streams_of[8], (CD, 2 * D), (4 * CD) ** -0.5, 0.5, (), jnp.float32)
    ada_mlp = gaussian(streams_of[9], (CD, 2 * D), (4 * CD) ** -0.5, 0.5, (), jnp.float32)
    cond = gaussian(streams_of[10], (CD,), 1.0, 4.0, (), jnp.float32)
    return dict(tokens=tokens, cotangent=cotangent, dest=dest, neighbours=neighbours, w_qkv=w_qkv, w_out=w_out, w_up=w_up, w_down=w_down, ada_attn=ada_attn, ada_mlp=ada_mlp, cond=cond)


@jax.custom_vjp
def low(v):
    return lax.optimization_barrier(v.astype(jnp.bfloat16)).astype(jnp.float32)

@jax.custom_vjp
def low_back(v):
    return v

def low_keep(v):
    return (low(v), None)

def low_pass(kept, grad):
    return (grad,)

def back_keep(v):
    return (v, None)

def back_low(kept, grad):
    return (low(grad),)
low.defvjp(low_keep, low_pass)
low_back.defvjp(back_keep, back_low)

def adaptive_norm(values_in, coeffs):
    centre = lax.optimization_barrier(jnp.mean(values_in, axis=-1, keepdims=True))
    centred = values_in - centre
    spread = lax.optimization_barrier(jnp.mean(centred * centred, axis=-1, keepdims=True))
    return centred * lax.rsqrt(spread + 1e-05) * (1.0 + coeffs[:D]) + coeffs[D:]

def layer_forward(node_band, w_qkv, w_out, w_up, w_down, ada_attn, ada_mlp, cond, order, neighbours):
    highest = lax.Precision.HIGHEST
    coeff_attn = jnp.dot(cond, ada_attn, precision=highest)
    coeff_mlp = jnp.dot(cond, ada_mlp, precision=highest)
    node_rows = node_band[order]
    normed = low(adaptive_norm(node_rows, coeff_attn))
    projected = jnp.dot(normed, w_qkv, precision=highest)
    queries = low_back(low(projected[:, :D]))
    key_rows = low_back(low(projected[:, D:2 * D]))
    value_rows = low_back(low(projected[:, 2 * D:]))
    block_rows = min(4096, NODES)
    score_scale = 1.0 / HD ** 0.5

    def attend(pieces):
        query_block, index_block = pieces
        key_block = key_rows[index_block].reshape(block_rows, NEIGH, H, HD)
        value_block = value_rows[index_block].reshape(block_rows, NEIGH, H, HD)
        scores = jnp.einsum('bhd,bjhd->bhj', query_block.reshape(block_rows, H, HD), key_block, precision=highest) * score_scale
        scores = low_back(scores)
        weights = low(jax.nn.softmax(scores, axis=-1))
        mixture = jnp.einsum('bhj,bjhd->bhd', weights, value_block, precision=highest)
        return mixture.reshape(block_rows, D)
    mixture = lax.map(jax.checkpoint(attend), (queries.reshape(-1, block_rows, D), neighbours.reshape(-1, block_rows, NEIGH)))
    heads_out = low_back(low(mixture.reshape(NODES, D)))
    residual = node_rows + low_back(jnp.dot(heads_out, w_out, precision=highest))
    normed_mlp = low(adaptive_norm(residual, coeff_mlp))
    up_proj = low_back(jnp.dot(normed_mlp, w_up, precision=highest))
    activation = low(jax.nn.silu(up_proj))
    output_rows = residual + jnp.dot(activation, w_down, precision=highest)
    return jnp.zeros_like(output_rows).at[order].set(output_rows)

def reference(tokens, cotangent, dest, neighbours, w_qkv, w_out, w_up, w_down, ada_attn, ada_mlp, cond):
    band_group = jnp.arange(NODES, dtype=jnp.int32) // TOK_DEV % N_REP
    order = jnp.argsort(dest * N_REP + band_group, stable=True).astype(jnp.int32)

    def forward_only(node_band, qkv_weight, out_weight, up_weight, down_weight, attn_map, mlp_map, cond_vec):
        return layer_forward(node_band, qkv_weight, out_weight, up_weight, down_weight, attn_map, mlp_map, cond_vec, order, neighbours)
    result, pullback = jax.vjp(forward_only, tokens.astype(jnp.float32), w_qkv.astype(jnp.float32), w_out.astype(jnp.float32), w_up.astype(jnp.float32), w_down.astype(jnp.float32), ada_attn, ada_mlp, cond)
    grads = pullback(cotangent.astype(jnp.float32))
    return (result.astype(jnp.bfloat16), grads[0].astype(jnp.bfloat16), grads[1], grads[2], grads[3], grads[4], grads[5], grads[6], grads[7])
```

```python
import jax
import jax.numpy as jnp
from jax import lax
from jax.sharding import PartitionSpec as P

H = 4
HD = 128
NORM_EPS = 1e-05
F32 = jnp.float32
BF16 = jnp.bfloat16


def norm_parts(v):
    centred = v - jnp.mean(v, axis=-1, keepdims=True)
    inverse = lax.rsqrt(jnp.mean(centred * centred, axis=-1, keepdims=True) + NORM_EPS)
    return centred * inverse, inverse


def norm_back(grad, plain, inverse, coeffs):
    width = plain.shape[-1]
    scaled = grad * (1.0 + coeffs[:width])
    inner = (
        scaled
        - jnp.mean(scaled, axis=-1, keepdims=True)
        - plain * jnp.mean(scaled * plain, axis=-1, keepdims=True)
    )
    coeff_grad = jnp.concatenate([jnp.sum(grad * plain, axis=0), jnp.sum(grad, axis=0)])
    return inverse * inner, coeff_grad


def dot(a, b, ca, cb):
    return lax.dot_general(a, b, (((ca,), (cb,)), ((), ())), preferred_element_type=F32)


def local(tokens, cotangent, dest, neighbours, w_qkv, w_out, w_up, w_down, ada_attn, ada_mlp, cond):
    highest = lax.Precision.HIGHEST
    rows, width = tokens.shape
    patches = lax.axis_size("patch")
    groups = lax.axis_size("rep")
    cap = rows // patches + 1
    me = lax.axis_index("patch")

    def from_side(array, by):
        return lax.ppermute(array, "patch", [(i, (i + by) % patches) for i in range(patches)])

    hot = dest[None, :] == jnp.arange(patches, dtype=jnp.int32)[:, None]
    hot_low = hot.astype(BF16)
    before = jnp.arange(rows)[:, None] < jnp.arange(rows)[None, :]
    earlier = dot(hot_low, before.astype(BF16), 1, 0)
    rank = jnp.sum(jnp.where(hot, earlier, 0.0), axis=0).astype(jnp.int32)
    slot = dest * cap + rank
    counts = jnp.sum(hot.astype(jnp.int32), axis=1)
    pick_out = (slot[None, :] == jnp.arange(patches * cap, dtype=jnp.int32)[:, None]).astype(BF16)
    outgoing = dot(pick_out, jnp.concatenate([tokens, cotangent], axis=1), 1, 0).astype(BF16)
    arrived = lax.all_to_all(
        outgoing.reshape(patches, cap, 2 * width), "patch", split_axis=0, concat_axis=0, tiled=True
    ).reshape(patches * cap, 2 * width)
    counts_in = lax.all_to_all(counts[:, None], "patch", split_axis=0, concat_axis=0, tiled=True)[:, 0]
    lower = jnp.arange(patches)[:, None] > jnp.arange(patches)[None, :]
    offsets = jnp.sum(jnp.where(lower, counts_in[None, :], 0), axis=1)
    step = jnp.arange(cap, dtype=jnp.int32)
    place = jnp.where(step[None, :] < counts_in[:, None], offsets[:, None] + step[None, :], rows).reshape(-1)
    pick_in = (place[None, :] == jnp.arange(rows, dtype=jnp.int32)[:, None]).astype(BF16)
    placed = dot(pick_in, arrived, 1, 0)
    x = placed[:, :width]
    upstream = placed[:, width:].astype(BF16)

    c1 = jnp.dot(cond, ada_attn, precision=highest)
    c2 = jnp.dot(cond, ada_mlp, precision=highest)
    plain1, inv1 = norm_parts(x)
    normed = (plain1 * (1.0 + c1[:width]) + c1[width:]).astype(BF16)
    sides = jnp.concatenate([from_side(normed, 1), normed, from_side(normed, -1)], axis=0)
    qkv = dot(sides, w_qkv, 1, 0).astype(BF16)
    q_all, k_all, v_all = qkv[:, :width], qkv[:, width : 2 * width], qkv[:, 2 * width :]

    owner = neighbours // (rows * groups)
    within = neighbours % rows
    rel = (owner - me + 1 + patches) % patches
    column = (rel * rows + within).T
    column_before, column_after = from_side(column, 1), from_side(column, -1)
    ids = jnp.arange(3 * rows, dtype=jnp.int32)
    counts_q = jnp.sum((column.T[:, :, None] == ids[None, None, :]).astype(F32), axis=1)
    mine = jnp.arange(rows, dtype=jnp.int32)

    def by_key(col, at):
        return jnp.sum((col[:, None, :] == (mine + at * rows)[None, :, None]).astype(F32), axis=0)

    counts_k = jnp.concatenate([by_key(column_before, 2), by_key(column, 1), by_key(column_after, 0)], axis=1)

    scale = 1.0 / HD**0.5
    q = q_all[rows : 2 * rows]
    k = k_all[rows : 2 * rows]
    v = v_all[rows : 2 * rows]
    weights_all, heads, logs = [], [], []
    for h in range(H):
        c = slice(h * HD, (h + 1) * HD)
        s = dot(q[:, c], k_all[:, c], 1, 1) * scale
        s = jnp.where(counts_q > 0, s, -1e30)
        top = jnp.max(s, axis=-1, keepdims=True)
        e = jnp.exp(s - top)
        total = jnp.sum(e * counts_q, axis=-1, keepdims=True)
        p = e / total
        weights_all.append(p * counts_q)
        heads.append(dot((p * counts_q).astype(BF16), v_all[:, c], 1, 0))
        logs.append(top + jnp.log(total))
    o = jnp.concatenate(heads, axis=1).astype(BF16)

    resid = x + dot(o, w_out, 1, 0)
    plain2, inv2 = norm_parts(resid)
    normed2 = (plain2 * (1.0 + c2[:width]) + c2[width:]).astype(BF16)
    u = dot(normed2, w_up, 1, 0)
    sig = jax.nn.sigmoid(u)
    a = (u * sig).astype(BF16)
    y = (resid + dot(a, w_down, 1, 0)).astype(BF16)
    grad_down = dot(a, upstream, 0, 0)
    ga = dot(upstream, w_down, 1, 1)
    gu = (ga * sig * (1.0 + u * (1.0 - sig))).astype(BF16)
    grad_up = dot(normed2, gu, 0, 0)
    gn2 = dot(gu, w_up, 1, 1)
    gw2, gc2 = norm_back(gn2, plain2, inv2, c2)
    gresid = upstream.astype(F32) + gw2
    gr = gresid.astype(BF16)
    grad_out = dot(o, gr, 0, 0)
    go = dot(gr, w_out, 1, 1).astype(BF16)

    gq, deltas = [], []
    for h in range(H):
        c = slice(h * HD, (h + 1) * HD)
        gp = dot(go[:, c], v_all[:, c], 1, 1)
        delta = jnp.sum(weights_all[h] * gp, axis=-1, keepdims=True)
        gs = (weights_all[h] * (gp - delta)).astype(BF16)
        gq.append(dot(gs, k_all[:, c], 1, 0) * scale)
        deltas.append(delta)
    stats = jnp.concatenate(logs + deltas, axis=1).T
    go_all = jnp.concatenate([from_side(go, 1), go, from_side(go, -1)], axis=0)
    stats_all = jnp.concatenate([from_side(stats, 1), stats, from_side(stats, -1)], axis=1)
    gk, gv = [], []
    for h in range(H):
        c = slice(h * HD, (h + 1) * HD)
        s = dot(k[:, c], q_all[:, c], 1, 1) * scale
        s = jnp.where(counts_k > 0, s, -1e30)
        w = jnp.exp(s - stats_all[h : h + 1]) * counts_k
        gp = dot(v[:, c], go_all[:, c], 1, 1)
        gs = (w * (gp - stats_all[H + h : H + h + 1])).astype(BF16)
        gk.append(dot(gs, q_all[:, c], 1, 0) * scale)
        gv.append(dot(w.astype(BF16), go_all[:, c], 1, 0))
    gqkv = jnp.concatenate(gq + gk + gv, axis=1).astype(BF16)
    grad_qkv = dot(normed, gqkv, 0, 0)
    gn1 = dot(gqkv, w_qkv, 1, 1)
    gw1, gc1 = norm_back(gn1, plain1, inv1, c1)
    gx = (gresid + gw1).astype(BF16)

    both = ("patch", "rep")
    grad_down, grad_up, grad_out, grad_qkv = (
        lax.psum(g.astype(BF16), both).astype(F32) for g in (grad_down, grad_up, grad_out, grad_qkv)
    )
    gc1, gc2 = lax.psum((gc1, gc2), both)
    grad_ada_attn = jnp.outer(cond, gc1)
    grad_ada_mlp = jnp.outer(cond, gc2)
    grad_cond = jnp.dot(ada_attn, gc1, precision=highest) + jnp.dot(ada_mlp, gc2, precision=highest)

    leaving = dot(pick_in, jnp.concatenate([y, gx], axis=1), 0, 0).astype(BF16)
    home = lax.all_to_all(
        leaving.reshape(patches, cap, 2 * width), "patch", split_axis=0, concat_axis=0, tiled=True
    ).reshape(patches * cap, 2 * width)
    band = dot(pick_out, home, 0, 0).astype(BF16)
    return (
        band[:, :width],
        band[:, width:],
        grad_qkv,
        grad_out,
        grad_up,
        grad_down,
        grad_ada_attn,
        grad_ada_mlp,
        grad_cond,
    )


def solution(mesh):
    row = P(("patch", "rep"), None)
    return jax.shard_map(
        local,
        mesh=mesh,
        in_specs=(row, row, P(("patch", "rep")), row) + (P(),) * 7,
        out_specs=(row, row) + (P(),) * 7,
        check_vma=False,
    )
```

```python
import functools
import types

import jax
import jax.numpy as jnp
from jax import lax
from jax.experimental import pallas as pl
from jax.experimental.pallas import tpu as pltpu
from jax.sharding import PartitionSpec as P

H = 4
HD = 128
EPS = 1e-05
F32 = jnp.float32
BF16 = jnp.bfloat16
I32 = jnp.int32
MESH = pl.DeviceIdType.MESH
NN = (((1,), (0,)), ((), ()))
NT = (((1,), (1,)), ((), ()))
TN = (((0,), (0,)), ((), ()))
TILE = 32
PARTS = 4
BLOCK = (512, 256)
MIN_ROWS = 16


def mm(a, b, dims=NN):
    return lax.dot_general(a, b, dims, preferred_element_type=F32)


def iota(shape, axis):
    return lax.broadcasted_iota(I32, shape, axis).astype(F32)


def hot(cond):
    return jnp.where(cond, 1.0, 0.0)


def sizes(patches, rows, width, hidden):
    cap = rows // patches + 1
    block = -(-(cap + 1) // 16) * 16
    bits = patches.bit_length() - 1
    halvings = 0
    while halvings < bits and BLOCK[0] >> (halvings + 1) >= MIN_ROWS:
        halvings += 1
    return types.SimpleNamespace(
        P=patches, R=rows, D=width, FF=hidden, cap=cap, T=block, PT=patches * block, bits=bits, halvings=halvings
    )


def bit_orders(bits):
    first = [(0, 1, 2), (1, 2, 0), (2, 0, 1), (1, 0, 2)]
    return [tuple(b for b in f if b < bits) + tuple(range(3, bits)) for f in first]


def scratch(z, nb):
    R, D, FF, PT = z.R, z.D, z.FF, z.PT
    recv_rows = []
    for k in range(z.bits):
        recv_rows.append(BLOCK[0] >> (min(k + 1, z.halvings)))
    vm, dma = pltpu.VMEM, pltpu.SemaphoreType.DMA
    s = dict(
        tok=vm((R, D), BF16),
        cot=vm((R, D), BF16),
        wqkv=vm((D, 3 * D), BF16),
        wout=vm((D, D), BF16),
        wup=vm((D, FF), BF16),
        wdown=vm((FF, D), BF16),
        ada1=vm((32, 2 * D), F32),
        ada2=vm((32, 2 * D), F32),
        c=vm((16, 2 * D), F32),
        pick=vm((R, PT), BF16),
        place=vm((PT, R), BF16),
        out_t=vm((PT, D), BF16),
        out_c=vm((PT, D), BF16),
        in_t=vm((PT, D), BF16),
        in_c=vm((PT, D), BF16),
        home_y=vm((PT, D), BF16),
        home_g=vm((PT, D), BF16),
        x=vm((R, D), F32),
        plain1=vm((R, D), F32),
        inv1=vm((R, 128), F32),
        plain2=vm((R, D), F32),
        inv2=vm((R, 128), F32),
        resid=vm((R, D), F32),
        gresid=vm((R, D), F32),
        tmp=vm((R, D), F32),
        ups=vm((2, R, D), BF16),
        normed=vm((3, R, D), BF16),
        normed_p=vm((R, D), BF16),
        qkv=vm((3, R, 3 * D), BF16),
        cols=vm((3, nb, R), F32),
        colq=vm((R, nb), F32),
        cq=vm((R, 3 * R), F32),
        ck=vm((3, R, R), F32),
        s=vm((R, 3 * R), F32),
        s2=vm((R, 3 * R), F32),
        w=vm((H, R, 3 * R), F32),
        low=vm((R, 3 * R), BF16),
        low2=vm((R, 3 * R), BF16),
        o=vm((2, R, D), BF16),
        u=vm((R, D), F32),
        ga=vm((R, FF), F32),
        a=vm((R, FF), BF16),
        a_p=vm((R, FF // 2), BF16),
        gu=vm((R, FF), BF16),
        gu_p=vm((R, FF // 2), BF16),
        normed2=vm((2, R, D), BF16),
        gr=vm((R, D), BF16),
        gr_p=vm((R, D // 2), BF16),
        go=vm((3, R, D), BF16),
        stat=vm((R, 128), F32),
        stats=vm((3, 2 * H, R), F32),
        gqkv=vm((R, 3 * D), BF16),
        gqkv_p=vm((R, 3 * D // 2), BF16),
        acc=vm((3, PARTS) + BLOCK, BF16),
        **{f"rcv{k}": vm((3, PARTS, n, BLOCK[1]), BF16) for k, n in enumerate(recv_rows)},
        grads=vm((3, 2, PARTS) + BLOCK, BF16),
        gcs=vm((z.bits + 2, 8, D), F32),
        gcr=vm((z.bits + 1, 8, D), F32),
        load_sem=dma((8,)),
        row_ss=dma((4,)),
        row_rs=dma((4,)),
        own_sem=dma((4,)),
        side_ss=dma((4, 2)),
        side_rs=dma((4, 2)),
        pair_ss=dma((8,)),
        pair_rs=dma((8,)),
        rs_ss=dma((3, z.bits, PARTS)),
        rs_rs=dma((3, z.bits, PARTS)),
        ag_ss=dma((3, z.bits, PARTS)),
        ag_rs=dma((3, z.bits, PARTS)),
        core_ss=dma((3,)),
        core_rs=dma((3,)),
        gc_ss=dma((z.bits + 1,)),
        gc_rs=dma((z.bits + 1,)),
        store_sem=dma((3,)),
    )
    return s


def layer(z, names, *refs):
    n = types.SimpleNamespace(**dict(zip(names, refs, strict=True)))
    Pn, R, D, FF, T, PT, cap = z.P, z.R, z.D, z.FF, z.T, z.PT, z.cap
    me = lax.axis_index("patch")
    rp = lax.axis_index("rep")
    mate = 1 - rp
    nxt = lax.rem(me + 1, Pn)
    prv = lax.rem(me + Pn - 1, Pn)
    started = []

    def tiles(total, fn, init=0, size=TILE):
        return lax.fori_loop(
            0, total // size, lambda i, c: fn(pl.ds(pl.multiple_of(i * size, size), size), c), init
        )

    def load(i, src, dst):
        copy = pltpu.make_async_copy(src, dst, n.load_sem.at[i])
        copy.start()
        return copy

    get_tok = load(0, n.tokens, n.tok)
    get_cot = load(1, n.cotangent, n.cot)
    get_ada1 = load(2, n.ada_attn, n.ada1)
    get_ada2 = load(3, n.ada_mlp, n.ada2)
    get_wqkv = load(4, n.w_qkv, n.wqkv)
    get_wdown = load(5, n.w_down, n.wdown)
    get_wout = load(6, n.w_out, n.wout)
    get_wup = load(7, n.w_up, n.wup)

    barrier = pltpu.get_barrier_semaphore()

    def greet(i, carry):
        pl.semaphore_signal(barrier, inc=1, device_id=(lax.rem(me + i, Pn), rp), device_id_type=MESH)
        return carry

    lax.fori_loop(1, Pn, greet, 0)
    pl.semaphore_signal(barrier, inc=1, device_id=(me, mate), device_id_type=MESH)

    def remote(src, dst, ss, rs, to):
        copy = pltpu.make_async_remote_copy(
            src_ref=src, dst_ref=dst, send_sem=ss, recv_sem=rs, device_id=to, device_id_type=MESH
        )
        copy.start()
        started.append(copy)
        return copy

    def send_rows(i, src, dst):
        def one(j, carry):
            to = lax.rem(me + j, Pn)
            pltpu.make_async_remote_copy(
                src_ref=src.at[pl.ds(pl.multiple_of(to * T, 16), T)],
                dst_ref=dst.at[pl.ds(pl.multiple_of(me * T, 16), T)],
                send_sem=n.row_ss.at[i],
                recv_sem=n.row_rs.at[i],
                device_id=(to, rp),
                device_id_type=MESH,
            ).start()
            return carry

        lax.fori_loop(1, Pn, one, 0)
        mine = pl.ds(pl.multiple_of(me * T, 16), T)
        pltpu.make_async_copy(src.at[mine], dst.at[mine], n.own_sem.at[i]).start()

    def rows_in(i, dst):
        most = dst.at[pl.ds(0, PT - T)]
        pltpu.make_async_copy(most, most, n.row_rs.at[i]).wait()
        mine = dst.at[pl.ds(0, T)]
        pltpu.make_async_copy(mine, mine, n.own_sem.at[i]).wait()

    def rows_gone(i, src):
        most = src.at[pl.ds(0, PT - T)]
        pltpu.make_async_copy(most, most, n.row_ss.at[i]).wait()

    def to_sides(i, ref):
        return (
            remote(ref.at[1], ref.at[0], n.side_ss.at[i, 0], n.side_rs.at[i, 0], (nxt, rp)),
            remote(ref.at[1], ref.at[2], n.side_ss.at[i, 1], n.side_rs.at[i, 1], (prv, rp)),
        )

    def to_mate(i, src, dst):
        return remote(src, dst, n.pair_ss.at[i], n.pair_rs.at[i], (me, mate))

    dest = n.dest[...].astype(F32)
    mine_hot = iota((Pn, R), 0) == dest
    before = hot(iota((R, R), 0) < iota((R, R), 1)).astype(BF16)
    earlier = mm(hot(mine_hot).astype(BF16), before)
    rank = jnp.sum(jnp.where(mine_hot, earlier, 0.0), axis=0, keepdims=True)
    slot = iota((PT, R), 0)
    pick = hot(dest * T + rank == slot)
    sent = jnp.sum(hot(dest * T + cap == slot), axis=1, keepdims=True)
    pick_low = pick.astype(BF16)
    get_tok.wait()
    n.out_t[...] = (mm(pick_low, n.tok[...]) + sent).astype(BF16)
    n.cols[1] = lists_of(z, n.neighbours[...], me)
    pl.semaphore_wait(barrier, Pn)
    send_rows(0, n.out_t, n.in_t)
    side_lists = to_sides(0, n.cols)
    get_cot.wait()
    n.out_c[...] = mm(pick_low, n.cot[...]).astype(BF16)
    send_rows(1, n.out_c, n.in_c)
    n.pick[...] = pick.T.astype(BF16)

    get_ada1.wait()
    get_ada2.wait()
    cond = jnp.broadcast_to(n.cond[...], (8, n.cond.shape[1]))
    n.c[0:8] = jnp.dot(cond, n.ada1[...], precision=lax.Precision.HIGHEST, preferred_element_type=F32)
    n.c[8:16] = jnp.dot(cond, n.ada2[...], precision=lax.Precision.HIGHEST, preferred_element_type=F32)
    n.colq[...] = n.cols[1].T
    lists = n.cols.shape[1]

    def count_q(t, carry):
        ids = iota((TILE, 3 * R), 1)
        col = n.colq[t, :]
        total = jnp.zeros((TILE, 3 * R), F32)
        for j in range(lists):
            total = total + hot(col[:, j : j + 1] == ids)
        n.cq[t, :] = total
        return carry

    tiles(R, count_q)

    def count_k(side, base):
        def one(t, carry):
            ids = iota((TILE, R), 0) + (t.start + base).astype(F32)
            total = jnp.zeros((TILE, R), F32)
            for j in range(lists):
                total = total + hot(n.cols[side, j : j + 1, :] == ids)
            n.ck[side, t, :] = total
            return carry

        tiles(R, one)

    count_k(1, R)
    for lists_copy in side_lists:
        lists_copy.wait_recv()
    count_k(0, 2 * R)
    count_k(2, 0)

    src_c = jnp.floor((iota((PT, 1), 0) + 0.5) * (1.0 / T))
    src_r = jnp.floor((iota((1, PT), 1) + 0.5) * (1.0 / T))
    step_c = iota((PT, 1), 0) - src_c * T
    step_r = iota((1, PT), 1) - src_r * T
    counting = step_r == cap
    lower = hot((src_r < src_c) & counting).astype(BF16)
    same = hot((src_r == src_c) & counting).astype(BF16)
    rows_in(0, n.in_t)
    first = n.in_t[:, 0:128]
    offset = mm(lower, first)[:, 0:1]
    count = mm(same, first)[:, 0:1]
    position = jnp.where(step_c < count, offset + step_c, -1.0)
    place = hot(position == iota((PT, R), 1))
    n.place[...] = place.astype(BF16)
    place_t = place.T.astype(BF16)
    n.x[...] = mm(place_t, n.in_t[...])

    def norm(src, coeffs, plain_ref, inv_ref, out):
        def one(t, carry):
            v = src[t, :]
            centred = v - jnp.sum(v, axis=-1, keepdims=True) * (1.0 / D)
            inverse = lax.rsqrt(jnp.sum(centred * centred, axis=-1, keepdims=True) * (1.0 / D) + EPS)
            plain = centred * inverse
            plain_ref[t, :] = plain
            inv_ref[t, :] = jnp.broadcast_to(inverse, (TILE, 128))
            out[t, :] = (plain * (1.0 + n.c[coeffs : coeffs + 1, :D]) + n.c[coeffs : coeffs + 1, D:]).astype(BF16)
            return carry

        tiles(R, one)

    def norm_back(grad, coeffs, plain_ref, inv_ref, finish):
        def one(t, carry):
            g = grad[t, :]
            plain = plain_ref[t, :]
            scaled = g * (1.0 + n.c[coeffs : coeffs + 1, :D])
            mean = jnp.sum(scaled, axis=-1, keepdims=True) * (1.0 / D)
            along = jnp.sum(scaled * plain, axis=-1, keepdims=True) * (1.0 / D)
            finish(t, inv_ref[t, 0:1] * (scaled - mean - plain * along))
            return (
                carry[0] + jnp.sum(g * plain, axis=0, keepdims=True),
                carry[1] + jnp.sum(g, axis=0, keepdims=True),
            )

        zero = jnp.zeros((1, D), F32)
        return tiles(R, one, (zero, zero))

    norm(n.x, 0, n.plain1, n.inv1, n.normed.at[1])
    side_normed = to_sides(1, n.normed)
    mate_normed = to_mate(0, n.normed.at[1], n.normed_p)
    get_wqkv.wait()

    def project(side):
        for j in range(3):
            c = slice(j * D, (j + 1) * D)
            n.qkv[side, :, c] = mm(n.normed[side], n.wqkv[:, c]).astype(BF16)

    project(1)
    rows_in(1, n.in_c)
    n.ups[0] = mm(place_t, n.in_c[...]).astype(BF16)
    mate_ups = to_mate(1, n.ups.at[0], n.ups.at[1])
    get_wdown.wait()
    for j in range(FF // D):
        c = slice(j * D, (j + 1) * D)
        n.ga[:, c] = mm(n.ups[0], n.wdown[c, :], NT)
    side_normed[0].wait_recv()
    project(0)
    side_normed[1].wait_recv()
    project(2)

    scale = 1.0 / HD**0.5

    def part(which, h):
        return slice(which * D + h * HD, which * D + (h + 1) * HD)

    for h in range(H):
        for side in range(3):
            n.s[:, side * R : (side + 1) * R] = mm(n.qkv[1, :, part(0, h)], n.qkv[side, :, part(1, h)], NT)

        def soft(t, carry, h=h):
            counts = n.cq[t, :]
            s = jnp.where(counts > 0.0, n.s[t, :] * scale, -1e30)
            top = jnp.max(s, axis=-1, keepdims=True)
            e = jnp.exp(s - top) * counts
            total = jnp.sum(e, axis=-1, keepdims=True)
            w = e * (1.0 / total)
            n.w[h, t, :] = w
            n.low[t, :] = w.astype(BF16)
            n.stat[t, h : h + 1] = top + jnp.log(total)
            return carry

        tiles(R, soft)
        mixed = jnp.zeros((R, HD), F32)
        for side in range(3):
            mixed = mixed + mm(n.low[:, side * R : (side + 1) * R], n.qkv[side, :, part(2, h)])
        n.o[0, :, h * HD : (h + 1) * HD] = mixed.astype(BF16)
    mate_o = to_mate(2, n.o.at[0], n.o.at[1])

    get_wout.wait()
    n.resid[...] = n.x[...] + mm(n.o[0], n.wout[...])
    norm(n.resid, 8, n.plain2, n.inv2, n.normed2.at[0])
    mate_normed2 = to_mate(3, n.normed2.at[0], n.normed2.at[1])
    get_wup.wait()
    half = FF // 2
    for j in range(FF // D):
        c = slice(j * D, (j + 1) * D)
        n.u[...] = mm(n.normed2[0], n.wup[:, c])

        def gate(t, carry, c=c):
            u = n.u[t, :]
            sig = 1.0 / (1.0 + jnp.exp(-u))
            n.a[t, c] = (u * sig).astype(BF16)
            n.gu[t, c] = (n.ga[t, c] * sig * (1.0 + u * (1.0 - sig))).astype(BF16)
            return carry

        tiles(R, gate)
    theirs = pl.ds(pl.multiple_of(mate * half, 128), half)
    ours = pl.ds(pl.multiple_of(rp * half, 128), half)
    mate_a = to_mate(4, n.a.at[:, theirs], n.a_p)
    mate_gu = to_mate(5, n.gu.at[:, theirs], n.gu_p)
    n.tmp[...] = mm(n.gu[...], n.wup[...], NT)

    def keep2(t, gw):
        total = n.ups[0, t, :].astype(F32) + gw
        n.gresid[t, :] = total
        n.gr[t, :] = total.astype(BF16)

    gc2 = norm_back(n.tmp, 8, n.plain2, n.inv2, keep2)
    n.go[1] = mm(n.gr[...], n.wout[...], NT).astype(BF16)
    side_go = to_sides(2, n.go)
    quarter = D // 2
    mate_gr = to_mate(6, n.gr.at[:, pl.ds(pl.multiple_of(mate * quarter, 128), quarter)], n.gr_p)
    y = (n.resid[...] + mm(n.a[...], n.wdown[...])).astype(BF16)
    rows_gone(0, n.out_t)
    n.out_t[...] = mm(n.place[...], y).astype(BF16)
    send_rows(2, n.out_t, n.home_y)

    orders = bit_orders(z.bits)

    def start_of(p, k):
        at = 0
        for i in range(k):
            at = at + ((me >> orders[p][i]) & 1) * (BLOCK[0] >> (i + 1))
        return at

    def span(p, k):
        k = min(k, z.halvings)
        rows = BLOCK[0] >> k
        at = start_of(p, k)
        return pl.ds(pl.multiple_of(at, rows) if k else 0, rows)

    def partner(p, k):
        return (me ^ (1 << orders[p][k]), rp)

    live = {}

    def reduce_start(c, k):
        for p in range(PARTS):
            if k < z.halvings:
                rows = BLOCK[0] >> (k + 1)
                gone = (1 - ((me >> orders[p][k]) & 1)) * rows + start_of(p, k)
                src = n.acc.at[c, p, pl.ds(pl.multiple_of(gone, rows), rows)]
            else:
                src = n.acc.at[c, p, span(p, k)]
            dst = getattr(n, f"rcv{k}").at[c, p]
            live[c, k, p] = remote(src, dst, n.rs_ss.at[c, k, p], n.rs_rs.at[c, k, p], partner(p, k))

    def reduce_end(c, k):
        for p in range(PARTS):
            copy = live[c, k, p]
            copy.wait_recv()
            if k >= z.halvings:
                copy.wait_send()
                started[:] = [s for s in started if s is not copy]
            kept = span(p, k + 1)
            n.acc[c, p, kept] = (n.acc[c, p, kept].astype(F32) + getattr(n, f"rcv{k}")[c, p].astype(F32)).astype(BF16)

    def gather_start(c, k):
        for p in range(PARTS):
            if k == z.halvings - 1:
                kept = span(p, k + 1)
                n.grads[c, rp, p, kept] = n.acc[c, p, kept]
            ref = n.grads.at[c, rp, p, span(p, k + 1)]
            live[c, -k - 1, p] = remote(ref, ref, n.ag_ss.at[c, k, p], n.ag_rs.at[c, k, p], partner(p, k))

    def gather_end(c, k):
        for p in range(PARTS):
            live[c, -k - 1, p].wait_recv()

    def core_start(c):
        ref = n.grads.at[c, rp]
        live[c, "core"] = remote(ref, ref, n.core_ss.at[c], n.core_rs.at[c], (me, mate))

    def core_end(c):
        live[c, "core"].wait_recv()
        pltpu.make_async_copy(n.grads.at[c], n.grads_out.at[c], n.store_sem.at[c]).start()

    plan = {}
    for c in range(3):
        steps = [(reduce_start, (c, 0))]
        for k in range(z.bits):
            steps.append((reduce_end, (c, k)))
            if k + 1 < z.bits:
                steps.append((reduce_start, (c, k + 1)))
        for k in range(z.halvings - 1, -1, -1):
            steps.append((gather_start, (c, k)))
            steps.append((gather_end, (c, k)))
        steps.append((core_start, (c,)))
        steps.append((core_end, (c,)))
        plan[c] = steps

    def advance(c, count=None):
        while plan[c] and (count is None or count > 0):
            fn, args = plan[c].pop(0)
            fn(*args)
            if fn in (reduce_start, gather_start, core_start) and count is not None:
                count -= 1

    mate_ups.wait_recv()
    mate_a.wait_recv()
    for j in range(2):
        r = pl.ds(pl.multiple_of(rp * half + j * BLOCK[0], 128), BLOCK[0])
        for i in range(2):
            c = slice(i * BLOCK[1], (i + 1) * BLOCK[1])
            total = mm(n.a[:, r], n.ups[0, :, c], TN) + mm(n.a_p[:, j * BLOCK[0] : (j + 1) * BLOCK[0]], n.ups[1, :, c], TN)
            n.acc[0, 2 * j + i] = total.astype(BF16)
    advance(0, 1)
    mate_normed2.wait_recv()
    mate_gu.wait_recv()
    for p in range(PARTS):
        c = pl.ds(pl.multiple_of(rp * half + p * BLOCK[1], 128), BLOCK[1])
        d = slice(p * BLOCK[1], (p + 1) * BLOCK[1])
        n.acc[1, p] = (mm(n.normed2[0], n.gu[:, c], TN) + mm(n.normed2[1], n.gu_p[:, d], TN)).astype(BF16)
    advance(1, 1)

    for h in range(H):
        head = slice(h * HD, (h + 1) * HD)
        for side in range(3):
            n.s[:, side * R : (side + 1) * R] = mm(n.go[1, :, head], n.qkv[side, :, part(2, h)], NT)

        def soft_back(t, carry, h=h):
            w = n.w[h, t, :]
            gp = n.s[t, :]
            delta = jnp.sum(w * gp, axis=-1, keepdims=True)
            n.low[t, :] = (w * (gp - delta)).astype(BF16)
            n.stat[t, H + h : H + h + 1] = delta
            return carry

        tiles(R, soft_back)
        total = jnp.zeros((R, HD), F32)
        for side in range(3):
            total = total + mm(n.low[:, side * R : (side + 1) * R], n.qkv[side, :, part(1, h)])
        n.gqkv[:, part(0, h)] = (total * scale).astype(BF16)
    n.stats[1] = n.stat[...].T[0 : 2 * H]
    side_stats = to_sides(3, n.stats)
    advance(0, 1)
    advance(1, 1)

    for i in range(2):
        side_go[i].wait_recv()
        side_stats[i].wait_recv()
    for h in range(H):
        head = slice(h * HD, (h + 1) * HD)
        for side in range(3):
            span_q = slice(side * R, (side + 1) * R)
            n.s[:, span_q] = mm(n.qkv[1, :, part(1, h)], n.qkv[side, :, part(0, h)], NT)
            n.s2[:, span_q] = mm(n.qkv[1, :, part(2, h)], n.go[side, :, head], NT)

        def key_back(t, carry, h=h):
            for side in range(3):
                span_q = slice(side * R, (side + 1) * R)
                counts = n.ck[side, t, :]
                s = n.s[t, span_q] * scale - n.stats[side, h : h + 1, :]
                w = jnp.exp(jnp.where(counts > 0.0, s, -1e30)) * counts
                n.low[t, span_q] = w.astype(BF16)
                n.low2[t, span_q] = (w * (n.s2[t, span_q] - n.stats[side, H + h : H + h + 1, :])).astype(BF16)
            return carry

        tiles(R, key_back)
        total_k = jnp.zeros((R, HD), F32)
        total_v = jnp.zeros((R, HD), F32)
        for side in range(3):
            span_q = slice(side * R, (side + 1) * R)
            total_k = total_k + mm(n.low2[:, span_q], n.qkv[side, :, part(0, h)])
            total_v = total_v + mm(n.low[:, span_q], n.go[side, :, head])
        n.gqkv[:, part(1, h)] = (total_k * scale).astype(BF16)
        n.gqkv[:, part(2, h)] = total_v.astype(BF16)
    wide = 3 * D // 2
    mate_gqkv = to_mate(7, n.gqkv.at[:, pl.ds(pl.multiple_of(mate * wide, 128), wide)], n.gqkv_p)
    advance(0, 1)
    advance(1, 1)

    n.tmp[...] = mm(n.gqkv[...], n.wqkv[...], NT)
    gx_ref = n.tok

    def keep1(t, gw):
        gx_ref[t, :] = (n.gresid[t, :] + gw).astype(BF16)

    gc1 = norm_back(n.tmp, 0, n.plain1, n.inv1, keep1)
    row = lax.broadcasted_iota(I32, (8, D), 0)
    sums = jnp.zeros((8, D), F32)
    for i, value in enumerate((*gc1, *gc2)):
        sums = jnp.where(row == i, value, sums)
    n.gcs[0] = sums

    def small_start(k):
        to = (me, mate) if k == 0 else (me ^ (1 << (k - 1)), rp)
        live["gc"] = remote(n.gcs.at[k], n.gcr.at[k], n.gc_ss.at[k], n.gc_rs.at[k], to)

    def small_end(k):
        live["gc"].wait_recv()
        n.gcs[k + 1] = n.gcs[k] + n.gcr[k]

    small_start(0)
    mate_gqkv.wait_recv()
    mate_normed.wait_recv()
    mate_o.wait_recv()
    mate_gr.wait_recv()
    for p in range(3):
        c = pl.ds(pl.multiple_of(rp * wide + p * BLOCK[1], 128), BLOCK[1])
        d = slice(p * BLOCK[1], (p + 1) * BLOCK[1])
        n.acc[2, p] = (mm(n.normed[1], n.gqkv[:, c], TN) + mm(n.normed_p[...], n.gqkv_p[:, d], TN)).astype(BF16)
    c = pl.ds(pl.multiple_of(rp * quarter, 128), quarter)
    n.acc[2, 3] = (mm(n.o[0], n.gr[:, c], TN) + mm(n.o[1], n.gr_p[...], TN)).astype(BF16)
    advance(2, 1)
    small_end(0)
    rows_gone(1, n.out_c)
    n.out_c[...] = mm(n.place[...], gx_ref[...]).astype(BF16)
    send_rows(3, n.out_c, n.home_g)
    small = 1
    while plan[0] or plan[1] or plan[2]:
        if small <= z.bits:
            small_start(small)
        for c in range(3):
            advance(c, 1)
        if small <= z.bits:
            small_end(small)
            small += 1
    n.sums_out[...] = n.gcs[z.bits + 1]
    rows_in(2, n.home_y)
    n.y_out[...] = mm(n.pick[...], n.home_y[...]).astype(BF16)
    rows_in(3, n.home_g)
    n.g_out[...] = mm(n.pick[...], n.home_g[...]).astype(BF16)

    rows_gone(2, n.out_t)
    rows_gone(3, n.out_c)
    for copy in started:
        copy.wait_send()
    for c in range(3):
        pltpu.make_async_copy(n.grads.at[c], n.grads_out.at[c], n.store_sem.at[c]).wait()


def lists_of(z, neighbours, me):
    within = neighbours & (z.R - 1)
    shift = (2 * z.R).bit_length() - 1
    away = (neighbours >> shift) - me
    after = (away == 1) | (away == 1 - z.P)
    base = jnp.where(away == 0, z.R, jnp.where(after, 2 * z.R, 0))
    return (base + within).astype(F32).T


def finish(z, g_ref, sums_ref, y_ref, gx_ref, ada1_ref, ada2_ref, cond_ref, *outs):
    y_out, gx_out, qkv_out, out_out, up_out, down_out, ga1_out, ga2_out, gcond_out = outs
    i, p = pl.program_id(0), pl.program_id(1)
    down_out[...] = g_ref[0, 0, 0].astype(F32)
    up_out[...] = g_ref[1, 0, 0].astype(F32)

    @pl.when(p < 3)
    def _():
        qkv_out[...] = g_ref[2, 0, 0].astype(F32)

    @pl.when(p == 3)
    def _():
        out_out[...] = g_ref[2, 0, 0].astype(F32)

    @pl.when((i == 0) & (p == 0))
    def _():
        y_out[...] = y_ref[...]
        gx_out[...] = gx_ref[...]
        count = cond_ref.shape[1]
        eye = lax.broadcasted_iota(I32, (count, count), 0) == lax.broadcasted_iota(I32, (count, count), 1)
        cond = jnp.sum(jnp.where(eye, cond_ref[...], 0.0), axis=1, keepdims=True)
        d = z.D
        total = jnp.zeros((count, 1), F32)
        for row, ada, out in ((0, ada1_ref, ga1_out), (2, ada2_ref, ga2_out)):
            for j in range(2):
                c = slice(j * d, (j + 1) * d)
                sums = sums_ref[row + j : row + j + 1, :]
                out[:, c] = cond * sums
                total = total + jnp.sum(ada[:, c] * sums, axis=1, keepdims=True)
        gcond_out[...] = jnp.sum(jnp.where(eye, total, 0.0), axis=0, keepdims=True)


def local(tokens, cotangent, dest, neighbours, w_qkv, w_out, w_up, w_down, ada_attn, ada_mlp, cond):
    rows, width = tokens.shape
    z = sizes(lax.axis_size("patch"), rows, width, w_up.shape[1])
    dest = dest.reshape(1, rows)
    cond = cond.reshape(1, cond.shape[0])
    inputs = dict(
        tokens=tokens,
        cotangent=cotangent,
        dest=dest,
        neighbours=neighbours,
        w_qkv=w_qkv,
        w_out=w_out,
        w_up=w_up,
        w_down=w_down,
        ada_attn=ada_attn,
        ada_mlp=ada_mlp,
        cond=cond,
    )
    small = ("dest", "neighbours", "cond")
    any_space = pl.BlockSpec(memory_space=pl.ANY)
    vmem = pl.BlockSpec(memory_space=pltpu.VMEM)
    shape = jax.ShapeDtypeStruct
    outs = dict(
        grads_out=shape((3, 2, PARTS) + BLOCK, BF16),
        sums_out=shape((8, width), F32),
        y_out=shape((rows, width), BF16),
        g_out=shape((rows, width), BF16),
    )
    held = scratch(z, neighbours.shape[1])
    grads, sums, y, gx = pl.pallas_call(
        functools.partial(layer, z, [*inputs, *outs, *held]),
        out_shape=list(outs.values()),
        in_specs=[vmem if k in small else any_space for k in inputs],
        out_specs=[any_space, vmem, vmem, vmem],
        scratch_shapes=list(held.values()),
        compiler_params=pltpu.CompilerParams(collective_id=0, has_side_effects=True, vmem_limit_bytes=62 << 20),
        name="layer",
    )(*inputs.values())

    whole = lambda i, p: (0, 0)
    block = pl.BlockSpec(BLOCK, None)
    rows_spec = pl.BlockSpec((rows, width), whole)
    ada_spec = pl.BlockSpec(ada_attn.shape, whole)
    cond_spec = pl.BlockSpec((1, cond.shape[1]), whole)
    y, gx, g_qkv, g_out, g_up, g_down, g_ada1, g_ada2, g_cond = pl.pallas_call(
        functools.partial(finish, z),
        grid=(2, PARTS),
        in_specs=[
            pl.BlockSpec((3, 1, 1) + BLOCK, lambda i, p: (0, i, p, 0, 0)),
            pl.BlockSpec((8, width), whole),
            rows_spec,
            rows_spec,
            ada_spec,
            ada_spec,
            cond_spec,
        ],
        out_specs=[
            rows_spec,
            rows_spec,
            pl.BlockSpec(BLOCK, lambda i, p: (0, i * 3 + jnp.minimum(p, 2))),
            pl.BlockSpec(BLOCK, lambda i, p: (0, i)),
            pl.BlockSpec(BLOCK, lambda i, p: (0, i * PARTS + p)),
            pl.BlockSpec(BLOCK, lambda i, p: (i * 2 + p // 2, p % 2)),
            ada_spec,
            ada_spec,
            cond_spec,
        ],
        out_shape=[
            shape((rows, width), BF16),
            shape((rows, width), BF16),
            shape(w_qkv.shape, F32),
            shape(w_out.shape, F32),
            shape(w_up.shape, F32),
            shape(w_down.shape, F32),
            shape(ada_attn.shape, F32),
            shape(ada_mlp.shape, F32),
            shape(cond.shape, F32),
        ],
        name="finish",
    )(grads, sums, y, gx, ada_attn, ada_mlp, cond)
    return y, gx, g_qkv, g_out, g_up, g_down, g_ada1, g_ada2, g_cond.reshape(cond.shape[1])


def solution(mesh):
    row = P(("patch", "rep"), None)
    return jax.shard_map(
        local,
        mesh=mesh,
        in_specs=(row, row, P(("patch", "rep")), row) + (P(),) * 7,
        out_specs=(row, row) + (P(),) * 7,
        check_vma=False,
    )
```

```python
import functools
import heapq
import itertools
import types

import jax
import jax.numpy as jnp
from jax import lax
from jax.experimental import pallas as pl
from jax.experimental.pallas import tpu as pltpu
from jax.sharding import PartitionSpec as P

H = 4
HD = 128
EPS = 1e-05
F32 = jnp.float32
BF16 = jnp.bfloat16
I32 = jnp.int32
MESH = pl.DeviceIdType.MESH
NN = (((1,), (0,)), ((), ()))
NT = (((1,), (1,)), ((), ()))
TN = (((0,), (0,)), ((), ()))
TILE = 32
NEVER = -1e30
LOG2E = 1.4426950408889634
BLOCK = (512, 256)
MIN_ROWS = 16


def mm(a, b, dims=NN):
    return lax.dot_general(a, b, dims, preferred_element_type=F32)


def iota(shape, axis):
    return lax.broadcasted_iota(I32, shape, axis).astype(F32)


def hot(cond):
    return jnp.where(cond, 1.0, 0.0)


def sizes(patches, rows, width, hidden):
    cap = rows // patches + 1
    block = -(-(cap - 1) // 16) * 16
    bits = patches.bit_length() - 1
    halvings = 0
    while halvings < bits and BLOCK[0] >> (halvings + 1) >= MIN_ROWS:
        halvings += 1
    return types.SimpleNamespace(
        P=patches, R=rows, D=width, FF=hidden, T=block, PT=patches * block, bits=bits, halvings=halvings
    )


XYZ, XZY, YXZ, YZX, ZXY, ZYX = itertools.permutations(range(3))
ORDERS = [XZY, YXZ, ZYX, XZY, XYZ, YZX, ZYX, YXZ, ZYX, YXZ, XZY, XYZ]
DOWN, UP, OUT, QKV = range(0, 4), range(4, 8), range(8, 9), range(9, 12)
STREAMS = len(ORDERS)
QKV_AT = 15.3
FREE_AT = (4.0, 5.0, 5.0)
COMPUTES = ((-1.0, 1.2), (1.2, 2.3), (2.3, 3.4), (3.4, 4.5), (4.5, 5.6), (8.5, 9.5), (9.5, 10.5), (10.5, 11.5), (11.5, 12.5), (12.5, 14.0), (14.0, 15.3))
PIECES = 4


def bit_orders(bits):
    return [tuple(b for b in f if b < bits) + tuple(range(3, bits)) for f in ORDERS]


def sum_plan(bits, halvings):
    whole, delay, turn, depth = 5.7, 1.8, 0.12, 2
    steps = []
    for order in bit_orders(bits):
        places = [(order[k], min(k + 1, halvings)) for k in range(bits)]
        places += [(order[k], k + 1) for k in range(halvings - 1, -1, -1)]
        far = 2.0 if bits == 4 else 1.0
        steps.append([(b, whole / (1 << k) * (far if b == 3 else 1.0)) for b, k in places] + [(None, 0.5)])
    at = [0] * STREAMS
    free, queued, waiting, plan = {}, {}, [], []
    number = itertools.count()
    events = [(QKV_AT if p in QKV else FREE_AT[ORDERS[p][0]], next(number), "ready", p) for p in range(STREAMS)]
    heapq.heapify(events)
    now = 0.0

    def able(t):
        return next((b for a, b in COMPUTES if a < t < b), t)

    while events:
        t, _, kind, p = heapq.heappop(events)
        if kind == "free":
            queued[p] -= 1
            kind = "look"
        if able(max(now, t)) > max(now, t):
            heapq.heappush(events, (able(max(now, t)), next(number), kind, p))
            continue
        now = max(now, t)
        if kind == "ready":
            waiting.append(p)
        elif kind == "end":
            now += turn
            plan.append((now, "await", p))
            at[p] += 1
            if at[p] < len(steps[p]):
                waiting.append(p)
        for q in sorted(waiting):
            link, time = steps[q][at[q]]
            if link is not None and queued.get(link, 0) >= depth:
                continue
            waiting.remove(q)
            now += 0.03
            plan.append((now, "start", q))
            queued[link] = queued.get(link, 0) + 1
            free[link] = max(free.get(link, 0.0), now) + time
            heapq.heappush(events, (free[link] + delay, next(number), "end", q))
            heapq.heappush(events, (free[link], next(number), "free", link))
    return plan


def scratch(z, nb):
    R, D, FF, PT, PS = z.R, z.D, z.FF, z.PT, z.PT + z.P
    recv_rows = []
    for k in range(z.bits):
        recv_rows.append(BLOCK[0] >> (min(k + 1, z.halvings)))
    vm, dma = pltpu.VMEM, pltpu.SemaphoreType.DMA
    s = dict(
        tok=vm((R, D), BF16),
        cot=vm((R, D), BF16),
        wqkv=vm((D, 3 * D), BF16),
        wout=vm((D, D), BF16),
        wup=vm((D, FF), BF16),
        wdown=vm((FF, D), BF16),
        ada1=vm((32, 2 * D), F32),
        ada2=vm((32, 2 * D), F32),
        c=vm((16, 2 * D), F32),
        pick=vm((R, PS), BF16),
        place=vm((PS, R), BF16),
        out_t=vm((PT, D), BF16),
        out_c=vm((PT, D), BF16),
        in_t=vm((PS, D), BF16),
        in_c=vm((PS, D), BF16),
        home_y=vm((PS, D), BF16),
        home_g=vm((PS, D), BF16),
        more_out=vm((4, z.P, 1, D + 128), F32),
        more_in=vm((4, z.P, 1, D + 128), F32),
        x=vm((R, D), F32),
        plain1=vm((R, D), F32),
        inv1=vm((R, 128), F32),
        plain2=vm((R, D), F32),
        inv2=vm((R, 128), F32),
        resid=vm((R, D), F32),
        gresid=vm((R, D), F32),
        tmp=vm((R, D), F32),
        ups=vm((2, R, D), BF16),
        normed=vm((3, R, D), BF16),
        normed_p=vm((R, D), BF16),
        qkv=vm((3, R, 3 * D), BF16),
        cols=vm((3, nb, R), F32),
        colq=vm((R, nb), F32),
        cq=vm((R, 3 * R), F32),
        ck=vm((3, R, R), F32),
        s=vm((R, 3 * R), F32),
        s2=vm((R, 3 * R), F32),
        w=vm((H, R, 3 * R), BF16),
        low=vm((R, 3 * R), BF16),
        low2=vm((R, 3 * R), BF16),
        o=vm((2, R, D), BF16),
        u=vm((R, D), F32),
        ga=vm((R, D), F32),
        a=vm((R, FF), BF16),
        a_p=vm((R, FF // 2), BF16),
        gu=vm((R, FF), BF16),
        gu_p=vm((R, FF // 2), BF16),
        normed2=vm((2, R, D), BF16),
        gr=vm((R, D), BF16),
        gr_p=vm((R, D // 2), BF16),
        go=vm((3, R, D), BF16),
        stat=vm((R, 128), F32),
        stats=vm((3, 2 * H, R), F32),
        gqkv=vm((R, 3 * D), BF16),
        gqkv_p=vm((R, 3 * D // 2), BF16),
        acc=vm((STREAMS,) + BLOCK, BF16),
        **{f"rcv{k}": vm((STREAMS, n, BLOCK[1]), BF16) for k, n in enumerate(recv_rows)},
        gcs=vm((z.bits + 2, 8, D), F32),
        gcr=vm((z.bits + 1, 8, D), F32),
        load_sem=dma((8,)),
        row_ss=dma((4,)),
        row_rs=dma((4,)),
        own_sem=dma((4,)),
        more_ss=dma((4,)),
        more_rs=dma((4,)),
        more_own=dma((4,)),
        side_ss=dma((4, 2)),
        side_rs=dma((4, 2)),
        piece_rs=dma((2, PIECES)),
        pair_ss=dma((8,)),
        pair_rs=dma((8,)),
        sum_ss=dma((1,)),
        late_ss=dma((STREAMS, max(z.bits - z.halvings, 1))),
        rs_rs=dma((STREAMS, z.bits)),
        ag_rs=dma((STREAMS, z.halvings)),
        core_ss=dma((1,)),
        core_rs=dma((1,)),
        gc_ss=dma((1,)),
        gc_rs=dma((z.bits + 1,)),
    )
    return s


def marker():
    def phase(name):
        del name

    return phase


def layer(z, names, *refs):
    n = types.SimpleNamespace(**dict(zip(names, refs, strict=True)))
    Pn, R, D, FF, T, PT, PS = z.P, z.R, z.D, z.FF, z.T, z.PT, z.PT + z.P
    me = lax.axis_index("patch")
    rp = lax.axis_index("rep")
    mate = 1 - rp
    nxt = lax.rem(me + 1, Pn)
    prv = lax.rem(me + Pn - 1, Pn)
    started = []
    phase = marker()

    def tiles(total, fn, init=0, size=TILE, together=1):
        def some(i, carry):
            for j in range(together):
                carry = fn(pl.ds(pl.multiple_of((i * together + j) * size, size), size), carry)
            return carry

        return lax.fori_loop(0, total // (size * together), some, init)

    def load(i, src, dst):
        copy = pltpu.make_async_copy(src, dst, n.load_sem.at[i])
        copy.start()
        return copy

    phase("entry")
    get_tok = load(0, n.tokens, n.tok)
    get_cot = load(1, n.cotangent, n.cot)
    get_ada1 = load(2, n.ada_attn, n.ada1)
    get_ada2 = load(3, n.ada_mlp, n.ada2)
    get_wqkv = load(4, n.w_qkv, n.wqkv)
    get_wdown = load(5, n.w_down, n.wdown)
    get_wout = load(6, n.w_out, n.wout)
    get_wup = load(7, n.w_up, n.wup)

    barrier = pltpu.get_barrier_semaphore()

    def greet(i, carry):
        pl.semaphore_signal(barrier, inc=1, device_id=(lax.rem(me + i, Pn), rp), device_id_type=MESH)
        return carry

    lax.fori_loop(1, Pn, greet, 0)
    pl.semaphore_signal(barrier, inc=1, device_id=(me, mate), device_id_type=MESH)

    def remote(src, dst, ss, rs, to, keep=False):
        copy = pltpu.make_async_remote_copy(
            src_ref=src, dst_ref=dst, send_sem=ss, recv_sem=rs, device_id=to, device_id_type=MESH
        )
        copy.start()
        if keep:
            started.append(copy)
        return copy

    def send_rows(i, src, dst):
        def one(j, carry):
            to = lax.rem(me + j, Pn)
            pltpu.make_async_remote_copy(
                src_ref=src.at[pl.ds(pl.multiple_of(to * T, 16), T)],
                dst_ref=dst.at[pl.ds(pl.multiple_of(me * T, 16), T)],
                send_sem=n.row_ss.at[i],
                recv_sem=n.row_rs.at[i],
                device_id=(to, rp),
                device_id_type=MESH,
            ).start()
            pltpu.make_async_remote_copy(
                src_ref=n.more_out.at[i, to],
                dst_ref=n.more_in.at[i, me],
                send_sem=n.more_ss.at[i],
                recv_sem=n.more_rs.at[i],
                device_id=(to, rp),
                device_id_type=MESH,
            ).start()
            return carry

        lax.fori_loop(1, Pn, one, 0)
        mine = pl.ds(pl.multiple_of(me * T, 16), T)
        pltpu.make_async_copy(src.at[mine], dst.at[mine], n.own_sem.at[i]).start()
        pltpu.make_async_copy(n.more_out.at[i, me], n.more_in.at[i, me], n.more_own.at[i]).start()

    def waits_for(ref, sem):
        pltpu.make_async_copy(ref, ref, sem).wait()

    def rows_in(i, dst):
        waits_for(n.more_in.at[i, pl.ds(0, Pn - 1)], n.more_rs.at[i])
        waits_for(n.more_in.at[i, 0], n.more_own.at[i])
        waits_for(dst.at[pl.ds(0, PT - T)], n.row_rs.at[i])
        waits_for(dst.at[pl.ds(0, T)], n.own_sem.at[i])
        dst[PT:PS] = n.more_in[i, :, 0, :D].astype(BF16)

    def rows_gone(i, src):
        waits_for(src.at[pl.ds(0, PT - T)], n.row_ss.at[i])
        waits_for(n.more_out.at[i, pl.ds(0, Pn - 1)], n.more_ss.at[i])

    def set_rows(i, hot_rows, values, out):
        total = mm(hot_rows, values)
        out[...] = total[:PT].astype(BF16)
        n.more_out[i, :, 0, :D] = total[PT:]

    even = lax.rem(me, 2) == 0
    near = me ^ 1
    near_slot = jnp.where(even, 2, 0)
    far_slot = 2 - near_slot
    onward = lax.rem(jnp.where(even, me + 2, me + Pn - 2), Pn)

    def to_sides(i, ref):
        return (
            remote(ref.at[1], ref.at[0], n.side_ss.at[i, 0], n.side_rs.at[i, 0], (nxt, rp), True),
            remote(ref.at[1], ref.at[2], n.side_ss.at[i, 1], n.side_rs.at[i, 1], (prv, rp), True),
        )

    def to_near(i, ref):
        size = R // PIECES
        return [
            remote(
                ref.at[1, pl.ds(c * size, size)],
                ref.at[far_slot, pl.ds(c * size, size)],
                n.side_ss.at[i, 0],
                n.piece_rs.at[i - 1, c],
                (near, rp),
            )
            for c in range(PIECES)
        ]

    def hand_on(i, ref, copies):
        size = R // PIECES
        for copy in copies:
            c = len(handed[i])
            copy.wait_recv()
            handed[i].append(
                remote(
                    ref.at[near_slot, pl.ds(c * size, size)],
                    ref.at[far_slot, pl.ds(c * size, size)],
                    n.side_ss.at[i, 1],
                    n.side_rs.at[i, 1],
                    (onward, rp),
                )
            )

    handed = {1: [], 2: []}

    def far_in(i, ref):
        waits_for(ref.at[far_slot], n.side_rs.at[i, 1])

    def to_mate(i, src, dst):
        return remote(src, dst, n.pair_ss.at[i], n.pair_rs.at[i], (me, mate), True)

    n.cols[1] = lists_of(z, n.neighbours[...], me)
    dest = n.dest[...].astype(F32)
    mine_hot = iota((Pn, R), 0) == dest
    before = hot(iota((R, R), 0) < iota((R, R), 1)).astype(BF16)
    earlier = mm(hot(mine_hot).astype(BF16), before)
    rank = jnp.sum(jnp.where(mine_hot, earlier, 0.0), axis=0, keepdims=True)
    code = jnp.where(rank < T, dest * T + rank, PT + dest)
    pick = hot(code == iota((PS, R), 0))
    pick_low = pick.astype(BF16)
    get_tok.wait()
    set_rows(0, pick_low, n.tok[...], n.out_t)
    n.more_out[0, :, 0, D:] = jnp.broadcast_to(jnp.sum(hot(mine_hot), axis=1, keepdims=True), (Pn, 128))
    phase("barrier")
    pl.semaphore_wait(barrier, Pn)
    phase("send tokens")
    side_lists = to_sides(0, n.cols)
    send_rows(0, n.out_t, n.in_t)
    get_cot.wait()
    set_rows(1, pick_low, n.cot[...], n.out_c)
    n.pick[...] = pick.T.astype(BF16)

    phase("counts")
    get_ada1.wait()
    get_ada2.wait()
    cond = jnp.broadcast_to(n.cond[...], (8, n.cond.shape[1]))
    n.c[0:8] = jnp.dot(cond, n.ada1[...], precision=lax.Precision.HIGHEST, preferred_element_type=F32)
    n.c[8:16] = jnp.dot(cond, n.ada2[...], precision=lax.Precision.HIGHEST, preferred_element_type=F32)
    n.colq[...] = n.cols[1].T
    lists = n.cols.shape[1]

    def count_q(t, carry):
        ids = iota((TILE, 3 * R), 1)
        col = n.colq[t, :]
        total = jnp.zeros((TILE, 3 * R), F32)
        for j in range(lists):
            total = total + hot(col[:, j : j + 1] == ids)
        n.cq[t, :] = jnp.where(total > 0.0, jnp.log2(total), NEVER)
        return carry

    tiles(R, count_q)

    def count_k(side, base):
        def one(t, carry):
            ids = iota((TILE, R), 0) + (t.start + base).astype(F32)
            total = jnp.zeros((TILE, R), F32)
            for j in range(lists):
                total = total + hot(n.cols[side, j : j + 1, :] == ids)
            n.ck[side, t, :] = jnp.where(total > 0.0, jnp.log2(total), NEVER)
            return carry

        tiles(R, one)

    count_k(1, R)
    phase("side counts")
    for lists_copy in side_lists:
        lists_copy.wait_recv()
    count_k(0, 2 * R)
    count_k(2, 0)

    phase("places")
    row = iota((PS, 1), 0)
    source = jnp.where(row < PT, jnp.floor((row + 0.5) * (1.0 / T)), row - PT)
    step = jnp.where(row < PT, row - source * T, T * 1.0)
    spread = hot(source == iota((PS, Pn), 1)).astype(BF16)
    earlier_sources = hot(iota((Pn, Pn), 0) > iota((Pn, Pn), 1)).astype(BF16)
    phase("wait tokens")
    rows_in(0, n.in_t)
    phase("place rows")
    count = n.more_in[0, :, 0, D:].astype(BF16)
    offset = mm(earlier_sources, count).astype(BF16)
    position = jnp.where(step < mm(spread, count)[:, 0:1], mm(spread, offset)[:, 0:1] + step, -1.0)
    place = hot(position == iota((PS, R), 1))
    n.place[...] = place.astype(BF16)
    place_t = place.T.astype(BF16)
    n.x[...] = mm(place_t, n.in_t[...])

    def norm(src, coeffs, plain_ref, inv_ref, out):
        def one(t, carry):
            v = src[t, :]
            centred = v - jnp.sum(v, axis=-1, keepdims=True) * (1.0 / D)
            inverse = lax.rsqrt(jnp.sum(centred * centred, axis=-1, keepdims=True) * (1.0 / D) + EPS)
            plain = centred * inverse
            plain_ref[t, :] = plain
            inv_ref[t, :] = jnp.broadcast_to(inverse, (TILE, 128))
            out[t, :] = (plain * (1.0 + n.c[coeffs : coeffs + 1, :D]) + n.c[coeffs : coeffs + 1, D:]).astype(BF16)
            return carry

        tiles(R, one)

    def norm_back(grad, coeffs, plain_ref, inv_ref, finish):
        def one(t, carry):
            g = grad[t, :]
            plain = plain_ref[t, :]
            scaled = g * (1.0 + n.c[coeffs : coeffs + 1, :D])
            mean = jnp.sum(scaled, axis=-1, keepdims=True) * (1.0 / D)
            along = jnp.sum(scaled * plain, axis=-1, keepdims=True) * (1.0 / D)
            finish(t, inv_ref[t, 0:1] * (scaled - mean - plain * along))
            return (
                carry[0] + jnp.sum(g * plain, axis=0, keepdims=True),
                carry[1] + jnp.sum(g, axis=0, keepdims=True),
            )

        zero = jnp.zeros((1, D), F32)
        return tiles(R, one, (zero, zero))

    phase("norm")
    norm(n.x, 0, n.plain1, n.inv1, n.normed.at[1])
    side_normed = to_near(1, n.normed)
    mate_normed = to_mate(0, n.normed.at[1], n.normed_p)
    phase("project")
    get_wqkv.wait()

    def project(side):
        for j in range(3):
            c = slice(j * D, (j + 1) * D)
            n.qkv[side, :, c] = mm(n.normed[side], n.wqkv[:, c]).astype(BF16)

    project(1)
    phase("wait halo")
    hand_on(1, n.normed, side_normed)
    send_rows(1, n.out_c, n.in_c)
    project(near_slot)
    phase("wait far")
    far_in(1, n.normed)
    project(far_slot)

    phase("attention")
    scale = 1.0 / HD**0.5

    def part(which, h):
        return slice(which * D + h * HD, which * D + (h + 1) * HD)

    for h in range(H):
        for side in range(3):
            n.s[:, side * R : (side + 1) * R] = mm(n.qkv[1, :, part(0, h)], n.qkv[side, :, part(1, h)], NT)

        def soft(t, carry, h=h):
            s = n.s[t, :] * (scale * LOG2E) + n.cq[t, :]
            top = jnp.max(s, axis=-1, keepdims=True)
            e = jnp.exp2(s - top)
            total = jnp.sum(e, axis=-1, keepdims=True)
            w = e * (1.0 / total)
            n.w[h, t, :] = w.astype(BF16)
            n.stat[t, h : h + 1] = top + jnp.log2(total)
            return carry

        tiles(R, soft, together=4)
        mixed = jnp.zeros((R, HD), F32)
        for side in range(3):
            mixed = mixed + mm(n.w[h, :, side * R : (side + 1) * R], n.qkv[side, :, part(2, h)])
        n.o[0, :, h * HD : (h + 1) * HD] = mixed.astype(BF16)
    mate_o = to_mate(2, n.o.at[0], n.o.at[1])

    phase("wait upstream")
    rows_in(1, n.in_c)
    n.ups[0] = mm(place_t, n.in_c[...]).astype(BF16)
    mate_ups = to_mate(1, n.ups.at[0], n.ups.at[1])
    phase("resid")
    get_wout.wait()
    n.resid[...] = n.x[...] + mm(n.o[0], n.wout[...])
    norm(n.resid, 8, n.plain2, n.inv2, n.normed2.at[0])
    mate_normed2 = to_mate(3, n.normed2.at[0], n.normed2.at[1])
    get_wup.wait()
    get_wdown.wait()
    phase("mlp")
    half = FF // 2
    for j in range(FF // D):
        c = slice(j * D, (j + 1) * D)
        n.u[...] = mm(n.normed2[0], n.wup[:, c])
        n.ga[...] = mm(n.ups[0], n.wdown[c, :], NT)

        def gate(t, carry, c=c):
            u = n.u[t, :]
            sig = 1.0 / (1.0 + jnp.exp(-u))
            n.a[t, c] = (u * sig).astype(BF16)
            n.gu[t, c] = (n.ga[t, :] * sig * (1.0 + u * (1.0 - sig))).astype(BF16)
            return carry

        tiles(R, gate)
    theirs = pl.ds(pl.multiple_of(mate * half, 128), half)
    ours = pl.ds(pl.multiple_of(rp * half, 128), half)
    mate_a = to_mate(4, n.a.at[:, theirs], n.a_p)
    mate_gu = to_mate(5, n.gu.at[:, theirs], n.gu_p)
    phase("mlp back")
    n.tmp[...] = mm(n.gu[...], n.wup[...], NT)

    def keep2(t, gw):
        total = n.ups[0, t, :].astype(F32) + gw
        n.gresid[t, :] = total
        n.gr[t, :] = total.astype(BF16)

    gc2 = norm_back(n.tmp, 8, n.plain2, n.inv2, keep2)
    phase("go")
    n.go[1] = mm(n.gr[...], n.wout[...], NT).astype(BF16)
    side_go = to_near(2, n.go)
    quarter = D // 2
    mate_gr = to_mate(6, n.gr.at[:, pl.ds(pl.multiple_of(mate * quarter, 128), quarter)], n.gr_p)
    orders = bit_orders(z.bits)
    top_rows = BLOCK[0]

    def bit(p, k):
        return (me >> orders[p][k]) & 1

    def start_of(p, k):
        at = 0
        for i in range(k):
            at = at + bit(p, i) * (top_rows >> (i + 1))
        return at

    def span(p, k):
        k = min(k, z.halvings)
        rows = top_rows >> k
        return pl.ds(pl.multiple_of(start_of(p, k), rows) if k else 0, rows)

    def partner(p, k):
        return (me ^ (1 << orders[p][k]), rp)

    live = {}

    def reduce_start(p, k):
        if k < z.halvings:
            rows = top_rows >> (k + 1)
            gone = (1 - bit(p, k)) * rows + start_of(p, k)
            src = n.acc.at[p, pl.ds(pl.multiple_of(gone, rows), rows)]
        else:
            src = n.acc.at[p, span(p, k)]
        ss = n.sum_ss.at[0] if k < z.halvings else n.late_ss.at[p, k - z.halvings]
        live[p] = remote(src, getattr(n, f"rcv{k}").at[p], ss, n.rs_rs.at[p, k], partner(p, k))

    def reduce_end(p, k):
        live[p].wait_recv()
        if k >= z.halvings:
            live[p].wait_send()
        kept = span(p, k + 1)
        total = n.acc[p, kept].astype(F32) + getattr(n, f"rcv{k}")[p].astype(F32)
        into = n.grads_out.at[rp, p, kept] if k + 1 == z.bits else n.acc.at[p, kept]
        into[...] = total.astype(BF16)

    def gather_start(p, k):
        ref = n.grads_out.at[rp, p, span(p, k + 1)]
        live[p] = remote(ref, ref, n.sum_ss.at[0], n.ag_rs.at[p, k], partner(p, k))

    def core_start(p):
        ref = n.grads_out.at[rp, p]
        remote(ref, ref, n.core_ss.at[0], n.core_rs.at[0], (me, mate))

    steps_left = {}
    for p in range(STREAMS):
        steps = []
        for k in range(z.bits):
            steps += [functools.partial(reduce_start, p, k), functools.partial(reduce_end, p, k)]
        for k in range(z.halvings - 1, -1, -1):
            steps += [functools.partial(gather_start, p, k), lambda p=p: live[p].wait_recv()]
        steps += [functools.partial(core_start, p), lambda: None]
        steps_left[p] = steps
    actions = sum_plan(z.bits, z.halvings)

    def service(until=None, most=None):
        while actions and (until is None or actions[0][0] <= until) and (most is None or most > 0):
            most = None if most is None else most - 1
            steps_left[actions.pop(0)[2]].pop(0)()

    phase("grad down")
    mate_ups.wait_recv()
    mate_a.wait_recv()
    for j in range(2):
        r = pl.ds(pl.multiple_of(rp * half + j * BLOCK[0], 128), BLOCK[0])
        for i in range(2):
            c = slice(i * BLOCK[1], (i + 1) * BLOCK[1])
            total = mm(n.a[:, r], n.ups[0, :, c], TN) + mm(n.a_p[:, j * BLOCK[0] : (j + 1) * BLOCK[0]], n.ups[1, :, c], TN)
            n.acc[2 * j + i] = total.astype(BF16)
    phase("grad up")
    mate_normed2.wait_recv()
    mate_gu.wait_recv()
    for p in range(len(UP)):
        c = pl.ds(pl.multiple_of(rp * half + p * BLOCK[1], 128), BLOCK[1])
        d = slice(p * BLOCK[1], (p + 1) * BLOCK[1])
        n.acc[UP[p]] = (mm(n.normed2[0], n.gu[:, c], TN) + mm(n.normed2[1], n.gu_p[:, d], TN)).astype(BF16)
    mate_o.wait_recv()
    mate_gr.wait_recv()
    c = pl.ds(pl.multiple_of(rp * quarter, 128), quarter)
    n.acc[OUT[0]] = (mm(n.o[0], n.gr[:, c], TN) + mm(n.o[1], n.gr_p[...], TN)).astype(BF16)

    phase("query back")
    for h in range(H):
        head = slice(h * HD, (h + 1) * HD)
        for side in range(3):
            n.s[:, side * R : (side + 1) * R] = mm(n.go[1, :, head], n.qkv[side, :, part(2, h)], NT)

        def soft_back(t, carry, h=h):
            w = n.w[h, t, :].astype(F32)
            gp = n.s[t, :]
            delta = jnp.sum(w * gp, axis=-1, keepdims=True)
            n.low[t, :] = (w * (gp - delta)).astype(BF16)
            n.stat[t, H + h : H + h + 1] = delta
            return carry

        tiles(R, soft_back, together=4)
        total = jnp.zeros((R, HD), F32)
        for side in range(3):
            total = total + mm(n.low[:, side * R : (side + 1) * R], n.qkv[side, :, part(1, h)])
        n.gqkv[:, part(0, h)] = (total * scale).astype(BF16)
        if h < PIECES:
            hand_on(2, n.go, side_go[h : h + 1])
        service(2.3 + 1.1 * h)
    n.stats[1] = n.stat[...].T[0 : 2 * H]
    side_stats = to_sides(3, n.stats)
    phase("y")
    y = (n.resid[...] + mm(n.a[...], n.wdown[...])).astype(BF16)
    rows_gone(0, n.out_t)
    set_rows(2, n.place[...], y, n.out_t)
    send_rows(2, n.out_t, n.home_y)

    service(7.2)

    phase("sums step")
    for copy in side_stats:
        copy.wait_recv()
    far_in(2, n.go)
    phase("key back")
    for h in range(H):
        head = slice(h * HD, (h + 1) * HD)
        for side in range(3):
            span_q = slice(side * R, (side + 1) * R)
            n.s[:, span_q] = mm(n.qkv[1, :, part(1, h)], n.qkv[side, :, part(0, h)], NT)
            n.s2[:, span_q] = mm(n.qkv[1, :, part(2, h)], n.go[side, :, head], NT)

        def key_back(t, carry, h=h):
            for side in range(3):
                span_q = slice(side * R, (side + 1) * R)
                s = n.s[t, span_q] * (scale * LOG2E) + n.ck[side, t, :]
                w = jnp.exp2(s - n.stats[side, h : h + 1, :])
                n.low[t, span_q] = w.astype(BF16)
                n.low2[t, span_q] = (w * (n.s2[t, span_q] - n.stats[side, H + h : H + h + 1, :])).astype(BF16)
            return carry

        tiles(R, key_back, together=4)
        total_k = jnp.zeros((R, HD), F32)
        total_v = jnp.zeros((R, HD), F32)
        for side in range(3):
            span_q = slice(side * R, (side + 1) * R)
            total_k = total_k + mm(n.low2[:, span_q], n.qkv[side, :, part(0, h)])
            total_v = total_v + mm(n.low[:, span_q], n.go[side, :, head])
        n.gqkv[:, part(1, h)] = (total_k * scale).astype(BF16)
        n.gqkv[:, part(2, h)] = total_v.astype(BF16)
        service(9.5 + h)
    phase("send gqkv")
    wide = 3 * D // 2
    mate_gqkv = to_mate(7, n.gqkv.at[:, pl.ds(pl.multiple_of(mate * wide, 128), wide)], n.gqkv_p)
    phase("gx")
    n.tmp[...] = mm(n.gqkv[...], n.wqkv[...], NT)
    gx_ref = n.tok

    def keep1(t, gw):
        gx_ref[t, :] = (n.gresid[t, :] + gw).astype(BF16)

    gc1 = norm_back(n.tmp, 0, n.plain1, n.inv1, keep1)
    row = lax.broadcasted_iota(I32, (8, D), 0)
    sums = jnp.zeros((8, D), F32)
    for i, value in enumerate((*gc1, *gc2)):
        sums = jnp.where(row == i, value, sums)
    n.gcs[0] = sums

    def small_start(k):
        to = (me, mate) if k == 0 else (me ^ (1 << (k - 1)), rp)
        live["gc"] = remote(n.gcs.at[k], n.gcr.at[k], n.gc_ss.at[0], n.gc_rs.at[k], to)

    def small_end(k):
        live["gc"].wait_recv()
        n.gcs[k + 1] = n.gcs[k] + n.gcr[k]

    phase("wait gqkv")
    small_start(0)
    service(14.0)
    mate_gqkv.wait_recv()
    mate_normed.wait_recv()
    phase("grad qkv")
    for p in range(3):
        c = pl.ds(pl.multiple_of(rp * wide + p * BLOCK[1], 128), BLOCK[1])
        d = slice(p * BLOCK[1], (p + 1) * BLOCK[1])
        n.acc[QKV[p]] = (mm(n.normed[1], n.gqkv[:, c], TN) + mm(n.normed_p[...], n.gqkv_p[:, d], TN)).astype(BF16)
    phase("leave gx")
    service(15.6)
    small_end(0)
    rows_gone(1, n.out_c)
    set_rows(3, n.place[...], gx_ref[...], n.out_c)
    send_rows(3, n.out_c, n.home_g)
    phase("sums")
    share = -(-len(actions) // (z.bits + 1))
    for small in range(1, z.bits + 1):
        small_start(small)
        service(most=share)
        small_end(small)
    service()
    waits_for(n.grads_out.at[mate], n.core_rs.at[0])
    n.sums_out[...] = n.gcs[z.bits + 1]
    phase("home")
    rows_in(2, n.home_y)
    n.y_out[...] = mm(n.pick[...], n.home_y[...]).astype(BF16)
    rows_in(3, n.home_g)
    n.g_out[...] = mm(n.pick[...], n.home_g[...]).astype(BF16)

    phase("end")
    rows_gone(2, n.out_t)
    rows_gone(3, n.out_c)
    for copy in started:
        copy.wait_send()
    for i, ref in ((1, n.normed), (2, n.go)):
        for leg in range(2):
            waits_for(ref.at[1], n.side_ss.at[i, leg])
    waits_for(n.grads_out.at[:, :, pl.ds(0, BLOCK[0] - (BLOCK[0] >> z.halvings))], n.sum_ss.at[0])
    waits_for(n.grads_out.at[rp], n.core_ss.at[0])
    waits_for(n.gcr, n.gc_ss.at[0])


def lists_of(z, neighbours, me):
    within = neighbours & (z.R - 1)
    shift = (2 * z.R).bit_length() - 1
    away = (neighbours >> shift) - me
    after = (away == 1) | (away == 1 - z.P)
    base = jnp.where(away == 0, z.R, jnp.where(after, 2 * z.R, 0))
    return (base + within).astype(F32)


def finish(z, g_ref, sums_ref, y_ref, gx_ref, ada1_ref, ada2_ref, cond_ref, *outs):
    y_out, gx_out, qkv_out, out_out, up_out, down_out, ga1_out, ga2_out, gcond_out = outs
    i, p = pl.program_id(0), pl.program_id(1)
    down_out[...] = g_ref[i, DOWN[0] + p].astype(F32)
    up_out[...] = g_ref[i, UP[0] + p].astype(F32)

    @pl.when(p < 3)
    def _():
        qkv_out[...] = g_ref[i, QKV[0] + p].astype(F32)

    @pl.when(p == 3)
    def _():
        out_out[...] = g_ref[i, OUT[0]].astype(F32)

    @pl.when((i == 0) & (p == 0))
    def _():
        y_out[...] = y_ref[...]
        gx_out[...] = gx_ref[...]
        count = cond_ref.shape[1]
        eye = lax.broadcasted_iota(I32, (count, count), 0) == lax.broadcasted_iota(I32, (count, count), 1)
        cond = jnp.sum(jnp.where(eye, cond_ref[...], 0.0), axis=1, keepdims=True)
        d = z.D
        total = jnp.zeros((count, 1), F32)
        for row, ada, out in ((0, ada1_ref, ga1_out), (2, ada2_ref, ga2_out)):
            for j in range(2):
                c = slice(j * d, (j + 1) * d)
                sums = sums_ref[row + j : row + j + 1, :]
                out[:, c] = cond * sums
                total = total + jnp.sum(ada[:, c] * sums, axis=1, keepdims=True)
        gcond_out[...] = jnp.sum(jnp.where(eye, total, 0.0), axis=0, keepdims=True)


def local(tokens, cotangent, dest, neighbours, w_qkv, w_out, w_up, w_down, ada_attn, ada_mlp, cond):
    rows, width = tokens.shape
    z = sizes(lax.axis_size("patch"), rows, width, w_up.shape[1])
    dest = dest.reshape(1, rows)
    neighbours = neighbours.T
    cond = cond.reshape(1, cond.shape[0])
    inputs = dict(
        tokens=tokens,
        cotangent=cotangent,
        dest=dest,
        neighbours=neighbours,
        w_qkv=w_qkv,
        w_out=w_out,
        w_up=w_up,
        w_down=w_down,
        ada_attn=ada_attn,
        ada_mlp=ada_mlp,
        cond=cond,
    )
    small = ("dest", "neighbours", "cond")
    any_space = pl.BlockSpec(memory_space=pl.ANY)
    vmem = pl.BlockSpec(memory_space=pltpu.VMEM)
    shape = jax.ShapeDtypeStruct
    outs = dict(
        grads_out=pltpu.VMEM((2, STREAMS) + BLOCK, BF16),
        sums_out=pltpu.VMEM((8, width), F32),
        y_out=pltpu.VMEM((rows, width), BF16),
        g_out=pltpu.VMEM((rows, width), BF16),
    )
    held = scratch(z, neighbours.shape[0])
    held_out = pl.pallas_call(
        functools.partial(layer, z, [*inputs, *outs, *held]),
        out_shape=list(outs.values()),
        in_specs=[vmem if k in small else any_space for k in inputs],
        out_specs=[vmem, vmem, vmem, vmem],
        scratch_shapes=list(held.values()),
        compiler_params=pltpu.CompilerParams(collective_id=0, has_side_effects=True, vmem_limit_bytes=56 << 20),
        name="layer",
    )(*inputs.values())

    held_out = [pltpu.with_memory_space_constraint(v, pltpu.VMEM) for v in held_out]
    whole = lambda i, p: (0, 0)
    rows_spec = pl.BlockSpec((rows, width), whole)
    ada_spec = pl.BlockSpec(ada_attn.shape, whole)
    cond_spec = pl.BlockSpec((1, cond.shape[1]), whole)
    y, gx, g_qkv, g_out, g_up, g_down, g_ada1, g_ada2, g_cond = pl.pallas_call(
        functools.partial(finish, z),
        grid=(2, 4),
        in_specs=[
            vmem,
            vmem,
            vmem,
            vmem,
            ada_spec,
            ada_spec,
            cond_spec,
        ],
        out_specs=[
            rows_spec,
            rows_spec,
            pl.BlockSpec(BLOCK, lambda i, p: (0, i * 3 + jnp.minimum(p, 2))),
            pl.BlockSpec(BLOCK, lambda i, p: (0, i)),
            pl.BlockSpec(BLOCK, lambda i, p: (0, i * 4 + p)),
            pl.BlockSpec(BLOCK, lambda i, p: (i * 2 + p // 2, p % 2)),
            ada_spec,
            ada_spec,
            cond_spec,
        ],
        out_shape=[
            shape((rows, width), BF16),
            shape((rows, width), BF16),
            shape(w_qkv.shape, F32),
            shape(w_out.shape, F32),
            shape(w_up.shape, F32),
            shape(w_down.shape, F32),
            shape(ada_attn.shape, F32),
            shape(ada_mlp.shape, F32),
            shape(cond.shape, F32),
        ],
        compiler_params=pltpu.CompilerParams(vmem_limit_bytes=32 << 20),
        name="finish",
    )(*held_out, ada_attn, ada_mlp, cond)
    return y, gx, g_qkv, g_out, g_up, g_down, g_ada1, g_ada2, g_cond.reshape(cond.shape[1])


def solution(mesh):
    row = P(("patch", "rep"), None)
    return jax.shard_map(
        local,
        mesh=mesh,
        in_specs=(row, row, P(("patch", "rep")), row) + (P(),) * 7,
        out_specs=(row, row) + (P(),) * 7,
        check_vma=False,
    )
```

```python
import functools
import heapq
import itertools
import types

import jax
import jax.numpy as jnp
from jax import lax
from jax.experimental import pallas as pl
from jax.experimental.pallas import tpu as pltpu
from jax.sharding import PartitionSpec as P

H = 4
HD = 128
EPS = 1e-05
F32 = jnp.float32
BF16 = jnp.bfloat16
I32 = jnp.int32
MESH = pl.DeviceIdType.MESH
NN = (((1,), (0,)), ((), ()))
NT = (((1,), (1,)), ((), ()))
TN = (((0,), (0,)), ((), ()))
TILE = 32
NEVER = -1e30
LOG2E = 1.4426950408889634
BLOCK = (512, 256)
MIN_ROWS = 16


def mm(a, b, dims=NN):
    return lax.dot_general(a, b, dims, preferred_element_type=F32)


def iota(shape, axis):
    return lax.broadcasted_iota(I32, shape, axis).astype(F32)


def hot(cond):
    return jnp.where(cond, 1.0, 0.0)


def sizes(patches, rows, width, hidden):
    cap = rows // patches + 1
    block = -(-(cap - 1) // 16) * 16
    bits = patches.bit_length() - 1
    return types.SimpleNamespace(
        P=patches, R=rows, D=width, FF=hidden, T=block, PT=patches * block, bits=bits, stages=stages_of(bits)
    )


XYZ, XZY, YXZ, YZX, ZXY, ZYX = itertools.permutations(range(3))
ORDERS = [XYZ, YXZ, ZYX, XYZ, YXZ, YXZ, XYZ, XYZ, ZXY, ZXY, YXZ, YXZ]
DOWN, UP, OUT, QKV = range(0, 4), range(4, 8), range(8, 9), range(9, 12)
STREAMS = len(ORDERS)
SUMS_AT, QKV_AT, COEFF_AT = 6.5, 16.3, 15.5
COMPUTES = ((-1.0, 1.2), (1.2, 2.2), (2.2, 3.6), (3.6, 5.1), (5.1, 6.5), (6.6, 7.8), (10.4, 11.4), (11.4, 12.4), (12.4, 13.4))
COMPUTES += ((13.4, 14.4), (14.4, 15.5), (15.5, 16.2), (16.4, 17.0))
ROWS_AT = (10.5, 17.1)
ROW_TIMES = (3.2, 3.2, 4.8, 6.4)
PIECES = 4


def stages_of(bits):
    found = []
    for first in ORDERS:
        order = [(b,) for b in first if b < bits] + [(b,) for b in range(3, bits)]
        rows, stages = BLOCK[0], []
        for over in order:
            after = rows >> len(over)
            if after < MIN_ROWS:
                after = rows
            stages.append((over, rows, after))
            rows = after
        found.append(stages)
    return found


def sum_plan(bits):
    whole, delay, turn, depth = 5.7, 1.8, 0.12, 3
    steps = []
    for stages in stages_of(bits):
        places = stages + [stage for stage in reversed(stages) if stage[1] > stage[2]]
        steps.append([(over[0], whole * after / BLOCK[0]) for over, _, after in places] + [(None, 0.5)])
    steps.append([(None, 0.1)] + [(b, 0.4) for b in range(bits)])
    at = [0] * len(steps)
    free, queued, waiting, plan = {}, {}, [], []
    number = itertools.count()
    events = [(QKV_AT if p in QKV else SUMS_AT, next(number), "ready", p) for p in range(STREAMS)]
    events.append((COEFF_AT, next(number), "ready", STREAMS))
    events += [(t, next(number), "rows", None) for t in ROWS_AT]
    heapq.heapify(events)
    now = 0.0

    def able(t):
        return next((b for a, b in COMPUTES if a < t < b), t)

    while events:
        t, _, kind, p = heapq.heappop(events)
        if kind == "rows":
            for link, time in enumerate(ROW_TIMES):
                free[link] = max(free.get(link, 0.0), t) + time
            continue
        if kind == "free":
            queued[p] -= 1
            kind = "look"
        if able(max(now, t)) > max(now, t):
            heapq.heappush(events, (able(max(now, t)), next(number), kind, p))
            continue
        now = max(now, t)
        if kind == "ready":
            waiting.append(p)
        elif kind == "end":
            now += turn
            plan.append((now, p))
            at[p] += 1
            if at[p] < len(steps[p]):
                waiting.append(p)
        for q in sorted(waiting, key=lambda q: (q < STREAMS, (q - QKV[0]) % STREAMS)):
            link, time = steps[q][at[q]]
            uses = {None: ()}.get(link, ((2, 1), (3, 2)) if bits == 4 and link == 3 else ((link, 1),))
            if any(queued.get(used, 0) >= depth for used, _ in uses):
                continue
            waiting.remove(q)
            now += 0.03
            plan.append((now, q))
            done = now if uses else now + time
            for used, share in uses:
                queued[used] = queued.get(used, 0) + 1
                free[used] = max(free.get(used, 0.0), now) + time * share
                heapq.heappush(events, (free[used], next(number), "free", used))
                done = max(done, free[used])
            heapq.heappush(events, (done + delay, next(number), "end", q))
    return plan


def scratch(z, nb):
    R, D, FF, PT, PS = z.R, z.D, z.FF, z.PT, z.PT + z.P
    stages = z.stages[0]
    vm, dma = pltpu.VMEM, pltpu.SemaphoreType.DMA
    s = dict(
        tok=vm((R, D), BF16),
        cot=vm((R, D), BF16),
        wqkv=vm((D, 3 * D), BF16),
        wout=vm((D, D), BF16),
        wup=vm((D, FF), BF16),
        wdown=vm((FF, D), BF16),
        ada1=vm((32, 2 * D), F32),
        ada2=vm((32, 2 * D), F32),
        c=vm((16, 2 * D), F32),
        pick=vm((R, PS), BF16),
        place=vm((PS, R), BF16),
        out_t=vm((PT, D), BF16),
        out_c=vm((PT, D), BF16),
        in_t=vm((PS, D), BF16),
        in_c=vm((PS, D), BF16),
        home_y=vm((PS, D), BF16),
        home_g=vm((PS, D), BF16),
        more_out=vm((4, z.P, 1, D + 128), F32),
        more_in=vm((4, z.P, 1, D + 128), F32),
        x=vm((R, D), F32),
        plain1=vm((R, D), F32),
        inv1=vm((R, 128), F32),
        plain2=vm((R, D), F32),
        inv2=vm((R, 128), F32),
        resid=vm((R, D), F32),
        gresid=vm((R, D), F32),
        tmp=vm((R, D), F32),
        ups=vm((2, R, D), BF16),
        normed=vm((3, R, D), BF16),
        normed_p=vm((R, D), BF16),
        qkv=vm((3, R, 3 * D), BF16),
        cols=vm((3, nb, R), F32),
        colq=vm((R, nb), F32),
        cq=vm((R, 3 * R), F32),
        ck=vm((3, R, R), F32),
        s=vm((R, 3 * R), F32),
        s2=vm((R, 3 * R), F32),
        w=vm((H, R, 3 * R), BF16),
        low=vm((R, 3 * R), BF16),
        low2=vm((R, 3 * R), BF16),
        o=vm((2, R, D), BF16),
        u=vm((R, D), F32),
        ga=vm((R, D), F32),
        a=vm((R, FF), BF16),
        a_p=vm((R, FF // 2), BF16),
        gu=vm((R, FF), BF16),
        gu_p=vm((R, FF // 2), BF16),
        normed2=vm((2, R, D), BF16),
        gr=vm((R, D), BF16),
        gr_p=vm((R, D // 2), BF16),
        go=vm((3, R, D), BF16),
        stat=vm((R, 128), F32),
        stats=vm((3, 2 * H, R), F32),
        gqkv=vm((R, 3 * D), BF16),
        gqkv_p=vm((R, 3 * D // 2), BF16),
        acc=vm((STREAMS,) + BLOCK, BF16),
        **{f"rcv{k}": vm((STREAMS, (1 << len(b)) - 1, n, BLOCK[1]), BF16) for k, (b, _, n) in enumerate(stages)},
        gcs=vm((z.bits + 2, 8, D), F32),
        gcr=vm((z.bits + 1, 8, D), F32),
        load_sem=dma((8,)),
        row_ss=dma((4,)),
        row_rs=dma((4,)),
        own_sem=dma((4,)),
        more_ss=dma((4,)),
        more_rs=dma((4,)),
        more_own=dma((4,)),
        side_ss=dma((4, 2)),
        side_rs=dma((4, 2)),
        piece_rs=dma((2, PIECES)),
        pair_ss=dma((8,)),
        pair_rs=dma((8,)),
        sum_ss=dma((1,)),
        late_ss=dma((STREAMS, len(stages))),
        rs_rs=dma((STREAMS, len(stages))),
        ag_rs=dma((STREAMS, len(stages))),
        core_ss=dma((1,)),
        core_rs=dma((1,)),
        gc_ss=dma((1,)),
        gc_rs=dma((z.bits + 1,)),
    )
    return s


def marker():
    def phase(name):
        del name

    return phase


def layer(z, names, *refs):
    n = types.SimpleNamespace(**dict(zip(names, refs, strict=True)))
    Pn, R, D, FF, T, PT, PS = z.P, z.R, z.D, z.FF, z.T, z.PT, z.PT + z.P
    me = lax.axis_index("patch")
    rp = lax.axis_index("rep")
    mate = 1 - rp
    nxt = lax.rem(me + 1, Pn)
    prv = lax.rem(me + Pn - 1, Pn)
    started = []
    phase = marker()

    def tiles(total, fn, init=0, size=TILE, together=1):
        def some(i, carry):
            for j in range(together):
                carry = fn(pl.ds(pl.multiple_of((i * together + j) * size, size), size), carry)
            return carry

        return lax.fori_loop(0, total // (size * together), some, init)

    def load(i, src, dst):
        copy = pltpu.make_async_copy(src, dst, n.load_sem.at[i])
        copy.start()
        return copy

    phase("entry")
    get_tok = load(0, n.tokens, n.tok)
    get_cot = load(1, n.cotangent, n.cot)
    get_ada1 = load(2, n.ada_attn, n.ada1)
    get_ada2 = load(3, n.ada_mlp, n.ada2)
    get_wqkv = load(4, n.w_qkv, n.wqkv)
    get_wdown = load(5, n.w_down, n.wdown)
    get_wout = load(6, n.w_out, n.wout)
    get_wup = load(7, n.w_up, n.wup)

    barrier = pltpu.get_barrier_semaphore()

    def greet(i, carry):
        pl.semaphore_signal(barrier, inc=1, device_id=(lax.rem(me + i, Pn), rp), device_id_type=MESH)
        return carry

    lax.fori_loop(1, Pn, greet, 0)
    pl.semaphore_signal(barrier, inc=1, device_id=(me, mate), device_id_type=MESH)

    def remote(src, dst, ss, rs, to, keep=False):
        copy = pltpu.make_async_remote_copy(
            src_ref=src, dst_ref=dst, send_sem=ss, recv_sem=rs, device_id=to, device_id_type=MESH
        )
        copy.start()
        if keep:
            started.append(copy)
        return copy

    def send_rows(i, src, dst):
        def one(j, carry):
            to = me ^ (Pn - j)
            pltpu.make_async_remote_copy(
                src_ref=src.at[pl.ds(pl.multiple_of(to * T, 16), T)],
                dst_ref=dst.at[pl.ds(pl.multiple_of(me * T, 16), T)],
                send_sem=n.row_ss.at[i],
                recv_sem=n.row_rs.at[i],
                device_id=(to, rp),
                device_id_type=MESH,
            ).start()
            pltpu.make_async_remote_copy(
                src_ref=n.more_out.at[i, to],
                dst_ref=n.more_in.at[i, me],
                send_sem=n.more_ss.at[i],
                recv_sem=n.more_rs.at[i],
                device_id=(to, rp),
                device_id_type=MESH,
            ).start()
            return carry

        lax.fori_loop(1, Pn, one, 0)
        mine = pl.ds(pl.multiple_of(me * T, 16), T)
        pltpu.make_async_copy(src.at[mine], dst.at[mine], n.own_sem.at[i]).start()
        pltpu.make_async_copy(n.more_out.at[i, me], n.more_in.at[i, me], n.more_own.at[i]).start()

    def waits_for(ref, sem):
        pltpu.make_async_copy(ref, ref, sem).wait()

    def rows_in(i, dst):
        waits_for(n.more_in.at[i, pl.ds(0, Pn - 1)], n.more_rs.at[i])
        waits_for(n.more_in.at[i, 0], n.more_own.at[i])
        waits_for(dst.at[pl.ds(0, PT - T)], n.row_rs.at[i])
        waits_for(dst.at[pl.ds(0, T)], n.own_sem.at[i])
        dst[PT:PS] = n.more_in[i, :, 0, :D].astype(BF16)

    def rows_gone(i, src):
        waits_for(src.at[pl.ds(0, PT - T)], n.row_ss.at[i])
        waits_for(n.more_out.at[i, pl.ds(0, Pn - 1)], n.more_ss.at[i])

    def set_rows(i, hot_rows, values, out):
        total = mm(hot_rows, values)
        out[...] = total[:PT].astype(BF16)
        n.more_out[i, :, 0, :D] = total[PT:]

    even = lax.rem(me, 2) == 0
    near = me ^ 1
    near_slot = jnp.where(even, 2, 0)
    far_slot = 2 - near_slot
    onward = lax.rem(jnp.where(even, me + 2, me + Pn - 2), Pn)

    def to_sides(i, ref):
        return (
            remote(ref.at[1], ref.at[0], n.side_ss.at[i, 0], n.side_rs.at[i, 0], (nxt, rp), True),
            remote(ref.at[1], ref.at[2], n.side_ss.at[i, 1], n.side_rs.at[i, 1], (prv, rp), True),
        )

    def to_near(i, ref, c):
        size = R // PIECES
        return remote(
            ref.at[1, pl.ds(c * size, size)],
            ref.at[far_slot, pl.ds(c * size, size)],
            n.side_ss.at[i, 0],
            n.piece_rs.at[i - 1, c],
            (near, rp),
        )

    def hand_on(i, ref, copies):
        size = R // PIECES
        for copy in copies:
            c = len(handed[i])
            copy.wait_recv()
            handed[i].append(
                remote(
                    ref.at[near_slot, pl.ds(c * size, size)],
                    ref.at[far_slot, pl.ds(c * size, size)],
                    n.side_ss.at[i, 1],
                    n.side_rs.at[i, 1],
                    (onward, rp),
                )
            )

    handed = {1: [], 2: []}

    def far_in(i, ref):
        waits_for(ref.at[far_slot], n.side_rs.at[i, 1])

    def to_mate(i, src, dst):
        return remote(src, dst, n.pair_ss.at[i], n.pair_rs.at[i], (me, mate), True)

    n.cols[1] = lists_of(z, n.neighbours[...], me)
    dest = n.dest[...].astype(F32)
    mine_hot = iota((Pn, R), 0) == dest
    before = hot(iota((R, R), 0) < iota((R, R), 1)).astype(BF16)
    earlier = mm(hot(mine_hot).astype(BF16), before)
    rank = jnp.sum(jnp.where(mine_hot, earlier, 0.0), axis=0, keepdims=True)
    code = jnp.where(rank < T, dest * T + rank, PT + dest)
    pick = hot(code == iota((PS, R), 0))
    pick_low = pick.astype(BF16)
    get_tok.wait()
    set_rows(0, pick_low, n.tok[...], n.out_t)
    n.more_out[0, :, 0, D:] = jnp.broadcast_to(jnp.sum(hot(mine_hot), axis=1, keepdims=True), (Pn, 128))
    phase("barrier")
    pl.semaphore_wait(barrier, Pn)
    phase("send tokens")
    side_lists = to_sides(0, n.cols)
    send_rows(0, n.out_t, n.in_t)
    get_cot.wait()
    set_rows(1, pick_low, n.cot[...], n.out_c)
    n.pick[...] = pick.T.astype(BF16)

    phase("counts")
    get_ada1.wait()
    get_ada2.wait()
    cond = jnp.broadcast_to(n.cond[...], (8, n.cond.shape[1]))
    n.c[0:8] = jnp.dot(cond, n.ada1[...], precision=lax.Precision.HIGHEST, preferred_element_type=F32)
    n.c[8:16] = jnp.dot(cond, n.ada2[...], precision=lax.Precision.HIGHEST, preferred_element_type=F32)
    n.colq[...] = n.cols[1].T
    lists = n.cols.shape[1]

    def count_q(t, carry):
        ids = iota((TILE, 3 * R), 1)
        col = n.colq[t, :]
        total = jnp.zeros((TILE, 3 * R), F32)
        for j in range(lists):
            total = total + hot(col[:, j : j + 1] == ids)
        n.cq[t, :] = jnp.where(total > 0.0, jnp.log2(total), NEVER)
        return carry

    tiles(R, count_q)

    def count_k(side, base):
        def one(t, carry):
            ids = iota((TILE, R), 0) + (t.start + base).astype(F32)
            total = jnp.zeros((TILE, R), F32)
            for j in range(lists):
                total = total + hot(n.cols[side, j : j + 1, :] == ids)
            n.ck[side, t, :] = jnp.where(total > 0.0, jnp.log2(total), NEVER)
            return carry

        tiles(R, one)

    count_k(1, R)
    phase("side counts")
    for lists_copy in side_lists:
        lists_copy.wait_recv()
    count_k(0, 2 * R)
    count_k(2, 0)

    phase("places")
    row = iota((PS, 1), 0)
    source = jnp.where(row < PT, jnp.floor((row + 0.5) * (1.0 / T)), row - PT)
    step = jnp.where(row < PT, row - source * T, T * 1.0)
    spread = hot(source == iota((PS, Pn), 1)).astype(BF16)
    earlier_sources = hot(iota((Pn, Pn), 0) > iota((Pn, Pn), 1)).astype(BF16)
    phase("wait tokens")
    rows_in(0, n.in_t)
    phase("place rows")
    count = n.more_in[0, :, 0, D:].astype(BF16)
    offset = mm(earlier_sources, count).astype(BF16)
    position = jnp.where(step < mm(spread, count)[:, 0:1], mm(spread, offset)[:, 0:1] + step, -1.0)
    place = hot(position == iota((PS, R), 1))
    n.place[...] = place.astype(BF16)
    place_t = place.T.astype(BF16)
    n.x[...] = mm(place_t, n.in_t[...])

    def norm(src, coeffs, plain_ref, inv_ref, out, after=None):
        def one(t, carry):
            v = src[t, :]
            centred = v - jnp.sum(v, axis=-1, keepdims=True) * (1.0 / D)
            inverse = lax.rsqrt(jnp.sum(centred * centred, axis=-1, keepdims=True) * (1.0 / D) + EPS)
            plain = centred * inverse
            plain_ref[t, :] = plain
            inv_ref[t, :] = jnp.broadcast_to(inverse, (TILE, 128))
            out[t, :] = (plain * (1.0 + n.c[coeffs : coeffs + 1, :D]) + n.c[coeffs : coeffs + 1, D:]).astype(BF16)
            return carry

        for c in range(PIECES):
            size = R // PIECES
            for j in range(size // TILE):
                one(pl.ds(c * size + j * TILE, TILE), 0)
            if after:
                after(c)

    def norm_back(grad, coeffs, plain_ref, inv_ref, finish):
        def one(t, carry):
            g = grad[t, :]
            plain = plain_ref[t, :]
            scaled = g * (1.0 + n.c[coeffs : coeffs + 1, :D])
            mean = jnp.sum(scaled, axis=-1, keepdims=True) * (1.0 / D)
            along = jnp.sum(scaled * plain, axis=-1, keepdims=True) * (1.0 / D)
            finish(t, inv_ref[t, 0:1] * (scaled - mean - plain * along))
            return (
                carry[0] + jnp.sum(g * plain, axis=0, keepdims=True),
                carry[1] + jnp.sum(g, axis=0, keepdims=True),
            )

        zero = jnp.zeros((1, D), F32)
        return tiles(R, one, (zero, zero), together=4)

    phase("norm")
    side_normed = []
    norm(n.x, 0, n.plain1, n.inv1, n.normed.at[1], lambda c: side_normed.append(to_near(1, n.normed, c)))
    mate_normed = to_mate(0, n.normed.at[1], n.normed_p)
    phase("project")
    get_wqkv.wait()

    def project(side):
        for j in range(3):
            c = slice(j * D, (j + 1) * D)
            n.qkv[side, :, c] = mm(n.normed[side], n.wqkv[:, c]).astype(BF16)

    project(1)
    phase("wait halo")
    hand_on(1, n.normed, side_normed)
    send_rows(1, n.out_c, n.in_c)
    project(near_slot)
    phase("wait far")
    far_in(1, n.normed)
    project(far_slot)

    phase("attention")
    scale = 1.0 / HD**0.5

    def part(which, h):
        return slice(which * D + h * HD, which * D + (h + 1) * HD)

    for h in range(H):
        for side in range(3):
            n.s[:, side * R : (side + 1) * R] = mm(n.qkv[1, :, part(0, h)], n.qkv[side, :, part(1, h)], NT)

        def soft(t, carry, h=h):
            s = n.s[t, :] * (scale * LOG2E) + n.cq[t, :]
            top = jnp.max(s, axis=-1, keepdims=True)
            e = jnp.exp2(s - top)
            total = jnp.sum(e, axis=-1, keepdims=True)
            w = e * (1.0 / total)
            n.w[h, t, :] = w.astype(BF16)
            n.stat[t, h : h + 1] = top + jnp.log2(total)
            return carry

        tiles(R, soft, together=8)
        mixed = jnp.zeros((R, HD), F32)
        for side in range(3):
            mixed = mixed + mm(n.w[h, :, side * R : (side + 1) * R], n.qkv[side, :, part(2, h)])
        n.o[0, :, h * HD : (h + 1) * HD] = mixed.astype(BF16)
    mate_o = to_mate(2, n.o.at[0], n.o.at[1])

    phase("wait upstream")
    rows_in(1, n.in_c)
    n.ups[0] = mm(place_t, n.in_c[...]).astype(BF16)
    mate_ups = to_mate(1, n.ups.at[0], n.ups.at[1])
    phase("resid")
    get_wout.wait()
    n.resid[...] = n.x[...] + mm(n.o[0], n.wout[...])
    norm(n.resid, 8, n.plain2, n.inv2, n.normed2.at[0])
    mate_normed2 = to_mate(3, n.normed2.at[0], n.normed2.at[1])
    get_wup.wait()
    get_wdown.wait()
    phase("mlp")
    half = FF // 2
    for j in range(FF // D):
        c = slice(j * D, (j + 1) * D)
        n.u[...] = mm(n.normed2[0], n.wup[:, c])
        n.ga[...] = mm(n.ups[0], n.wdown[c, :], NT)

        def gate(t, carry, c=c):
            u = n.u[t, :]
            sig = 1.0 / (1.0 + jnp.exp(-u))
            n.a[t, c] = (u * sig).astype(BF16)
            n.gu[t, c] = (n.ga[t, :] * sig * (1.0 + u * (1.0 - sig))).astype(BF16)
            return carry

        tiles(R, gate, together=8)
    theirs = pl.ds(pl.multiple_of(mate * half, 128), half)
    ours = pl.ds(pl.multiple_of(rp * half, 128), half)
    mate_a = to_mate(4, n.a.at[:, theirs], n.a_p)
    mate_gu = to_mate(5, n.gu.at[:, theirs], n.gu_p)
    phase("mlp back")
    n.tmp[...] = mm(n.gu[...], n.wup[...], NT)

    def keep2(t, gw):
        total = n.ups[0, t, :].astype(F32) + gw
        n.gresid[t, :] = total
        n.gr[t, :] = total.astype(BF16)

    gc2 = norm_back(n.tmp, 8, n.plain2, n.inv2, keep2)
    phase("go")
    n.go[1] = mm(n.gr[...], n.wout[...], NT).astype(BF16)
    side_go = [to_near(2, n.go, c) for c in range(PIECES)]
    quarter = D // 2
    mate_gr = to_mate(6, n.gr.at[:, pl.ds(pl.multiple_of(mate * quarter, 128), quarter)], n.gr_p)
    live = {}

    def place_in(p, k):
        return sum(((me >> b) & 1) << i for i, b in enumerate(z.stages[p][k][0]))

    def start_of(p, k):
        return sum(place_in(p, i) * z.stages[p][i][2] for i in range(k) if z.stages[p][i][1] > z.stages[p][i][2])

    def span(p, k):
        rows = z.stages[p][k - 1][2] if k else BLOCK[0]
        return pl.ds(pl.multiple_of(start_of(p, k), rows) if k else 0, rows)

    def partners(p, k):
        over = z.stages[p][k][0]
        for j in range(1, 1 << len(over)):
            yield j, (me ^ sum(1 << b for i, b in enumerate(over) if j >> i & 1), rp)

    def reduce_start(p, k):
        _, rows, after = z.stages[p][k]
        for j, to in partners(p, k):
            if after < rows:
                at = start_of(p, k) + (place_in(p, k) ^ j) * after
                src, ss = n.acc.at[p, pl.ds(pl.multiple_of(at, after), after)], n.sum_ss.at[0]
            else:
                src, ss = n.acc.at[p, span(p, k)], n.late_ss.at[p, k]
            live[p] = remote(src, getattr(n, f"rcv{k}").at[p, j - 1], ss, n.rs_rs.at[p, k], to)

    def reduce_end(p, k):
        _, rows, after = z.stages[p][k]
        got = getattr(n, f"rcv{k}")
        waits_for(got.at[p], n.rs_rs.at[p, k])
        if after == rows:
            live[p].wait_send()
        kept = span(p, k + 1)
        total = n.acc[p, kept].astype(F32)
        for j in range(got.shape[1]):
            total = total + got[p, j].astype(F32)
        into = n.grads_out.at[rp, p, kept] if k + 1 == len(z.stages[p]) else n.acc.at[p, kept]
        into[...] = total.astype(BF16)

    def gather_start(p, k):
        ref = n.grads_out.at[rp, p, span(p, k + 1)]
        for _, to in partners(p, k):
            remote(ref, ref, n.sum_ss.at[0], n.ag_rs.at[p, k], to)

    def gather_end(p, k):
        _, rows, after = z.stages[p][k]
        waits_for(n.grads_out.at[rp, p, pl.ds(0, rows - after)], n.ag_rs.at[p, k])

    def core_start(p):
        ref = n.grads_out.at[rp, p]
        remote(ref, ref, n.core_ss.at[0], n.core_rs.at[0], (me, mate))

    steps_left = {}
    for p in range(STREAMS):
        steps = []
        kept = [k for k, stage in enumerate(z.stages[p]) if stage[1] > stage[2]]
        for k in range(len(z.stages[p])):
            steps += [functools.partial(reduce_start, p, k), functools.partial(reduce_end, p, k)]
        for k in reversed(kept):
            steps += [functools.partial(gather_start, p, k), functools.partial(gather_end, p, k)]
        steps += [functools.partial(core_start, p), lambda: None]
        steps_left[p] = steps

    def small_start(k):
        to = (me, mate) if k == 0 else (me ^ (1 << (k - 1)), rp)
        live["gc"] = remote(n.gcs.at[k], n.gcr.at[k], n.gc_ss.at[0], n.gc_rs.at[k], to)

    def small_end(k):
        live["gc"].wait_recv()
        n.gcs[k + 1] = n.gcs[k] + n.gcr[k]

    steps = []
    for k in range(z.bits + 1):
        steps += [functools.partial(small_start, k), functools.partial(small_end, k)]
    steps_left[STREAMS] = steps
    actions = sum_plan(z.bits)

    def service(until=None):
        while actions and (until is None or actions[0][0] <= until):
            phase(f"sums {2 * int(actions[0][0] / 2)}")
            steps_left[actions.pop(0)[1]].pop(0)()

    phase("grad down")
    mate_ups.wait_recv()
    mate_a.wait_recv()
    for j in range(2):
        r = pl.ds(pl.multiple_of(rp * half + j * BLOCK[0], 128), BLOCK[0])
        for i in range(2):
            c = slice(i * BLOCK[1], (i + 1) * BLOCK[1])
            total = mm(n.a[:, r], n.ups[0, :, c], TN) + mm(n.a_p[:, j * BLOCK[0] : (j + 1) * BLOCK[0]], n.ups[1, :, c], TN)
            n.acc[2 * j + i] = total.astype(BF16)
    phase("grad up")
    mate_normed2.wait_recv()
    mate_gu.wait_recv()
    for p in range(len(UP)):
        c = pl.ds(pl.multiple_of(rp * half + p * BLOCK[1], 128), BLOCK[1])
        d = slice(p * BLOCK[1], (p + 1) * BLOCK[1])
        n.acc[UP[p]] = (mm(n.normed2[0], n.gu[:, c], TN) + mm(n.normed2[1], n.gu_p[:, d], TN)).astype(BF16)
    mate_o.wait_recv()
    mate_gr.wait_recv()
    c = pl.ds(pl.multiple_of(rp * quarter, 128), quarter)
    n.acc[OUT[0]] = (mm(n.o[0], n.gr[:, c], TN) + mm(n.o[1], n.gr_p[...], TN)).astype(BF16)

    phase("query back")
    for h in range(H):
        head = slice(h * HD, (h + 1) * HD)
        for side in range(3):
            n.s[:, side * R : (side + 1) * R] = mm(n.go[1, :, head], n.qkv[side, :, part(2, h)], NT)

        def soft_back(t, carry, h=h):
            w = n.w[h, t, :].astype(F32)
            gp = n.s[t, :]
            delta = jnp.sum(w * gp, axis=-1, keepdims=True)
            n.low[t, :] = (w * (gp - delta)).astype(BF16)
            n.stat[t, H + h : H + h + 1] = delta
            return carry

        tiles(R, soft_back, together=8)
        total = jnp.zeros((R, HD), F32)
        for side in range(3):
            total = total + mm(n.low[:, side * R : (side + 1) * R], n.qkv[side, :, part(1, h)])
        n.gqkv[:, part(0, h)] = (total * scale).astype(BF16)
        if h < PIECES:
            hand_on(2, n.go, side_go[h : h + 1])
    n.stats[1] = n.stat[...].T[0 : 2 * H]
    side_stats = to_sides(3, n.stats)
    phase("y")
    y = (n.resid[...] + mm(n.a[...], n.wdown[...])).astype(BF16)
    rows_gone(0, n.out_t)
    set_rows(2, n.place[...], y, n.out_t)

    service(10.3)

    phase("sums step")
    for copy in side_stats:
        copy.wait_recv()
    far_in(2, n.go)
    send_rows(2, n.out_t, n.home_y)
    phase("key back")
    for h in range(H):
        head = slice(h * HD, (h + 1) * HD)
        for side in range(3):
            span_q = slice(side * R, (side + 1) * R)
            n.s[:, span_q] = mm(n.qkv[1, :, part(1, h)], n.qkv[side, :, part(0, h)], NT)
            n.s2[:, span_q] = mm(n.qkv[1, :, part(2, h)], n.go[side, :, head], NT)

        def key_back(t, carry, h=h):
            for side in range(3):
                span_q = slice(side * R, (side + 1) * R)
                s = n.s[t, span_q] * (scale * LOG2E) + n.ck[side, t, :]
                w = jnp.exp2(s - n.stats[side, h : h + 1, :])
                n.low[t, span_q] = w.astype(BF16)
                n.low2[t, span_q] = (w * (n.s2[t, span_q] - n.stats[side, H + h : H + h + 1, :])).astype(BF16)
            return carry

        tiles(R, key_back, together=4)
        total_k = jnp.zeros((R, HD), F32)
        total_v = jnp.zeros((R, HD), F32)
        for side in range(3):
            span_q = slice(side * R, (side + 1) * R)
            total_k = total_k + mm(n.low2[:, span_q], n.qkv[side, :, part(0, h)])
            total_v = total_v + mm(n.low[:, span_q], n.go[side, :, head])
        n.gqkv[:, part(1, h)] = (total_k * scale).astype(BF16)
        n.gqkv[:, part(2, h)] = total_v.astype(BF16)
        service(11.45 + h)
    phase("send gqkv")
    wide = 3 * D // 2
    mate_gqkv = to_mate(7, n.gqkv.at[:, pl.ds(pl.multiple_of(mate * wide, 128), wide)], n.gqkv_p)
    phase("gx")
    n.tmp[...] = mm(n.gqkv[...], n.wqkv[...], NT)
    gx_ref = n.tok

    def keep1(t, gw):
        gx_ref[t, :] = (n.gresid[t, :] + gw).astype(BF16)

    gc1 = norm_back(n.tmp, 0, n.plain1, n.inv1, keep1)
    row = lax.broadcasted_iota(I32, (8, D), 0)
    sums = jnp.zeros((8, D), F32)
    for i, value in enumerate((*gc1, *gc2)):
        sums = jnp.where(row == i, value, sums)
    n.gcs[0] = sums

    service(15.6)
    mate_gqkv.wait_recv()
    mate_normed.wait_recv()
    phase("grad qkv")
    for p in range(3):
        c = pl.ds(pl.multiple_of(rp * wide + p * BLOCK[1], 128), BLOCK[1])
        d = slice(p * BLOCK[1], (p + 1) * BLOCK[1])
        n.acc[QKV[p]] = (mm(n.normed[1], n.gqkv[:, c], TN) + mm(n.normed_p[...], n.gqkv_p[:, d], TN)).astype(BF16)
    phase("leave gx")
    service(16.5)
    rows_gone(1, n.out_c)
    set_rows(3, n.place[...], gx_ref[...], n.out_c)
    send_rows(3, n.out_c, n.home_g)
    phase("sums")
    service()
    waits_for(n.grads_out.at[mate], n.core_rs.at[0])
    n.sums_out[...] = n.gcs[z.bits + 1]
    phase("home")
    rows_in(2, n.home_y)
    n.y_out[...] = mm(n.pick[...], n.home_y[...]).astype(BF16)
    rows_in(3, n.home_g)
    n.g_out[...] = mm(n.pick[...], n.home_g[...]).astype(BF16)

    phase("end")
    rows_gone(2, n.out_t)
    rows_gone(3, n.out_c)
    for copy in started:
        copy.wait_send()
    for i, ref in ((1, n.normed), (2, n.go)):
        for leg in range(2):
            waits_for(ref.at[1], n.side_ss.at[i, leg])
    waits_for(n.grads_out.at[:, :, pl.ds(0, BLOCK[0] - z.stages[0][-1][2])], n.sum_ss.at[0])
    waits_for(n.grads_out.at[rp], n.core_ss.at[0])
    waits_for(n.gcr, n.gc_ss.at[0])


def lists_of(z, neighbours, me):
    within = neighbours & (z.R - 1)
    shift = (2 * z.R).bit_length() - 1
    away = (neighbours >> shift) - me
    after = (away == 1) | (away == 1 - z.P)
    base = jnp.where(away == 0, z.R, jnp.where(after, 2 * z.R, 0))
    return (base + within).astype(F32)


def finish(z, g_ref, sums_ref, y_ref, gx_ref, ada1_ref, ada2_ref, cond_ref, *rest):
    y_out, gx_out, qkv_out, out_out, up_out, down_out, ga1_out, ga2_out, gcond_out, wide, wide_sem, row_sem = rest
    rows = [pltpu.make_async_copy(a, b, row_sem.at[i]) for i, (a, b) in enumerate(((y_ref, y_out), (gx_ref, gx_out)))]
    for copy in rows:
        copy.start()
    high, across = BLOCK
    copies = []
    for i in range(2):
        for p in range(STREAMS):
            if p in DOWN:
                r, c, out = 2 * i + p // 2, p % 2, down_out
            elif p in UP:
                r, c, out = 0, len(UP) * i + p - UP[0], up_out
            elif p in OUT:
                r, c, out = 0, i, out_out
            else:
                r, c, out = 0, len(QKV) * i + p - QKV[0], qkv_out
            wide[i, p] = g_ref[i, p].astype(F32)
            to = out.at[r * high : (r + 1) * high, c * across : (c + 1) * across]
            copies.append(pltpu.make_async_copy(wide.at[i, p], to, wide_sem.at[i, p]))
            copies[-1].start()
    count = cond_ref.shape[1]
    eye = lax.broadcasted_iota(I32, (count, count), 0) == lax.broadcasted_iota(I32, (count, count), 1)
    cond = jnp.sum(jnp.where(eye, cond_ref[...], 0.0), axis=1, keepdims=True)
    d = z.D
    total = jnp.zeros((count, 1), F32)
    for row, ada, out in ((0, ada1_ref, ga1_out), (2, ada2_ref, ga2_out)):
        for j in range(2):
            c = slice(j * d, (j + 1) * d)
            sums = sums_ref[row + j : row + j + 1, :]
            out[:, c] = cond * sums
            total = total + jnp.sum(ada[:, c] * sums, axis=1, keepdims=True)
    gcond_out[...] = jnp.sum(jnp.where(eye, total, 0.0), axis=0, keepdims=True)
    for copy in (*copies, *rows):
        copy.wait()


def local(tokens, cotangent, dest, neighbours, w_qkv, w_out, w_up, w_down, ada_attn, ada_mlp, cond):
    rows, width = tokens.shape
    z = sizes(lax.axis_size("patch"), rows, width, w_up.shape[1])
    dest = dest.reshape(1, rows)
    neighbours = neighbours.T
    cond = cond.reshape(1, cond.shape[0])
    inputs = dict(
        tokens=tokens,
        cotangent=cotangent,
        dest=dest,
        neighbours=neighbours,
        w_qkv=w_qkv,
        w_out=w_out,
        w_up=w_up,
        w_down=w_down,
        ada_attn=ada_attn,
        ada_mlp=ada_mlp,
        cond=cond,
    )
    small = ("dest", "neighbours", "cond")
    any_space = pl.BlockSpec(memory_space=pl.ANY)
    vmem = pl.BlockSpec(memory_space=pltpu.VMEM)
    shape = jax.ShapeDtypeStruct
    outs = dict(
        grads_out=pltpu.VMEM((2, STREAMS) + BLOCK, BF16),
        sums_out=pltpu.VMEM((8, width), F32),
        y_out=pltpu.VMEM((rows, width), BF16),
        g_out=pltpu.VMEM((rows, width), BF16),
    )
    held = scratch(z, neighbours.shape[0])
    held_out = pl.pallas_call(
        functools.partial(layer, z, [*inputs, *outs, *held]),
        out_shape=list(outs.values()),
        in_specs=[vmem if k in small else any_space for k in inputs],
        out_specs=[vmem, vmem, vmem, vmem],
        scratch_shapes=list(held.values()),
        compiler_params=pltpu.CompilerParams(collective_id=0, has_side_effects=True, vmem_limit_bytes=56 << 20),
        name="layer",
    )(*inputs.values())

    held_out = [pltpu.with_memory_space_constraint(v, pltpu.VMEM) for v in held_out]
    y, gx, g_qkv, g_out, g_up, g_down, g_ada1, g_ada2, g_cond = pl.pallas_call(
        functools.partial(finish, z),
        in_specs=[vmem] * 7,
        out_specs=[any_space] * 6 + [vmem] * 3,
        scratch_shapes=[
            pltpu.VMEM((2, STREAMS) + BLOCK, F32),
            pltpu.SemaphoreType.DMA((2, STREAMS)),
            pltpu.SemaphoreType.DMA((2,)),
        ],
        out_shape=[
            shape((rows, width), BF16),
            shape((rows, width), BF16),
            shape(w_qkv.shape, F32),
            shape(w_out.shape, F32),
            shape(w_up.shape, F32),
            shape(w_down.shape, F32),
            shape(ada_attn.shape, F32),
            shape(ada_mlp.shape, F32),
            shape(cond.shape, F32),
        ],
        compiler_params=pltpu.CompilerParams(vmem_limit_bytes=32 << 20),
        name="finish",
    )(*held_out, ada_attn, ada_mlp, cond)
    return y, gx, g_qkv, g_out, g_up, g_down, g_ada1, g_ada2, g_cond.reshape(cond.shape[1])


def solution(mesh):
    row = P(("patch", "rep"), None)
    return jax.shard_map(
        local,
        mesh=mesh,
        in_specs=(row, row, P(("patch", "rep")), row) + (P(),) * 7,
        out_specs=(row, row) + (P(),) * 7,
        check_vma=False,
    )
```

```python
import functools
import heapq
import itertools
import types

import jax
import jax.numpy as jnp
from jax import lax
from jax.experimental import pallas as pl
from jax.experimental.pallas import tpu as pltpu
from jax.sharding import PartitionSpec as P

H = 4
HD = 128
EPS = 1e-05
F32 = jnp.float32
BF16 = jnp.bfloat16
I32 = jnp.int32
MESH = pl.DeviceIdType.MESH
NN = (((1,), (0,)), ((), ()))
NT = (((1,), (1,)), ((), ()))
TN = (((0,), (0,)), ((), ()))
TILE = 32
NEVER = -1e30
LOG2E = 1.4426950408889634
BLOCK = (512, 256)
MIN_ROWS = 64


def mm(a, b, dims=NN):
    return lax.dot_general(a, b, dims, preferred_element_type=F32)


def iota(shape, axis):
    return lax.broadcasted_iota(I32, shape, axis).astype(F32)


def hot(cond):
    return jnp.where(cond, 1.0, 0.0)


def sizes(patches, rows, width, hidden):
    cap = rows // patches + 1
    block = -(-(cap - 1) // 16) * 16
    bits = patches.bit_length() - 1
    return types.SimpleNamespace(
        P=patches, R=rows, D=width, FF=hidden, T=block, PT=patches * block, bits=bits, stages=stages_of(bits)
    )


XYZ, XZY, YXZ, YZX, ZXY, ZYX = itertools.permutations(range(3))
ORDERS = [ZXY, ZXY, ZXY, YXZ, XYZ, XYZ, YXZ, XYZ, YXZ, YZX, XYZ, YXZ]
DOWN, UP, OUT, QKV = range(0, 4), range(4, 8), range(8, 9), range(9, 12)
STREAMS = len(ORDERS)
SUMS_AT, FIRST_AT = (6.4, 8.5, 9.5), (6.4, 2.2, 2.2)
QKV_AT, COEFF_AT = 16.3, 15.5
COMPUTES = ((-1.0, 2.2), (2.3, 3.0), (3.0, 3.6), (3.6, 5.1), (5.1, 6.4), (10.4, 11.4), (11.4, 12.4), (12.4, 13.4))
COMPUTES += ((13.4, 14.4), (14.4, 15.5), (15.5, 16.2), (16.4, 17.0))
ROW_LOADS = ((1.2, (0.0, 1.6, 2.4, 3.2)), (3.0, (3.0, 5.7, 2.9)), (10.5, (3.2, 1.6, 2.4, 3.2)), (17.1, (3.2, 3.2, 4.8, 6.4)))
PIECES = 4


def stages_of(bits):
    found = []
    for first in ORDERS:
        order = [(b,) for b in first if b < bits] + [(b,) for b in range(3, bits)]
        rows, stages = BLOCK[0], []
        for over in order:
            after = rows >> len(over)
            if after < MIN_ROWS:
                after = rows
            stages.append((over, rows, after))
            rows = after
        found.append(stages)
    return found


def sum_plan(bits):
    whole, delay, turn, depth = 5.7, 1.8, 0.12, 3
    steps = []
    for stages in stages_of(bits):
        places = stages + [stage for stage in reversed(stages) if stage[1] > stage[2]]
        steps.append([(over[0], whole * after / BLOCK[0]) for over, _, after in places] + [(None, 0.5)])
    steps.append([(None, 0.1)] + [(b, 0.4) for b in range(bits)])
    at = [0] * len(steps)
    free, queued, waiting, plan = {}, {}, [], []
    number = itertools.count()
    events, begun = [], set()
    for p in range(STREAMS):
        first = ORDERS[p][0]
        begin = QKV_AT if p in QKV else SUMS_AT[first] if first in begun else FIRST_AT[first]
        events.append((begin, next(number), "ready", p))
        begun.add(first)
    events.append((COEFF_AT, next(number), "ready", STREAMS))
    events += [(t, next(number), "rows", times) for t, times in ROW_LOADS]
    heapq.heapify(events)
    now = 0.0

    def able(t):
        return next((b for a, b in COMPUTES if a < t < b), t)

    while events:
        t, _, kind, p = heapq.heappop(events)
        if kind == "rows":
            for link, time in enumerate(p):
                free[link] = max(free.get(link, 0.0), t) + time
            continue
        if kind == "free":
            queued[p] -= 1
            kind = "look"
        if able(max(now, t)) > max(now, t):
            heapq.heappush(events, (able(max(now, t)), next(number), kind, p))
            continue
        now = max(now, t)
        if kind == "ready":
            waiting.append(p)
        elif kind == "end":
            now += turn
            plan.append((now, p))
            at[p] += 1
            if at[p] < len(steps[p]):
                waiting.append(p)
        for q in sorted(waiting, key=lambda q: (q < STREAMS, (q - QKV[0]) % STREAMS)):
            link, time = steps[q][at[q]]
            uses = {None: ()}.get(link, ((2, 1), (3, 2)) if bits == 4 and link == 3 else ((link, 1),))
            if any(queued.get(used, 0) >= depth for used, _ in uses):
                continue
            waiting.remove(q)
            now += 0.03
            plan.append((now, q))
            done = now if uses else now + time
            for used, share in uses:
                queued[used] = queued.get(used, 0) + 1
                free[used] = max(free.get(used, 0.0), now) + time * share
                heapq.heappush(events, (free[used], next(number), "free", used))
                done = max(done, free[used])
            heapq.heappush(events, (done + delay, next(number), "end", q))
    return plan


def scratch(z, nb):
    R, D, FF, PT, PS = z.R, z.D, z.FF, z.PT, z.PT + z.P
    stages = z.stages[0]
    vm, dma = pltpu.VMEM, pltpu.SemaphoreType.DMA
    s = dict(
        tok=vm((R, D), BF16),
        cot=vm((R, D), BF16),
        wqkv=vm((D, 3 * D), BF16),
        wout=vm((D, D), BF16),
        wup=vm((D, FF), BF16),
        wdown=vm((FF, D), BF16),
        ada1=vm((32, 2 * D), F32),
        ada2=vm((32, 2 * D), F32),
        c=vm((16, 2 * D), F32),
        pick=vm((R, PS), BF16),
        place=vm((PS, R), BF16),
        out_t=vm((PT, D), BF16),
        out_c=vm((PT, D), BF16),
        in_t=vm((PS, D), BF16),
        in_c=vm((PS, D), BF16),
        home_y=vm((PS, D), BF16),
        home_g=vm((PS, D), BF16),
        more_out=vm((4, z.P, 1, D + 128), F32),
        more_in=vm((4, z.P, 1, D + 128), F32),
        x=vm((R, D), F32),
        plain1=vm((R, D), F32),
        inv1=vm((R, 128), F32),
        plain2=vm((R, D), F32),
        inv2=vm((R, 128), F32),
        resid=vm((R, D), F32),
        gresid=vm((R, D), F32),
        tmp=vm((R, D), F32),
        ups=vm((2, R, D), BF16),
        normed=vm((3, R, D), BF16),
        normed_p=vm((R, D), BF16),
        qkv=vm((3, R, 3 * D), BF16),
        cols=vm((3, nb, R), F32),
        colq=vm((R, nb), F32),
        cq=vm((R, 3 * R), F32),
        ck=vm((3, R, R), F32),
        s=vm((R, 3 * R), F32),
        s2=vm((R, 3 * R), F32),
        w=vm((H, R, 3 * R), BF16),
        low=vm((R, 3 * R), BF16),
        low2=vm((R, 3 * R), BF16),
        o=vm((2, R, D), BF16),
        wide_o=vm((R, D), F32),
        u=vm((R, D), F32),
        ga=vm((R, D), F32),
        a=vm((R, FF), BF16),
        a_p=vm((R, FF // 2), BF16),
        gu=vm((R, FF), BF16),
        gu_p=vm((R, FF // 2), BF16),
        normed2=vm((2, R, D), BF16),
        gr=vm((R, D), BF16),
        gr_p=vm((R, D // 2), BF16),
        go=vm((3, R, D), BF16),
        stat=vm((R, 128), F32),
        stats=vm((3, 2 * H, R), F32),
        gqkv=vm((R, 3 * D), BF16),
        gqkv_p=vm((R, 3 * D // 2), BF16),
        acc=vm((STREAMS,) + BLOCK, BF16),
        **{f"rcv{k}": vm((STREAMS, (1 << len(b)) - 1, n, BLOCK[1]), BF16) for k, (b, _, n) in enumerate(stages)},
        gcs=vm((z.bits + 2, 8, D), F32),
        gcr=vm((z.bits + 1, 8, D), F32),
        load_sem=dma((8,)),
        row_ss=dma((4,)),
        row_rs=dma((4,)),
        own_sem=dma((4,)),
        more_ss=dma((4,)),
        more_rs=dma((4,)),
        more_own=dma((4,)),
        side_ss=dma((4, 2)),
        side_rs=dma((4, 2)),
        piece_rs=dma((2, PIECES)),
        pair_ss=dma((8,)),
        pair_rs=dma((8,)),
        sum_ss=dma((1,)),
        late_ss=dma((STREAMS, len(stages))),
        rs_rs=dma((STREAMS, len(stages))),
        ag_rs=dma((STREAMS, len(stages))),
        core_ss=dma((1,)),
        core_rs=dma((1,)),
        gc_ss=dma((1,)),
        gc_rs=dma((z.bits + 1,)),
    )
    return s


def marker():
    def phase(name):
        del name

    return phase


def layer(z, names, *refs):
    n = types.SimpleNamespace(**dict(zip(names, refs, strict=True)))
    Pn, R, D, FF, T, PT, PS = z.P, z.R, z.D, z.FF, z.T, z.PT, z.PT + z.P
    me = lax.axis_index("patch")
    rp = lax.axis_index("rep")
    mate = 1 - rp
    nxt = lax.rem(me + 1, Pn)
    prv = lax.rem(me + Pn - 1, Pn)
    started = []
    phase = marker()

    def tiles(total, fn, init=0, size=TILE, together=1):
        def some(i, carry):
            for j in range(together):
                carry = fn(pl.ds(pl.multiple_of((i * together + j) * size, size), size), carry)
            return carry

        return lax.fori_loop(0, total // (size * together), some, init)

    def load(i, src, dst):
        copy = pltpu.make_async_copy(src, dst, n.load_sem.at[i])
        copy.start()
        return copy

    phase("entry")
    get_tok = load(0, n.tokens, n.tok)
    get_cot = load(1, n.cotangent, n.cot)
    get_ada1 = load(2, n.ada_attn, n.ada1)
    get_ada2 = load(3, n.ada_mlp, n.ada2)
    get_wqkv = load(4, n.w_qkv, n.wqkv)
    get_wdown = load(5, n.w_down, n.wdown)
    get_wout = load(6, n.w_out, n.wout)
    get_wup = load(7, n.w_up, n.wup)

    barrier = pltpu.get_barrier_semaphore()

    def greet(i, carry):
        pl.semaphore_signal(barrier, inc=1, device_id=(lax.rem(me + i, Pn), rp), device_id_type=MESH)
        return carry

    lax.fori_loop(1, Pn, greet, 0)
    pl.semaphore_signal(barrier, inc=1, device_id=(me, mate), device_id_type=MESH)

    def remote(src, dst, ss, rs, to, keep=False):
        copy = pltpu.make_async_remote_copy(
            src_ref=src, dst_ref=dst, send_sem=ss, recv_sem=rs, device_id=to, device_id_type=MESH
        )
        copy.start()
        if keep:
            started.append(copy)
        return copy

    def send_rows(i, src, dst, odd=None):
        def one(j, carry):
            to = me ^ (Pn - j if odd is None else Pn + odd - 2 * j)
            pltpu.make_async_remote_copy(
                src_ref=src.at[pl.ds(pl.multiple_of(to * T, 16), T)],
                dst_ref=dst.at[pl.ds(pl.multiple_of(me * T, 16), T)],
                send_sem=n.row_ss.at[i],
                recv_sem=n.row_rs.at[i],
                device_id=(to, rp),
                device_id_type=MESH,
            ).start()
            pltpu.make_async_remote_copy(
                src_ref=n.more_out.at[i, to],
                dst_ref=n.more_in.at[i, me],
                send_sem=n.more_ss.at[i],
                recv_sem=n.more_rs.at[i],
                device_id=(to, rp),
                device_id_type=MESH,
            ).start()
            return carry

        lax.fori_loop(1, Pn if odd is None else Pn // 2 + odd, one, 0)
        if odd == 0:
            return
        mine = pl.ds(pl.multiple_of(me * T, 16), T)
        pltpu.make_async_copy(src.at[mine], dst.at[mine], n.own_sem.at[i]).start()
        pltpu.make_async_copy(n.more_out.at[i, me], n.more_in.at[i, me], n.more_own.at[i]).start()

    def waits_for(ref, sem):
        pltpu.make_async_copy(ref, ref, sem).wait()

    def rows_in(i, dst):
        waits_for(n.more_in.at[i, pl.ds(0, Pn - 1)], n.more_rs.at[i])
        waits_for(n.more_in.at[i, 0], n.more_own.at[i])
        waits_for(dst.at[pl.ds(0, PT - T)], n.row_rs.at[i])
        waits_for(dst.at[pl.ds(0, T)], n.own_sem.at[i])
        dst[PT:PS] = n.more_in[i, :, 0, :D].astype(BF16)

    def rows_gone(i, src):
        waits_for(src.at[pl.ds(0, PT - T)], n.row_ss.at[i])
        waits_for(n.more_out.at[i, pl.ds(0, Pn - 1)], n.more_ss.at[i])

    def set_rows(i, hot_rows, values, out):
        total = mm(hot_rows, values)
        out[...] = total[:PT].astype(BF16)
        n.more_out[i, :, 0, :D] = total[PT:]

    even = lax.rem(me, 2) == 0
    near = me ^ 1
    near_slot = jnp.where(even, 2, 0)
    far_slot = 2 - near_slot
    onward = lax.rem(jnp.where(even, me + 2, me + Pn - 2), Pn)

    def to_sides(i, ref):
        return (
            remote(ref.at[1], ref.at[0], n.side_ss.at[i, 0], n.side_rs.at[i, 0], (nxt, rp), True),
            remote(ref.at[1], ref.at[2], n.side_ss.at[i, 1], n.side_rs.at[i, 1], (prv, rp), True),
        )

    def to_near(i, ref, c):
        size = R // PIECES
        return remote(
            ref.at[1, pl.ds(c * size, size)],
            ref.at[far_slot, pl.ds(c * size, size)],
            n.side_ss.at[i, 0],
            n.piece_rs.at[i - 1, c],
            (near, rp),
        )

    def hand_on(i, ref, copies):
        size = R // PIECES
        for copy in copies:
            c = len(handed[i])
            copy.wait_recv()
            handed[i].append(
                remote(
                    ref.at[near_slot, pl.ds(c * size, size)],
                    ref.at[far_slot, pl.ds(c * size, size)],
                    n.side_ss.at[i, 1],
                    n.side_rs.at[i, 1],
                    (onward, rp),
                )
            )

    handed = {1: [], 2: []}

    def far_in(i, ref):
        waits_for(ref.at[far_slot], n.side_rs.at[i, 1])

    def to_mate(i, src, dst):
        return remote(src, dst, n.pair_ss.at[i], n.pair_rs.at[i], (me, mate), True)

    n.cols[1] = lists_of(z, n.neighbours[...], me)
    dest = n.dest[...].astype(F32)
    mine_hot = iota((Pn, R), 0) == dest
    before = hot(iota((R, R), 0) < iota((R, R), 1)).astype(BF16)
    earlier = mm(hot(mine_hot).astype(BF16), before)
    rank = jnp.sum(jnp.where(mine_hot, earlier, 0.0), axis=0, keepdims=True)
    code = jnp.where(rank < T, dest * T + rank, PT + dest)
    pick = hot(code == iota((PS, R), 0))
    pick_low = pick.astype(BF16)
    get_tok.wait()
    set_rows(0, pick_low, n.tok[...], n.out_t)
    n.more_out[0, :, 0, D:] = jnp.broadcast_to(jnp.sum(hot(mine_hot), axis=1, keepdims=True), (Pn, 128))
    phase("barrier")
    pl.semaphore_wait(barrier, Pn)
    phase("send tokens")
    side_lists = to_sides(0, n.cols)
    send_rows(0, n.out_t, n.in_t)
    get_cot.wait()
    set_rows(1, pick_low, n.cot[...], n.out_c)
    n.pick[...] = pick.T.astype(BF16)

    phase("counts")
    get_ada1.wait()
    get_ada2.wait()
    cond = jnp.broadcast_to(n.cond[...], (8, n.cond.shape[1]))
    n.c[0:8] = jnp.dot(cond, n.ada1[...], precision=lax.Precision.HIGHEST, preferred_element_type=F32)
    n.c[8:16] = jnp.dot(cond, n.ada2[...], precision=lax.Precision.HIGHEST, preferred_element_type=F32)
    n.colq[...] = n.cols[1].T
    lists = n.cols.shape[1]

    def count_q(t, carry):
        ids = iota((TILE, 3 * R), 1)
        col = n.colq[t, :]
        total = jnp.zeros((TILE, 3 * R), F32)
        for j in range(lists):
            total = total + hot(col[:, j : j + 1] == ids)
        n.cq[t, :] = jnp.where(total > 0.0, jnp.log2(total), NEVER)
        return carry

    tiles(R, count_q)

    def count_k(side, base):
        def one(t, carry):
            ids = iota((TILE, R), 0) + (t.start + base).astype(F32)
            total = jnp.zeros((TILE, R), F32)
            for j in range(lists):
                total = total + hot(n.cols[side, j : j + 1, :] == ids)
            n.ck[side, t, :] = jnp.where(total > 0.0, jnp.log2(total), NEVER)
            return carry

        tiles(R, one)

    count_k(1, R)
    phase("side counts")
    for lists_copy in side_lists:
        lists_copy.wait_recv()
    count_k(0, 2 * R)
    count_k(2, 0)

    phase("places")
    row = iota((PS, 1), 0)
    source = jnp.where(row < PT, jnp.floor((row + 0.5) * (1.0 / T)), row - PT)
    step = jnp.where(row < PT, row - source * T, T * 1.0)
    spread = hot(source == iota((PS, Pn), 1)).astype(BF16)
    earlier_sources = hot(iota((Pn, Pn), 0) > iota((Pn, Pn), 1)).astype(BF16)
    phase("wait tokens")
    rows_in(0, n.in_t)
    phase("place rows")
    count = n.more_in[0, :, 0, D:].astype(BF16)
    offset = mm(earlier_sources, count).astype(BF16)
    position = jnp.where(step < mm(spread, count)[:, 0:1], mm(spread, offset)[:, 0:1] + step, -1.0)
    place = hot(position == iota((PS, R), 1))
    n.place[...] = place.astype(BF16)
    place_t = place.T.astype(BF16)
    n.x[...] = mm(place_t, n.in_t[...])

    def norm(src, coeffs, plain_ref, inv_ref, out, after=None):
        def one(t, carry):
            v = src[t, :]
            centred = v - jnp.sum(v, axis=-1, keepdims=True) * (1.0 / D)
            inverse = lax.rsqrt(jnp.sum(centred * centred, axis=-1, keepdims=True) * (1.0 / D) + EPS)
            plain = centred * inverse
            plain_ref[t, :] = plain
            inv_ref[t, :] = jnp.broadcast_to(inverse, (TILE, 128))
            out[t, :] = (plain * (1.0 + n.c[coeffs : coeffs + 1, :D]) + n.c[coeffs : coeffs + 1, D:]).astype(BF16)
            return carry

        for c in range(PIECES):
            size = R // PIECES
            for j in range(size // TILE):
                one(pl.ds(c * size + j * TILE, TILE), 0)
            if after:
                after(c)

    def norm_back(grad, coeffs, plain_ref, inv_ref, finish):
        def one(t, carry):
            g = grad[t, :]
            plain = plain_ref[t, :]
            scaled = g * (1.0 + n.c[coeffs : coeffs + 1, :D])
            mean = jnp.sum(scaled, axis=-1, keepdims=True) * (1.0 / D)
            along = jnp.sum(scaled * plain, axis=-1, keepdims=True) * (1.0 / D)
            finish(t, inv_ref[t, 0:1] * (scaled - mean - plain * along))
            return (
                carry[0] + jnp.sum(g * plain, axis=0, keepdims=True),
                carry[1] + jnp.sum(g, axis=0, keepdims=True),
            )

        zero = jnp.zeros((1, D), F32)
        return tiles(R, one, (zero, zero), together=4)

    phase("norm")
    side_normed = []
    norm(n.x, 0, n.plain1, n.inv1, n.normed.at[1], lambda c: side_normed.append(to_near(1, n.normed, c)))
    mate_normed = to_mate(0, n.normed.at[1], n.normed_p)
    send_rows(1, n.out_c, n.in_c, 0)
    phase("project")
    get_wqkv.wait()

    def project(side):
        for j in range(3):
            c = slice(j * D, (j + 1) * D)
            n.qkv[side, :, c] = mm(n.normed[side], n.wqkv[:, c]).astype(BF16)

    project(1)
    phase("wait halo")
    hand_on(1, n.normed, side_normed)
    send_rows(1, n.out_c, n.in_c, 1)
    project(near_slot)
    phase("wait far")
    far_in(1, n.normed)
    project(far_slot)

    phase("attention")
    scale = 1.0 / HD**0.5

    def part(which, h):
        return slice(which * D + h * HD, which * D + (h + 1) * HD)

    for h in range(H):
        for side in range(3):
            n.s[:, side * R : (side + 1) * R] = mm(n.qkv[1, :, part(0, h)], n.qkv[side, :, part(1, h)], NT)

        def soft(t, carry, h=h):
            s = n.s[t, :] * (scale * LOG2E) + n.cq[t, :]
            top = jnp.max(s, axis=-1, keepdims=True)
            e = jnp.exp2(s - top)
            total = jnp.sum(e, axis=-1, keepdims=True)
            w = e * (1.0 / total)
            n.w[h, t, :] = w.astype(BF16)
            n.stat[t, h : h + 1] = top + jnp.log2(total)
            return carry

        tiles(R, soft, together=8)
        mixed = jnp.zeros((R, HD), F32)
        for side in range(3):
            mixed = mixed + mm(n.w[h, :, side * R : (side + 1) * R], n.qkv[side, :, part(2, h)])
        n.wide_o[:, h * HD : (h + 1) * HD] = mixed
        n.o[0, :, h * HD : (h + 1) * HD] = mixed.astype(BF16)
    mate_o = to_mate(2, n.o.at[0], n.o.at[1])

    phase("wait upstream")
    rows_in(1, n.in_c)
    n.ups[0] = mm(place_t, n.in_c[...]).astype(BF16)
    mate_ups = to_mate(1, n.ups.at[0], n.ups.at[1])
    phase("resid")
    get_wout.wait()
    n.resid[...] = n.x[...] + mm(n.o[0], n.wout[...])
    norm(n.resid, 8, n.plain2, n.inv2, n.normed2.at[0])
    mate_normed2 = to_mate(3, n.normed2.at[0], n.normed2.at[1])
    get_wup.wait()
    get_wdown.wait()
    phase("mlp")
    half = FF // 2
    for j in range(FF // D):
        c = slice(j * D, (j + 1) * D)
        n.u[...] = mm(n.normed2[0], n.wup[:, c])
        n.ga[...] = mm(n.ups[0], n.wdown[c, :], NT)

        def gate(t, carry, c=c):
            u = n.u[t, :]
            sig = 1.0 / (1.0 + jnp.exp(-u))
            n.a[t, c] = (u * sig).astype(BF16)
            n.gu[t, c] = (n.ga[t, :] * sig * (1.0 + u * (1.0 - sig))).astype(BF16)
            return carry

        tiles(R, gate, together=8)
    theirs = pl.ds(pl.multiple_of(mate * half, 128), half)
    ours = pl.ds(pl.multiple_of(rp * half, 128), half)
    mate_a = to_mate(4, n.a.at[:, theirs], n.a_p)
    mate_gu = to_mate(5, n.gu.at[:, theirs], n.gu_p)
    phase("mlp back")
    n.tmp[...] = mm(n.gu[...], n.wup[...], NT)

    def keep2(t, gw):
        total = n.ups[0, t, :].astype(F32) + gw
        n.gresid[t, :] = total
        n.gr[t, :] = total.astype(BF16)

    gc2 = norm_back(n.tmp, 8, n.plain2, n.inv2, keep2)
    phase("go")
    n.go[1] = mm(n.gr[...], n.wout[...], NT).astype(BF16)
    side_go = [to_near(2, n.go, c) for c in range(PIECES)]

    def against(t, carry):
        product = n.go[1, t, :].astype(F32) * n.wide_o[t, :]
        for h in range(H):
            n.stat[t, H + h : H + h + 1] = jnp.sum(product[:, h * HD : (h + 1) * HD], axis=-1, keepdims=True)
        return carry

    tiles(R, against, together=8)
    n.stats[1] = n.stat[...].T[0 : 2 * H]
    side_stats = to_sides(3, n.stats)
    quarter = D // 2
    mate_gr = to_mate(6, n.gr.at[:, pl.ds(pl.multiple_of(mate * quarter, 128), quarter)], n.gr_p)
    live = {}

    def place_in(p, k):
        return sum(((me >> b) & 1) << i for i, b in enumerate(z.stages[p][k][0]))

    def start_of(p, k):
        return sum(place_in(p, i) * z.stages[p][i][2] for i in range(k) if z.stages[p][i][1] > z.stages[p][i][2])

    def span(p, k):
        rows = z.stages[p][k - 1][2] if k else BLOCK[0]
        return pl.ds(pl.multiple_of(start_of(p, k), rows) if k else 0, rows)

    def partners(p, k):
        over = z.stages[p][k][0]
        for j in range(1, 1 << len(over)):
            yield j, (me ^ sum(1 << b for i, b in enumerate(over) if j >> i & 1), rp)

    def reduce_start(p, k):
        _, rows, after = z.stages[p][k]
        for j, to in partners(p, k):
            if after < rows:
                at = start_of(p, k) + (place_in(p, k) ^ j) * after
                src, ss = n.acc.at[p, pl.ds(pl.multiple_of(at, after), after)], n.sum_ss.at[0]
            else:
                src, ss = n.acc.at[p, span(p, k)], n.late_ss.at[p, k]
            live[p] = remote(src, getattr(n, f"rcv{k}").at[p, j - 1], ss, n.rs_rs.at[p, k], to)

    def reduce_end(p, k):
        _, rows, after = z.stages[p][k]
        got = getattr(n, f"rcv{k}")
        waits_for(got.at[p], n.rs_rs.at[p, k])
        if after == rows:
            live[p].wait_send()
        kept = span(p, k + 1)
        total = n.acc[p, kept].astype(F32)
        for j in range(got.shape[1]):
            total = total + got[p, j].astype(F32)
        into = n.grads_out.at[rp, p, kept] if k + 1 == len(z.stages[p]) else n.acc.at[p, kept]
        into[...] = total.astype(BF16)

    def gather_start(p, k):
        ref = n.grads_out.at[rp, p, span(p, k + 1)]
        for _, to in partners(p, k):
            remote(ref, ref, n.sum_ss.at[0], n.ag_rs.at[p, k], to)

    def gather_end(p, k):
        _, rows, after = z.stages[p][k]
        waits_for(n.grads_out.at[rp, p, pl.ds(0, rows - after)], n.ag_rs.at[p, k])

    def core_start(p):
        ref = n.grads_out.at[rp, p]
        remote(ref, ref, n.core_ss.at[0], n.core_rs.at[0], (me, mate))

    steps_left = {}
    for p in range(STREAMS):
        steps = []
        kept = [k for k, stage in enumerate(z.stages[p]) if stage[1] > stage[2]]
        for k in range(len(z.stages[p])):
            steps += [functools.partial(reduce_start, p, k), functools.partial(reduce_end, p, k)]
        for k in reversed(kept):
            steps += [functools.partial(gather_start, p, k), functools.partial(gather_end, p, k)]
        steps += [functools.partial(core_start, p), lambda: None]
        steps_left[p] = steps

    def small_start(k):
        to = (me, mate) if k == 0 else (me ^ (1 << (k - 1)), rp)
        live["gc"] = remote(n.gcs.at[k], n.gcr.at[k], n.gc_ss.at[0], n.gc_rs.at[k], to)

    def small_end(k):
        live["gc"].wait_recv()
        n.gcs[k + 1] = n.gcs[k] + n.gcr[k]

    steps = []
    for k in range(z.bits + 1):
        steps += [functools.partial(small_start, k), functools.partial(small_end, k)]
    steps_left[STREAMS] = steps
    actions = sum_plan(z.bits)

    def service(until=None):
        while actions and (until is None or actions[0][0] <= until):
            phase(f"sums {2 * int(actions[0][0] / 2)}")
            steps_left[actions.pop(0)[1]].pop(0)()

    phase("y")
    y = (n.resid[...] + mm(n.a[...], n.wdown[...])).astype(BF16)
    rows_gone(0, n.out_t)
    set_rows(2, n.place[...], y, n.out_t)
    send_rows(2, n.out_t, n.home_y, 0)
    phase("grad down")
    mate_ups.wait_recv()
    mate_a.wait_recv()
    for j in range(2):
        r = pl.ds(pl.multiple_of(rp * half + j * BLOCK[0], 128), BLOCK[0])
        for i in range(2):
            c = slice(i * BLOCK[1], (i + 1) * BLOCK[1])
            total = mm(n.a[:, r], n.ups[0, :, c], TN) + mm(n.a_p[:, j * BLOCK[0] : (j + 1) * BLOCK[0]], n.ups[1, :, c], TN)
            n.acc[2 * j + i] = total.astype(BF16)
    phase("grad up")
    mate_normed2.wait_recv()
    mate_gu.wait_recv()
    for p in range(len(UP)):
        c = pl.ds(pl.multiple_of(rp * half + p * BLOCK[1], 128), BLOCK[1])
        d = slice(p * BLOCK[1], (p + 1) * BLOCK[1])
        n.acc[UP[p]] = (mm(n.normed2[0], n.gu[:, c], TN) + mm(n.normed2[1], n.gu_p[:, d], TN)).astype(BF16)
    mate_o.wait_recv()
    mate_gr.wait_recv()
    c = pl.ds(pl.multiple_of(rp * quarter, 128), quarter)
    n.acc[OUT[0]] = (mm(n.o[0], n.gr[:, c], TN) + mm(n.o[1], n.gr_p[...], TN)).astype(BF16)

    phase("query back")
    service(2.25)
    for h in range(H):
        head = slice(h * HD, (h + 1) * HD)
        for side in range(3):
            n.s[:, side * R : (side + 1) * R] = mm(n.go[1, :, head], n.qkv[side, :, part(2, h)], NT)

        def soft_back(t, carry, h=h):
            w = n.w[h, t, :].astype(F32)
            gp = n.s[t, :]
            n.low[t, :] = (w * (gp - n.stat[t, H + h : H + h + 1])).astype(BF16)
            return carry

        tiles(R, soft_back, together=8)
        total = jnp.zeros((R, HD), F32)
        for side in range(3):
            total = total + mm(n.low[:, side * R : (side + 1) * R], n.qkv[side, :, part(1, h)])
        n.gqkv[:, part(0, h)] = (total * scale).astype(BF16)
        if h < PIECES:
            hand_on(2, n.go, side_go[h : h + 1])
        service((3.05, 3.65, 5.15, 6.45)[h])
    service(10.3)

    phase("sums step")
    for copy in side_stats:
        copy.wait_recv()
    phase("far go")
    far_in(2, n.go)
    phase("send y")
    send_rows(2, n.out_t, n.home_y, 1)
    phase("key back")
    for h in range(H):
        head = slice(h * HD, (h + 1) * HD)
        for side in range(3):
            span_q = slice(side * R, (side + 1) * R)
            n.s[:, span_q] = mm(n.qkv[1, :, part(1, h)], n.qkv[side, :, part(0, h)], NT)
            n.s2[:, span_q] = mm(n.qkv[1, :, part(2, h)], n.go[side, :, head], NT)

        def key_back(t, carry, h=h):
            for side in range(3):
                span_q = slice(side * R, (side + 1) * R)
                s = n.s[t, span_q] * (scale * LOG2E) + n.ck[side, t, :]
                w = jnp.exp2(s - n.stats[side, h : h + 1, :])
                n.low[t, span_q] = w.astype(BF16)
                n.low2[t, span_q] = (w * (n.s2[t, span_q] - n.stats[side, H + h : H + h + 1, :])).astype(BF16)
            return carry

        tiles(R, key_back, together=4)
        total_k = jnp.zeros((R, HD), F32)
        total_v = jnp.zeros((R, HD), F32)
        for side in range(3):
            span_q = slice(side * R, (side + 1) * R)
            total_k = total_k + mm(n.low2[:, span_q], n.qkv[side, :, part(0, h)])
            total_v = total_v + mm(n.low[:, span_q], n.go[side, :, head])
        n.gqkv[:, part(1, h)] = (total_k * scale).astype(BF16)
        n.gqkv[:, part(2, h)] = total_v.astype(BF16)
        service(11.45 + h)
    phase("send gqkv")
    wide = 3 * D // 2
    mate_gqkv = to_mate(7, n.gqkv.at[:, pl.ds(pl.multiple_of(mate * wide, 128), wide)], n.gqkv_p)
    phase("gx")
    n.tmp[...] = mm(n.gqkv[...], n.wqkv[...], NT)
    gx_ref = n.tok

    def keep1(t, gw):
        gx_ref[t, :] = (n.gresid[t, :] + gw).astype(BF16)

    gc1 = norm_back(n.tmp, 0, n.plain1, n.inv1, keep1)
    row = lax.broadcasted_iota(I32, (8, D), 0)
    sums = jnp.zeros((8, D), F32)
    for i, value in enumerate((*gc1, *gc2)):
        sums = jnp.where(row == i, value, sums)
    n.gcs[0] = sums

    service(15.6)
    mate_gqkv.wait_recv()
    mate_normed.wait_recv()
    phase("grad qkv")
    for p in range(3):
        c = pl.ds(pl.multiple_of(rp * wide + p * BLOCK[1], 128), BLOCK[1])
        d = slice(p * BLOCK[1], (p + 1) * BLOCK[1])
        n.acc[QKV[p]] = (mm(n.normed[1], n.gqkv[:, c], TN) + mm(n.normed_p[...], n.gqkv_p[:, d], TN)).astype(BF16)
    phase("leave gx")
    service(16.5)
    rows_gone(1, n.out_c)
    set_rows(3, n.place[...], gx_ref[...], n.out_c)
    send_rows(3, n.out_c, n.home_g)
    phase("sums")
    service()
    waits_for(n.grads_out.at[mate], n.core_rs.at[0])
    n.sums_out[...] = n.gcs[z.bits + 1]
    phase("home")
    rows_in(2, n.home_y)
    n.y_out[...] = mm(n.pick[...], n.home_y[...]).astype(BF16)
    rows_in(3, n.home_g)
    n.g_out[...] = mm(n.pick[...], n.home_g[...]).astype(BF16)

    phase("end")
    rows_gone(2, n.out_t)
    rows_gone(3, n.out_c)
    for copy in started:
        copy.wait_send()
    for i, ref in ((1, n.normed), (2, n.go)):
        for leg in range(2):
            waits_for(ref.at[1], n.side_ss.at[i, leg])
    waits_for(n.grads_out.at[:, :, pl.ds(0, BLOCK[0] - z.stages[0][-1][2])], n.sum_ss.at[0])
    waits_for(n.grads_out.at[rp], n.core_ss.at[0])
    waits_for(n.gcr, n.gc_ss.at[0])


def lists_of(z, neighbours, me):
    within = neighbours & (z.R - 1)
    shift = (2 * z.R).bit_length() - 1
    away = (neighbours >> shift) - me
    after = (away == 1) | (away == 1 - z.P)
    base = jnp.where(away == 0, z.R, jnp.where(after, 2 * z.R, 0))
    return (base + within).astype(F32)


def finish(z, g_ref, sums_ref, y_ref, gx_ref, ada1_ref, ada2_ref, cond_ref, *rest):
    y_out, gx_out, qkv_out, out_out, up_out, down_out, ga1_out, ga2_out, gcond_out, wide, wide_sem, row_sem = rest
    rows = [pltpu.make_async_copy(a, b, row_sem.at[i]) for i, (a, b) in enumerate(((y_ref, y_out), (gx_ref, gx_out)))]
    for copy in rows:
        copy.start()
    high, across = BLOCK
    copies = []
    for i in range(2):
        for p in range(STREAMS):
            if p in DOWN:
                r, c, out = 2 * i + p // 2, p % 2, down_out
            elif p in UP:
                r, c, out = 0, len(UP) * i + p - UP[0], up_out
            elif p in OUT:
                r, c, out = 0, i, out_out
            else:
                r, c, out = 0, len(QKV) * i + p - QKV[0], qkv_out
            wide[i, p] = g_ref[i, p].astype(F32)
            to = out.at[r * high : (r + 1) * high, c * across : (c + 1) * across]
            copies.append(pltpu.make_async_copy(wide.at[i, p], to, wide_sem.at[i, p]))
            copies[-1].start()
    count = cond_ref.shape[1]
    eye = lax.broadcasted_iota(I32, (count, count), 0) == lax.broadcasted_iota(I32, (count, count), 1)
    cond = jnp.sum(jnp.where(eye, cond_ref[...], 0.0), axis=1, keepdims=True)
    d = z.D
    total = jnp.zeros((count, 1), F32)
    for row, ada, out in ((0, ada1_ref, ga1_out), (2, ada2_ref, ga2_out)):
        for j in range(2):
            c = slice(j * d, (j + 1) * d)
            sums = sums_ref[row + j : row + j + 1, :]
            out[:, c] = cond * sums
            total = total + jnp.sum(ada[:, c] * sums, axis=1, keepdims=True)
    gcond_out[...] = jnp.sum(jnp.where(eye, total, 0.0), axis=0, keepdims=True)
    for copy in (*copies, *rows):
        copy.wait()


def local(tokens, cotangent, dest, neighbours, w_qkv, w_out, w_up, w_down, ada_attn, ada_mlp, cond):
    rows, width = tokens.shape
    z = sizes(lax.axis_size("patch"), rows, width, w_up.shape[1])
    dest = dest.reshape(1, rows)
    neighbours = neighbours.T
    cond = cond.reshape(1, cond.shape[0])
    inputs = dict(
        tokens=tokens,
        cotangent=cotangent,
        dest=dest,
        neighbours=neighbours,
        w_qkv=w_qkv,
        w_out=w_out,
        w_up=w_up,
        w_down=w_down,
        ada_attn=ada_attn,
        ada_mlp=ada_mlp,
        cond=cond,
    )
    small = ("dest", "neighbours", "cond")
    any_space = pl.BlockSpec(memory_space=pl.ANY)
    vmem = pl.BlockSpec(memory_space=pltpu.VMEM)
    shape = jax.ShapeDtypeStruct
    outs = dict(
        grads_out=pltpu.VMEM((2, STREAMS) + BLOCK, BF16),
        sums_out=pltpu.VMEM((8, width), F32),
        y_out=pltpu.VMEM((rows, width), BF16),
        g_out=pltpu.VMEM((rows, width), BF16),
    )
    held = scratch(z, neighbours.shape[0])
    held_out = pl.pallas_call(
        functools.partial(layer, z, [*inputs, *outs, *held]),
        out_shape=list(outs.values()),
        in_specs=[vmem if k in small else any_space for k in inputs],
        out_specs=[vmem, vmem, vmem, vmem],
        scratch_shapes=list(held.values()),
        compiler_params=pltpu.CompilerParams(collective_id=0, has_side_effects=True, vmem_limit_bytes=56 << 20),
        name="layer",
    )(*inputs.values())

    held_out = [pltpu.with_memory_space_constraint(v, pltpu.VMEM) for v in held_out]
    y, gx, g_qkv, g_out, g_up, g_down, g_ada1, g_ada2, g_cond = pl.pallas_call(
        functools.partial(finish, z),
        in_specs=[vmem] * 7,
        out_specs=[any_space] * 6 + [vmem] * 3,
        scratch_shapes=[
            pltpu.VMEM((2, STREAMS) + BLOCK, F32),
            pltpu.SemaphoreType.DMA((2, STREAMS)),
            pltpu.SemaphoreType.DMA((2,)),
        ],
        out_shape=[
            shape((rows, width), BF16),
            shape((rows, width), BF16),
            shape(w_qkv.shape, F32),
            shape(w_out.shape, F32),
            shape(w_up.shape, F32),
            shape(w_down.shape, F32),
            shape(ada_attn.shape, F32),
            shape(ada_mlp.shape, F32),
            shape(cond.shape, F32),
        ],
        compiler_params=pltpu.CompilerParams(vmem_limit_bytes=32 << 20),
        name="finish",
    )(*held_out, ada_attn, ada_mlp, cond)
    return y, gx, g_qkv, g_out, g_up, g_down, g_ada1, g_ada2, g_cond.reshape(cond.shape[1])


def solution(mesh):
    row = P(("patch", "rep"), None)
    return jax.shard_map(
        local,
        mesh=mesh,
        in_specs=(row, row, P(("patch", "rep")), row) + (P(),) * 7,
        out_specs=(row, row) + (P(),) * 7,
        check_vma=False,
    )
```

```python
import functools
import heapq
import itertools
import types

import jax
import jax.numpy as jnp
from jax import lax
from jax.experimental import pallas as pl
from jax.experimental.pallas import tpu as pltpu
from jax.sharding import PartitionSpec as P

H = 4
HD = 128
EPS = 1e-05
F32 = jnp.float32
BF16 = jnp.bfloat16
I32 = jnp.int32
MESH = pl.DeviceIdType.MESH
NN = (((1,), (0,)), ((), ()))
NT = (((1,), (1,)), ((), ()))
TN = (((0,), (0,)), ((), ()))
TILE = 32
NEVER = -1e30
LOG2E = 1.4426950408889634
BLOCK = (512, 256)
MIN_ROWS = 64


def mm(a, b, dims=NN):
    return lax.dot_general(a, b, dims, preferred_element_type=F32)


def iota(shape, axis):
    return lax.broadcasted_iota(I32, shape, axis).astype(F32)


def hot(cond):
    return jnp.where(cond, 1.0, 0.0)


def sizes(patches, rows, width, hidden):
    cap = rows // patches + 1
    block = -(-(cap - 1) // 16) * 16
    bits = patches.bit_length() - 1
    return types.SimpleNamespace(
        P=patches, R=rows, D=width, FF=hidden, T=block, PT=patches * block, bits=bits, stages=stages_of(bits)
    )


XYZ, XZY, YXZ, YZX, ZXY, ZYX = itertools.permutations(range(3))
ORDERS = [XYZ, ZXY, YXZ, XYZ, XYZ, XZY, YXZ, ZYX, ZYX, XZY, YZX, XYZ]
DOWN, UP, OUT, QKV = range(0, 4), range(4, 8), range(8, 9), range(9, 12)
STREAMS = len(ORDERS)
SUMS_AT, FIRST_AT = (6.4, 8.5, 9.5), (6.4, 2.2, 2.2)
QKV_AT, COEFF_AT = 14.8, 13.6
COMPUTES = ((-1.0, 2.2), (2.3, 3.0), (3.0, 3.6), (3.6, 5.1), (5.1, 6.4), (10.4, 11.0), (11.0, 11.6), (11.6, 12.2))
COMPUTES += ((12.2, 12.8), (12.8, 13.6), (13.6, 14.8), (14.9, 15.4))
ROW_LOADS = ((1.2, (0.0, 1.6, 2.4, 3.2)), (3.0, (3.0, 5.7, 2.9)), (10.5, (3.2, 1.6, 2.4, 3.2)), (15.5, (3.2, 3.2, 4.8, 6.4)))
PIECES = 8


def stages_of(bits):
    found = []
    for first in ORDERS:
        order = [(b,) for b in first if b < bits] + [(b,) for b in range(3, bits)]
        rows, stages = BLOCK[0], []
        for over in order:
            after = rows >> len(over)
            if after < MIN_ROWS:
                after = rows
            stages.append((over, rows, after))
            rows = after
        found.append(stages)
    return found


def sum_plan(bits):
    whole, delay, turn, depth = 5.7, 1.8, 0.12, 3
    steps = []
    for stages in stages_of(bits):
        places = stages + [stage for stage in reversed(stages) if stage[1] > stage[2]]
        steps.append([(over[0], whole * after / BLOCK[0]) for over, _, after in places] + [(None, 0.5)])
    steps.append([(None, 0.1)] + [(b, 0.4) for b in range(bits)])
    at = [0] * len(steps)
    free, queued, waiting, plan = {}, {}, [], []
    number = itertools.count()
    events, begun = [], set()
    for p in range(STREAMS):
        first = ORDERS[p][0]
        begin = QKV_AT if p in QKV else SUMS_AT[first] if first in begun else FIRST_AT[first]
        begun.add(first)
        events.append((begin, next(number), "ready", p))
    events.append((COEFF_AT, next(number), "ready", STREAMS))
    events += [(t, next(number), "rows", times) for t, times in ROW_LOADS]
    heapq.heapify(events)
    now = 0.0

    def able(t):
        return next((b for a, b in COMPUTES if a < t < b), t)

    while events:
        t, _, kind, p = heapq.heappop(events)
        if kind == "rows":
            for link, time in enumerate(p):
                free[link] = max(free.get(link, 0.0), t) + time
            continue
        if kind == "free":
            queued[p] -= 1
            kind = "look"
        if able(max(now, t)) > max(now, t):
            heapq.heappush(events, (able(max(now, t)), next(number), kind, p))
            continue
        now = max(now, t)
        if kind == "ready":
            waiting.append(p)
        elif kind == "end":
            now += turn
            plan.append((now, p))
            at[p] += 1
            if at[p] < len(steps[p]):
                waiting.append(p)
        for q in sorted(waiting, key=lambda q: (q < STREAMS, (q - QKV[0]) % STREAMS)):
            link, time = steps[q][at[q]]
            uses = {None: ()}.get(link, ((2, 1), (3, 2)) if bits == 4 and link == 3 else ((link, 1),))
            if any(queued.get(used, 0) >= depth for used, _ in uses):
                continue
            waiting.remove(q)
            now += 0.03
            plan.append((now, q))
            done = now if uses else now + time
            for used, share in uses:
                queued[used] = queued.get(used, 0) + 1
                free[used] = max(free.get(used, 0.0), now) + time * share
                heapq.heappush(events, (free[used], next(number), "free", used))
                done = max(done, free[used])
            heapq.heappush(events, (done + delay, next(number), "end", q))
    return plan


def scratch(z, nb):
    R, D, FF, PT, PS = z.R, z.D, z.FF, z.PT, z.PT + z.P
    stages = z.stages[0]
    halved = sum(before > after for _, before, after in stages)
    vm, dma = pltpu.VMEM, pltpu.SemaphoreType.DMA
    s = dict(
        tok=vm((R, D), BF16),
        cot=vm((R, D), BF16),
        wqkv=vm((D, 3 * D), BF16),
        wout=vm((D, D), BF16),
        wup=vm((D, FF), BF16),
        wdown=vm((FF, D), BF16),
        ada1=vm((32, 2 * D), F32),
        ada2=vm((32, 2 * D), F32),
        c=vm((16, 2 * D), F32),
        pick=vm((R, PS), BF16),
        place=vm((PS, R), BF16),
        out_t=vm((PT, D), BF16),
        out_c=vm((PT, D), BF16),
        in_t=vm((PS, D), BF16),
        in_c=vm((PS, D), BF16),
        home_y=vm((PS, D), BF16),
        home_g=vm((PS, D), BF16),
        more_out=vm((4, z.P, 1, D + 128), F32),
        more_in=vm((4, z.P, 1, D + 128), F32),
        x=vm((R, D), F32),
        plain1=vm((R, D), F32),
        inv1=vm((R, 128), F32),
        plain2=vm((R, D), F32),
        inv2=vm((R, 128), F32),
        resid=vm((R, D), F32),
        gresid=vm((R, D), F32),
        tmp=vm((R, D), F32),
        ups=vm((2, R, D), BF16),
        normed=vm((3, R, D), BF16),
        normed_p=vm((R, D), BF16),
        qkv=vm((3, R, 3 * D), BF16),
        cols=vm((3, nb, R), F32),
        colq=vm((R, nb), F32),
        cq=vm((R, 3 * R), F32),
        ck=vm((3, R, R), F32),
        s=vm((R, 3 * R), F32),
        s2=vm((R, 3 * R), F32),
        w=vm((H, R, 3 * R), BF16),
        low=vm((R, 3 * R), BF16),
        low2=vm((R, 3 * R), BF16),
        o=vm((2, R, D), BF16),
        wide_o=vm((R, D), F32),
        u=vm((R, D), F32),
        ga=vm((R, D), F32),
        a=vm((R, FF), BF16),
        a_p=vm((R, FF // 2), BF16),
        gu=vm((R, FF), BF16),
        gu_p=vm((R, FF // 2), BF16),
        normed2=vm((2, R, D), BF16),
        gr=vm((R, D), BF16),
        gr_p=vm((R, D // 2), BF16),
        go=vm((3, R, D), BF16),
        stat=vm((R, 128), F32),
        stats=vm((3, 2 * H, R), F32),
        gqkv=vm((R, 3 * D), BF16),
        gqkv_p=vm((R, 3 * D // 2), BF16),
        acc=vm((STREAMS,) + BLOCK, BF16),
        **{f"rcv{k}": vm((STREAMS, (1 << len(b)) - 1, n, BLOCK[1]), BF16) for k, (b, _, n) in enumerate(stages)},
        gcs=vm((z.bits + 2, 8, D), F32),
        gcr=vm((z.bits + 1, 8, D), F32),
        load_sem=dma((8,)),
        row_ss=dma((2,)),
        row_rs=dma((4,)),
        own_sem=dma((2,)),
        more_ss=dma((2,)),
        more_rs=dma((4,)),
        more_own=dma((2,)),
        side_ss=dma((4, 2)),
        side_rs=dma((4, 2)),
        piece_rs=dma((2, PIECES)),
        pair_ss=dma((1,)),
        pair_rs=dma((8,)),
        sum_ss=dma((1,)),
        late_ss=dma((STREAMS, len(stages) - halved) if len(stages) > halved + 1 else (1, 1)),
        rs_rs=dma((STREAMS, len(stages))),
        ag_rs=dma((STREAMS,)),
        core_ss=dma((1,)),
        core_rs=dma((1,)),
        gc_ss=dma((1,)),
        gc_rs=dma((z.bits + 1,)),
    )
    return s


def marker():
    def phase(name):
        del name

    return phase


def layer(z, names, *refs):
    n = types.SimpleNamespace(**dict(zip(names, refs, strict=True)))
    Pn, R, D, FF, T, PT, PS = z.P, z.R, z.D, z.FF, z.T, z.PT, z.PT + z.P
    me = lax.axis_index("patch")
    rp = lax.axis_index("rep")
    mate = 1 - rp
    nxt = lax.rem(me + 1, Pn)
    prv = lax.rem(me + Pn - 1, Pn)
    started = []
    phase = marker()

    def tiles(total, fn, init=0, size=TILE, together=1):
        def some(i, carry):
            for j in range(together):
                carry = fn(pl.ds(pl.multiple_of((i * together + j) * size, size), size), carry)
            return carry

        return lax.fori_loop(0, total // (size * together), some, init)

    def load(i, src, dst):
        copy = pltpu.make_async_copy(src, dst, n.load_sem.at[i])
        copy.start()
        return copy

    phase("entry")
    get_tok = load(0, n.tokens, n.tok)
    get_cot = load(1, n.cotangent, n.cot)
    get_ada1 = load(2, n.ada_attn, n.ada1)
    get_ada2 = load(3, n.ada_mlp, n.ada2)
    get_wqkv = load(4, n.w_qkv, n.wqkv)
    get_wdown = load(5, n.w_down, n.wdown)
    get_wout = load(6, n.w_out, n.wout)
    get_wup = load(7, n.w_up, n.wup)

    barrier = pltpu.get_barrier_semaphore()

    def greet(i, carry):
        pl.semaphore_signal(barrier, inc=1, device_id=(lax.rem(me + i, Pn), rp), device_id_type=MESH)
        return carry

    lax.fori_loop(1, Pn, greet, 0)
    pl.semaphore_signal(barrier, inc=1, device_id=(me, mate), device_id_type=MESH)

    def remote(src, dst, ss, rs, to, keep=False):
        copy = pltpu.make_async_remote_copy(
            src_ref=src, dst_ref=dst, send_sem=ss, recv_sem=rs, device_id=to, device_id_type=MESH
        )
        copy.start()
        if keep:
            started.append(copy)
        return copy

    def more(ref, i, at):
        return ref.at[i, at] if i == 0 else ref.at[i, at, :, pl.ds(0, D)]

    def send_rows(i, src, dst, odd=None):
        def one(j, carry):
            to = me ^ (Pn - j if odd is None else Pn + odd - 2 * j)
            pltpu.make_async_remote_copy(
                src_ref=src.at[pl.ds(pl.multiple_of(to * T, 16), T)],
                dst_ref=dst.at[pl.ds(pl.multiple_of(me * T, 16), T)],
                send_sem=n.row_ss.at[i % 2],
                recv_sem=n.row_rs.at[i],
                device_id=(to, rp),
                device_id_type=MESH,
            ).start()
            pltpu.make_async_remote_copy(
                src_ref=more(n.more_out, i, to),
                dst_ref=more(n.more_in, i, me),
                send_sem=n.more_ss.at[i % 2],
                recv_sem=n.more_rs.at[i],
                device_id=(to, rp),
                device_id_type=MESH,
            ).start()
            return carry

        lax.fori_loop(1, Pn if odd is None else Pn // 2 + odd, one, 0)
        if odd == 0:
            return
        mine = pl.ds(pl.multiple_of(me * T, 16), T)
        pltpu.make_async_copy(src.at[mine], dst.at[mine], n.own_sem.at[i // 3]).start()
        pltpu.make_async_copy(more(n.more_out, i, me), more(n.more_in, i, me), n.more_own.at[i // 3]).start()

    def waits_for(ref, sem):
        pltpu.make_async_copy(ref, ref, sem).wait()

    def rows_in(i, dst):
        waits_for(more(n.more_in, i, pl.ds(0, Pn - 1)), n.more_rs.at[i])
        waits_for(more(n.more_in, i, 0), n.more_own.at[i // 3])
        waits_for(dst.at[pl.ds(0, PT - T)], n.row_rs.at[i])
        waits_for(dst.at[pl.ds(0, T)], n.own_sem.at[i // 3])
        dst[PT:PS] = n.more_in[i, :, 0, :D].astype(BF16)

    def rows_gone(i, src):
        waits_for(src.at[pl.ds(0, PT - T)], n.row_ss.at[i % 2])
        waits_for(more(n.more_out, i, pl.ds(0, Pn - 1)), n.more_ss.at[i % 2])

    def set_rows(i, hot_rows, values, out):
        total = mm(hot_rows, values)
        out[...] = total[:PT].astype(BF16)
        n.more_out[i, :, 0, :D] = total[PT:]

    even = lax.rem(me, 2) == 0
    near = me ^ 1
    near_slot = jnp.where(even, 2, 0)
    far_slot = 2 - near_slot
    onward = lax.rem(jnp.where(even, me + 2, me + Pn - 2), Pn)

    def to_sides(i, ref):
        return (
            remote(ref.at[1], ref.at[0], n.side_ss.at[i, 0], n.side_rs.at[i, 0], (nxt, rp), True),
            remote(ref.at[1], ref.at[2], n.side_ss.at[i, 1], n.side_rs.at[i, 1], (prv, rp), True),
        )

    def to_near(i, ref, c):
        size = R // PIECES
        return remote(
            ref.at[1, pl.ds(c * size, size)],
            ref.at[far_slot, pl.ds(c * size, size)],
            n.side_ss.at[i, 0],
            n.piece_rs.at[i - 1, c],
            (near, rp),
        )

    def hand_on(i, ref, copies):
        size = R // PIECES
        for copy in copies:
            c = len(handed[i])
            copy.wait_recv()
            handed[i].append(
                remote(
                    ref.at[near_slot, pl.ds(c * size, size)],
                    ref.at[far_slot, pl.ds(c * size, size)],
                    n.side_ss.at[i, 1],
                    n.side_rs.at[i, 1],
                    (onward, rp),
                )
            )

    handed = {1: [], 2: []}

    def far_in(i, ref):
        waits_for(ref.at[far_slot], n.side_rs.at[i, 1])

    def to_mate(i, src, dst):
        return remote(src, dst, n.pair_ss.at[0], n.pair_rs.at[i], (me, mate))

    n.cols[1] = lists_of(z, n.neighbours[...], me)
    dest = n.dest[...].astype(F32)
    mine_hot = iota((Pn, R), 0) == dest
    before = hot(iota((R, R), 0) < iota((R, R), 1)).astype(BF16)
    earlier = mm(hot(mine_hot).astype(BF16), before)
    rank = jnp.sum(jnp.where(mine_hot, earlier, 0.0), axis=0, keepdims=True)
    code = jnp.where(rank < T, dest * T + rank, PT + dest)
    pick = hot(code == iota((PS, R), 0))
    pick_low = pick.astype(BF16)
    get_tok.wait()
    set_rows(0, pick_low, n.tok[...], n.out_t)
    n.more_out[0, :, 0, D:] = jnp.broadcast_to(jnp.sum(hot(mine_hot), axis=1, keepdims=True), (Pn, 128))
    phase("barrier")
    pl.semaphore_wait(barrier, Pn)
    phase("send tokens")
    side_lists = to_sides(0, n.cols)
    send_rows(0, n.out_t, n.in_t)
    get_cot.wait()
    set_rows(1, pick_low, n.cot[...], n.out_c)
    n.pick[...] = pick.T.astype(BF16)

    phase("counts")
    get_ada1.wait()
    get_ada2.wait()
    cond = jnp.broadcast_to(n.cond[...], (8, n.cond.shape[1]))
    n.c[0:8] = jnp.dot(cond, n.ada1[...], precision=lax.Precision.HIGHEST, preferred_element_type=F32)
    n.c[8:16] = jnp.dot(cond, n.ada2[...], precision=lax.Precision.HIGHEST, preferred_element_type=F32)
    n.colq[...] = n.cols[1].T
    lists = n.cols.shape[1]

    def count_q(t, carry):
        ids = iota((TILE, 3 * R), 1)
        col = n.colq[t, :]
        total = jnp.zeros((TILE, 3 * R), F32)
        for j in range(lists):
            total = total + hot(col[:, j : j + 1] == ids)
        n.cq[t, :] = jnp.where(total > 0.0, jnp.log2(total), NEVER)
        return carry

    tiles(R, count_q)

    def count_k(side, base):
        def one(t, carry):
            ids = iota((TILE, R), 0) + (t.start + base).astype(F32)
            total = jnp.zeros((TILE, R), F32)
            for j in range(lists):
                total = total + hot(n.cols[side, j : j + 1, :] == ids)
            n.ck[side, t, :] = jnp.where(total > 0.0, jnp.log2(total), NEVER)
            return carry

        tiles(R, one)

    count_k(1, R)
    phase("side counts")
    for lists_copy in side_lists:
        lists_copy.wait_recv()
    count_k(0, 2 * R)
    count_k(2, 0)

    phase("places")
    row = iota((PS, 1), 0)
    source = jnp.where(row < PT, jnp.floor((row + 0.5) * (1.0 / T)), row - PT)
    step = jnp.where(row < PT, row - source * T, T * 1.0)
    spread = hot(source == iota((PS, Pn), 1)).astype(BF16)
    earlier_sources = hot(iota((Pn, Pn), 0) > iota((Pn, Pn), 1)).astype(BF16)
    phase("wait tokens")
    rows_in(0, n.in_t)
    send_rows(1, n.out_c, n.in_c, 0)
    phase("place rows")
    count = n.more_in[0, :, 0, D:].astype(BF16)
    offset = mm(earlier_sources, count).astype(BF16)
    position = jnp.where(step < mm(spread, count)[:, 0:1], mm(spread, offset)[:, 0:1] + step, -1.0)
    place = hot(position == iota((PS, R), 1))
    n.place[...] = place.astype(BF16)
    place_t = place.T.astype(BF16)
    n.x[...] = mm(place_t, n.in_t[...])

    def norm(src, coeffs, plain_ref, inv_ref, out, after=None):
        def one(t, carry):
            v = src[t, :]
            centred = v - jnp.sum(v, axis=-1, keepdims=True) * (1.0 / D)
            inverse = lax.rsqrt(jnp.sum(centred * centred, axis=-1, keepdims=True) * (1.0 / D) + EPS)
            plain = centred * inverse
            plain_ref[t, :] = plain
            inv_ref[t, :] = jnp.broadcast_to(inverse, (TILE, 128))
            out[t, :] = (plain * (1.0 + n.c[coeffs : coeffs + 1, :D]) + n.c[coeffs : coeffs + 1, D:]).astype(BF16)
            return carry

        for c in range(PIECES):
            size = R // PIECES
            for j in range(size // TILE):
                one(pl.ds(c * size + j * TILE, TILE), 0)
            if after:
                after(c)

    def norm_back(grad, coeffs, plain_ref, inv_ref, finish):
        def one(t, carry):
            g = grad[t, :]
            plain = plain_ref[t, :]
            scaled = g * (1.0 + n.c[coeffs : coeffs + 1, :D])
            mean = jnp.sum(scaled, axis=-1, keepdims=True) * (1.0 / D)
            along = jnp.sum(scaled * plain, axis=-1, keepdims=True) * (1.0 / D)
            finish(t, inv_ref[t, 0:1] * (scaled - mean - plain * along))
            return (
                carry[0] + jnp.sum(g * plain, axis=0, keepdims=True),
                carry[1] + jnp.sum(g, axis=0, keepdims=True),
            )

        zero = jnp.zeros((1, D), F32)
        return tiles(R, one, (zero, zero), together=8)

    phase("norm")
    side_normed = []
    norm(n.x, 0, n.plain1, n.inv1, n.normed.at[1], lambda c: side_normed.append(to_near(1, n.normed, c)))
    mate_normed = to_mate(0, n.normed.at[1], n.normed_p)
    phase("project")
    get_wqkv.wait()

    def project(side):
        for j in range(3):
            c = slice(j * D, (j + 1) * D)
            n.qkv[side, :, c] = mm(n.normed[side], n.wqkv[:, c]).astype(BF16)

    project(1)
    phase("wait halo")
    hand_on(1, n.normed, side_normed)
    send_rows(1, n.out_c, n.in_c, 1)
    project(near_slot)
    phase("wait far")
    far_in(1, n.normed)
    project(far_slot)

    phase("attention")
    scale = 1.0 / HD**0.5

    def part(which, h):
        return slice(which * D + h * HD, which * D + (h + 1) * HD)

    for h in range(H):
        for side in range(3):
            n.s[:, side * R : (side + 1) * R] = mm(n.qkv[1, :, part(0, h)], n.qkv[side, :, part(1, h)], NT)

        def soft(t, carry, h=h):
            s = n.s[t, :] * (scale * LOG2E) + n.cq[t, :]
            top = jnp.max(s, axis=-1, keepdims=True)
            e = jnp.exp2(s - top)
            total = jnp.sum(e, axis=-1, keepdims=True)
            w = e * (1.0 / total)
            n.w[h, t, :] = w.astype(BF16)
            n.stat[t, h : h + 1] = top + jnp.log2(total)
            return carry

        tiles(R, soft, together=8)
        mixed = jnp.zeros((R, HD), F32)
        for side in range(3):
            mixed = mixed + mm(n.w[h, :, side * R : (side + 1) * R], n.qkv[side, :, part(2, h)])
        n.wide_o[:, h * HD : (h + 1) * HD] = mixed
        n.o[0, :, h * HD : (h + 1) * HD] = mixed.astype(BF16)
    mate_o = to_mate(2, n.o.at[0], n.o.at[1])

    phase("wait upstream")
    rows_in(1, n.in_c)
    n.ups[0] = mm(place_t, n.in_c[...]).astype(BF16)
    mate_ups = to_mate(1, n.ups.at[0], n.ups.at[1])
    phase("resid")
    get_wout.wait()
    n.resid[...] = n.x[...] + mm(n.o[0], n.wout[...])
    norm(n.resid, 8, n.plain2, n.inv2, n.normed2.at[0])
    mate_normed2 = to_mate(3, n.normed2.at[0], n.normed2.at[1])
    get_wup.wait()
    get_wdown.wait()
    phase("mlp")
    half = FF // 2
    for j in range(FF // D):
        c = slice(j * D, (j + 1) * D)
        n.u[...] = mm(n.normed2[0], n.wup[:, c])
        n.ga[...] = mm(n.ups[0], n.wdown[c, :], NT)

        def gate(t, carry, c=c):
            u = n.u[t, :]
            sig = 1.0 / (1.0 + jnp.exp(-u))
            n.a[t, c] = (u * sig).astype(BF16)
            n.gu[t, c] = (n.ga[t, :] * sig * (1.0 + u * (1.0 - sig))).astype(BF16)
            return carry

        tiles(R, gate, together=8)
    theirs = pl.ds(pl.multiple_of(mate * half, 128), half)
    ours = pl.ds(pl.multiple_of(rp * half, 128), half)
    mate_a = to_mate(4, n.a.at[:, theirs], n.a_p)
    mate_gu = to_mate(5, n.gu.at[:, theirs], n.gu_p)
    phase("mlp back")
    n.tmp[...] = mm(n.gu[...], n.wup[...], NT)

    def keep2(t, gw):
        total = n.ups[0, t, :].astype(F32) + gw
        n.gresid[t, :] = total
        n.gr[t, :] = total.astype(BF16)

    gc2 = norm_back(n.tmp, 8, n.plain2, n.inv2, keep2)
    phase("go")
    n.go[1] = mm(n.gr[...], n.wout[...], NT).astype(BF16)
    side_go = [to_near(2, n.go, c) for c in range(PIECES)]

    def against(t, carry):
        product = n.go[1, t, :].astype(F32) * n.wide_o[t, :]
        for h in range(H):
            n.stat[t, H + h : H + h + 1] = jnp.sum(product[:, h * HD : (h + 1) * HD], axis=-1, keepdims=True)
        return carry

    tiles(R, against, together=8)
    n.stats[1] = n.stat[...].T[0 : 2 * H]
    side_stats = to_sides(3, n.stats)
    quarter = D // 2
    mate_gr = to_mate(6, n.gr.at[:, pl.ds(pl.multiple_of(mate * quarter, 128), quarter)], n.gr_p)
    live = {}
    one_late = sum(rows == after for _, rows, after in z.stages[0]) == 1

    def place_in(p, k):
        return sum(((me >> b) & 1) << i for i, b in enumerate(z.stages[p][k][0]))

    def start_of(p, k):
        return sum(place_in(p, i) * z.stages[p][i][2] for i in range(k) if z.stages[p][i][1] > z.stages[p][i][2])

    def span(p, k):
        rows = z.stages[p][k - 1][2] if k else BLOCK[0]
        return pl.ds(pl.multiple_of(start_of(p, k), rows) if k else 0, rows)

    def partners(p, k):
        over = z.stages[p][k][0]
        for j in range(1, 1 << len(over)):
            yield j, (me ^ sum(1 << b for i, b in enumerate(over) if j >> i & 1), rp)

    def reduce_start(p, k):
        _, rows, after = z.stages[p][k]
        for j, to in partners(p, k):
            if after < rows:
                at = start_of(p, k) + (place_in(p, k) ^ j) * after
                src, ss = n.acc.at[p, pl.ds(pl.multiple_of(at, after), after)], n.sum_ss.at[0]
            else:
                src = n.acc.at[p, span(p, k)]
                ss = n.sum_ss.at[0] if one_late else n.late_ss.at[p, len(z.stages[p]) - 1 - k]
            live[p] = remote(src, getattr(n, f"rcv{k}").at[p, j - 1], ss, n.rs_rs.at[p, k], to)

    def reduce_end(p, k):
        _, rows, after = z.stages[p][k]
        got = getattr(n, f"rcv{k}")
        waits_for(got.at[p], n.rs_rs.at[p, k])
        if after == rows and not one_late:
            live[p].wait_send()
        kept = span(p, k + 1)
        total = n.acc[p, kept].astype(F32)
        for j in range(got.shape[1]):
            total = total + got[p, j].astype(F32)
        into = n.grads_out.at[rp, p, kept] if k + 1 == len(z.stages[p]) else n.acc.at[p, kept]
        into[...] = total.astype(BF16)

    def gather_start(p, k):
        ref = n.grads_out.at[rp, p, span(p, k + 1)]
        for _, to in partners(p, k):
            remote(ref, ref, n.sum_ss.at[0], n.ag_rs.at[p] if k == 0 else n.rs_rs.at[p, k - 1], to)
        if k == 0:
            remote(ref, ref, n.core_ss.at[0], n.core_rs.at[0], (me, mate))

    def gather_end(p, k):
        _, rows, after = z.stages[p][k]
        waits_for(n.grads_out.at[rp, p, pl.ds(0, rows - after)], n.ag_rs.at[p] if k == 0 else n.rs_rs.at[p, k - 1])

    def core_start(p):
        rows = z.stages[p][0][2]
        ref = n.grads_out.at[rp, p, pl.ds(pl.multiple_of((1 - place_in(p, 0)) * rows, rows), rows)]
        remote(ref, ref, n.core_ss.at[0], n.core_rs.at[0], (me, mate))

    steps_left = {}
    for p in range(STREAMS):
        steps = []
        kept = [k for k, stage in enumerate(z.stages[p]) if stage[1] > stage[2]]
        for k in range(len(z.stages[p])):
            steps += [functools.partial(reduce_start, p, k), functools.partial(reduce_end, p, k)]
        for k in reversed(kept):
            steps += [functools.partial(gather_start, p, k), functools.partial(gather_end, p, k)]
        steps += [functools.partial(core_start, p), lambda: None]
        steps_left[p] = steps

    def small_start(k):
        to = (me, mate) if k == 0 else (me ^ (1 << (k - 1)), rp)
        live["gc"] = remote(n.gcs.at[k], n.gcr.at[k], n.gc_ss.at[0], n.gc_rs.at[k], to)

    def small_end(k):
        live["gc"].wait_recv()
        n.gcs[k + 1] = n.gcs[k] + n.gcr[k]

    steps = []
    for k in range(z.bits + 1):
        steps += [functools.partial(small_start, k), functools.partial(small_end, k)]
    steps_left[STREAMS] = steps
    actions = sum_plan(z.bits)

    def service(until=None):
        while actions and (until is None or actions[0][0] <= until):
            phase(f"sums {2 * int(actions[0][0] / 2)}")
            steps_left[actions.pop(0)[1]].pop(0)()

    phase("y")
    y = (n.resid[...] + mm(n.a[...], n.wdown[...])).astype(BF16)
    rows_gone(0, n.out_t)
    set_rows(2, n.place[...], y, n.out_t)
    send_rows(2, n.out_t, n.home_y, 0)
    phase("grad down")
    mate_ups.wait_recv()
    mate_a.wait_recv()
    for j in range(2):
        r = pl.ds(pl.multiple_of(rp * half + j * BLOCK[0], 128), BLOCK[0])
        for i in range(2):
            c = slice(i * BLOCK[1], (i + 1) * BLOCK[1])
            total = mm(n.a[:, r], n.ups[0, :, c], TN) + mm(n.a_p[:, j * BLOCK[0] : (j + 1) * BLOCK[0]], n.ups[1, :, c], TN)
            n.acc[2 * j + i] = total.astype(BF16)
    phase("grad up")
    mate_normed2.wait_recv()
    mate_gu.wait_recv()
    for p in range(len(UP)):
        c = pl.ds(pl.multiple_of(rp * half + p * BLOCK[1], 128), BLOCK[1])
        d = slice(p * BLOCK[1], (p + 1) * BLOCK[1])
        n.acc[UP[p]] = (mm(n.normed2[0], n.gu[:, c], TN) + mm(n.normed2[1], n.gu_p[:, d], TN)).astype(BF16)
    mate_o.wait_recv()
    mate_gr.wait_recv()
    c = pl.ds(pl.multiple_of(rp * quarter, 128), quarter)
    n.acc[OUT[0]] = (mm(n.o[0], n.gr[:, c], TN) + mm(n.o[1], n.gr_p[...], TN)).astype(BF16)

    phase("query back")
    service(2.25)
    for h in range(H):
        head = slice(h * HD, (h + 1) * HD)
        for side in range(3):
            n.s[:, side * R : (side + 1) * R] = mm(n.go[1, :, head], n.qkv[side, :, part(2, h)], NT)

        def soft_back(t, carry, h=h):
            w = n.w[h, t, :].astype(F32)
            gp = n.s[t, :]
            n.low[t, :] = (w * (gp - n.stat[t, H + h : H + h + 1])).astype(BF16)
            return carry

        tiles(R, soft_back, together=8)
        total = jnp.zeros((R, HD), F32)
        for side in range(3):
            total = total + mm(n.low[:, side * R : (side + 1) * R], n.qkv[side, :, part(1, h)])
        n.gqkv[:, part(0, h)] = (total * scale).astype(BF16)
        if h < PIECES:
            hand_on(2, n.go, side_go[PIECES // H * h : PIECES // H * (h + 1)])
        service((3.05, 3.65, 5.15, 6.45)[h])
    service(10.3)

    phase("sums step")
    for copy in side_stats:
        copy.wait_recv()
    phase("far go")
    far_in(2, n.go)
    phase("send y")
    send_rows(2, n.out_t, n.home_y, 1)
    phase("key back")
    for h in range(H):
        head = slice(h * HD, (h + 1) * HD)
        for side in range(3):
            span_q = slice(side * R, (side + 1) * R)
            n.s[:, span_q] = mm(n.qkv[1, :, part(1, h)], n.qkv[side, :, part(0, h)], NT)
            n.s2[:, span_q] = mm(n.qkv[1, :, part(2, h)], n.go[side, :, head], NT)

        def key_back(t, carry, h=h):
            for side in range(3):
                span_q = slice(side * R, (side + 1) * R)
                s = n.s[t, span_q] * (scale * LOG2E) + n.ck[side, t, :]
                w = jnp.exp2(s - n.stats[side, h : h + 1, :])
                n.low[t, span_q] = w.astype(BF16)
                n.low2[t, span_q] = (w * (n.s2[t, span_q] - n.stats[side, H + h : H + h + 1, :])).astype(BF16)
            return carry

        tiles(R, key_back, together=8)
        total_k = jnp.zeros((R, HD), F32)
        total_v = jnp.zeros((R, HD), F32)
        for side in range(3):
            span_q = slice(side * R, (side + 1) * R)
            total_k = total_k + mm(n.low2[:, span_q], n.qkv[side, :, part(0, h)])
            total_v = total_v + mm(n.low[:, span_q], n.go[side, :, head])
        n.gqkv[:, part(1, h)] = (total_k * scale).astype(BF16)
        n.gqkv[:, part(2, h)] = total_v.astype(BF16)
        service(11.05 + 0.6 * h)
    phase("send gqkv")
    wide = 3 * D // 2
    mate_gqkv = to_mate(7, n.gqkv.at[:, pl.ds(pl.multiple_of(mate * wide, 128), wide)], n.gqkv_p)
    phase("gx")
    n.tmp[...] = mm(n.gqkv[...], n.wqkv[...], NT)
    gx_ref = n.tok

    def keep1(t, gw):
        gx_ref[t, :] = (n.gresid[t, :] + gw).astype(BF16)

    gc1 = norm_back(n.tmp, 0, n.plain1, n.inv1, keep1)
    row = lax.broadcasted_iota(I32, (8, D), 0)
    sums = jnp.zeros((8, D), F32)
    for i, value in enumerate((*gc1, *gc2)):
        sums = jnp.where(row == i, value, sums)
    n.gcs[0] = sums

    service(13.7)
    mate_gqkv.wait_recv()
    mate_normed.wait_recv()
    phase("grad qkv")
    for p in range(3):
        c = pl.ds(pl.multiple_of(rp * wide + p * BLOCK[1], 128), BLOCK[1])
        d = slice(p * BLOCK[1], (p + 1) * BLOCK[1])
        n.acc[QKV[p]] = (mm(n.normed[1], n.gqkv[:, c], TN) + mm(n.normed_p[...], n.gqkv_p[:, d], TN)).astype(BF16)
    phase("leave gx")
    service(14.95)
    rows_gone(1, n.out_c)
    set_rows(3, n.place[...], gx_ref[...], n.out_c)
    send_rows(3, n.out_c, n.home_g)
    phase("sums")
    service(50.0)
    phase("home")
    rows_in(2, n.home_y)
    n.y_out[...] = mm(n.pick[...], n.home_y[...]).astype(BF16)
    rows_in(3, n.home_g)
    n.g_out[...] = mm(n.pick[...], n.home_g[...]).astype(BF16)

    service()
    waits_for(n.grads_out.at[mate], n.core_rs.at[0])
    n.sums_out[...] = n.gcs[z.bits + 1]
    phase("end")
    rows_gone(2, n.out_t)
    rows_gone(3, n.out_c)
    for copy in started:
        copy.wait_send()
    blocks = R * (6 * D + FF) // (BLOCK[0] * BLOCK[1])
    waits_for(n.grads_out.at[0, pl.ds(0, blocks)], n.pair_ss.at[0])
    for i, ref in ((1, n.normed), (2, n.go)):
        for leg in range(2):
            waits_for(ref.at[1], n.side_ss.at[i, leg])
    last = z.stages[0][-1][2]
    waits_for(n.grads_out.at[:, :, pl.ds(0, BLOCK[0] - last + (last // 2 if one_late else 0))], n.sum_ss.at[0])
    waits_for(n.grads_out.at[rp], n.core_ss.at[0])
    waits_for(n.gcr, n.gc_ss.at[0])


def lists_of(z, neighbours, me):
    within = neighbours & (z.R - 1)
    shift = (2 * z.R).bit_length() - 1
    away = (neighbours >> shift) - me
    after = (away == 1) | (away == 1 - z.P)
    base = jnp.where(away == 0, z.R, jnp.where(after, 2 * z.R, 0))
    return (base + within).astype(F32)


def finish(z, g_ref, sums_ref, y_ref, gx_ref, ada1_ref, ada2_ref, cond_ref, *rest):
    y_out, gx_out, qkv_out, out_out, up_out, down_out, ga1_out, ga2_out, gcond_out, wide, ga1, ga2, gcond, wide_sem, row_sem = rest
    count = cond_ref.shape[1]
    eye = lax.broadcasted_iota(I32, (count, count), 0) == lax.broadcasted_iota(I32, (count, count), 1)
    cond = jnp.sum(jnp.where(eye, cond_ref[...], 0.0), axis=1, keepdims=True)
    d = z.D
    total = jnp.zeros((count, 1), F32)
    for row, ada, out in ((0, ada1_ref, ga1), (2, ada2_ref, ga2)):
        for j in range(2):
            c = slice(j * d, (j + 1) * d)
            sums = sums_ref[row + j : row + j + 1, :]
            out[:, c] = cond * sums
            total = total + jnp.sum(ada[:, c] * sums, axis=1, keepdims=True)
    gcond[...] = jnp.sum(jnp.where(eye, total, 0.0), axis=0, keepdims=True)
    pairs = ((y_ref, y_out), (gx_ref, gx_out), (ga1, ga1_out), (ga2, ga2_out), (gcond, gcond_out))
    rows = [pltpu.make_async_copy(a, b, row_sem.at[i]) for i, (a, b) in enumerate(pairs)]
    for copy in rows:
        copy.start()
    high, across = BLOCK
    copies = []
    for i in range(2):
        for p in range(STREAMS):
            if p in DOWN:
                r, c, out = 2 * i + p // 2, p % 2, down_out
            elif p in UP:
                r, c, out = 0, len(UP) * i + p - UP[0], up_out
            elif p in OUT:
                r, c, out = 0, i, out_out
            else:
                r, c, out = 0, len(QKV) * i + p - QKV[0], qkv_out
            wide[i, p] = g_ref[i, p].astype(F32)
            to = out.at[r * high : (r + 1) * high, c * across : (c + 1) * across]
            copies.append(pltpu.make_async_copy(wide.at[i, p], to, wide_sem.at[i, p]))
            copies[-1].start()
    for copy in (*copies, *rows):
        copy.wait()


def local(tokens, cotangent, dest, neighbours, w_qkv, w_out, w_up, w_down, ada_attn, ada_mlp, cond):
    rows, width = tokens.shape
    z = sizes(lax.axis_size("patch"), rows, width, w_up.shape[1])
    dest = dest.reshape(1, rows)
    neighbours = neighbours.T
    cond = cond.reshape(1, cond.shape[0])
    inputs = dict(
        tokens=tokens,
        cotangent=cotangent,
        dest=dest,
        neighbours=neighbours,
        w_qkv=w_qkv,
        w_out=w_out,
        w_up=w_up,
        w_down=w_down,
        ada_attn=ada_attn,
        ada_mlp=ada_mlp,
        cond=cond,
    )
    small = ("dest", "neighbours", "cond")
    any_space = pl.BlockSpec(memory_space=pl.ANY)
    vmem = pl.BlockSpec(memory_space=pltpu.VMEM)
    shape = jax.ShapeDtypeStruct
    outs = dict(
        grads_out=pltpu.VMEM((2, STREAMS) + BLOCK, BF16),
        sums_out=pltpu.VMEM((8, width), F32),
        y_out=pltpu.VMEM((rows, width), BF16),
        g_out=pltpu.VMEM((rows, width), BF16),
    )
    held = scratch(z, neighbours.shape[0])
    held_out = pl.pallas_call(
        functools.partial(layer, z, [*inputs, *outs, *held]),
        out_shape=list(outs.values()),
        in_specs=[vmem if k in small else any_space for k in inputs],
        out_specs=[vmem, vmem, vmem, vmem],
        scratch_shapes=list(held.values()),
        compiler_params=pltpu.CompilerParams(collective_id=0, has_side_effects=True, vmem_limit_bytes=56 << 20),
        name="layer",
    )(*inputs.values())

    held_out = [pltpu.with_memory_space_constraint(v, pltpu.VMEM) for v in held_out]
    y, gx, g_qkv, g_out, g_up, g_down, g_ada1, g_ada2, g_cond = pl.pallas_call(
        functools.partial(finish, z),
        in_specs=[vmem] * 7,
        out_specs=[any_space] * 9,
        scratch_shapes=[
            pltpu.VMEM((2, STREAMS) + BLOCK, F32),
            pltpu.VMEM(ada_attn.shape, F32),
            pltpu.VMEM(ada_mlp.shape, F32),
            pltpu.VMEM(cond.shape, F32),
            pltpu.SemaphoreType.DMA((2, STREAMS)),
            pltpu.SemaphoreType.DMA((5,)),
        ],
        out_shape=[
            shape((rows, width), BF16),
            shape((rows, width), BF16),
            shape(w_qkv.shape, F32),
            shape(w_out.shape, F32),
            shape(w_up.shape, F32),
            shape(w_down.shape, F32),
            shape(ada_attn.shape, F32),
            shape(ada_mlp.shape, F32),
            shape(cond.shape, F32),
        ],
        compiler_params=pltpu.CompilerParams(vmem_limit_bytes=32 << 20),
        name="finish",
    )(*held_out, ada_attn, ada_mlp, cond)
    return y, gx, g_qkv, g_out, g_up, g_down, g_ada1, g_ada2, g_cond.reshape(cond.shape[1])


def solution(mesh):
    row = P(("patch", "rep"), None)
    return jax.shard_map(
        local,
        mesh=mesh,
        in_specs=(row, row, P(("patch", "rep")), row) + (P(),) * 7,
        out_specs=(row, row) + (P(),) * 7,
        check_vma=False,
    )
```

```python
import functools
import heapq
import itertools
import types

import jax
import jax.numpy as jnp
from jax import lax
from jax.experimental import pallas as pl
from jax.experimental.pallas import tpu as pltpu
from jax.sharding import PartitionSpec as P

H = 4
HD = 128
EPS = 1e-05
F32 = jnp.float32
BF16 = jnp.bfloat16
I32 = jnp.int32
MESH = pl.DeviceIdType.MESH
NN = (((1,), (0,)), ((), ()))
NT = (((1,), (1,)), ((), ()))
TN = (((0,), (0,)), ((), ()))
TILE = 32
NEVER = -1e30
LOG2E = 1.4426950408889634
BLOCK = (512, 256)
MIN_ROWS = 64


def mm(a, b, dims=NN):
    return lax.dot_general(a, b, dims, preferred_element_type=F32)


def iota(shape, axis):
    return lax.broadcasted_iota(I32, shape, axis).astype(F32)


def hot(cond):
    return jnp.where(cond, 1.0, 0.0)


def sizes(patches, rows, width, hidden):
    cap = rows // patches + 1
    block = -(-(cap - 1) // 16) * 16
    bits = patches.bit_length() - 1
    return types.SimpleNamespace(
        P=patches, R=rows, D=width, FF=hidden, T=block, PT=patches * block, bits=bits, stages=stages_of(bits)
    )


XYZ, XZY, YXZ, YZX, ZXY, ZYX = itertools.permutations(range(3))
ORDERS = [XYZ, ZXY, XYZ, YXZ, XYZ, XZY, YXZ, ZYX, ZYX, XZY, YZX, XYZ]
DOWN, UP, OUT, QKV = range(0, 4), range(4, 8), range(8, 9), range(9, 12)
STREAMS = len(ORDERS)
SUMS_AT, FIRST_AT = (6.4, 8.5, 9.5), (6.4, 2.2, 2.2)
QKV_AT, COEFF_AT = 14.8, 13.6
COMPUTES = ((-1.0, 2.2), (2.3, 3.0), (3.0, 3.6), (3.6, 5.1), (5.1, 6.4), (10.4, 11.0), (11.0, 11.6), (11.6, 12.2))
COMPUTES += ((12.2, 12.8), (12.8, 13.6), (13.6, 14.8), (14.9, 15.4))
ROW_LOADS = ((1.2, (0.0, 1.6, 2.4, 3.2)), (3.0, (3.0, 5.7, 2.9)), (10.5, (3.2, 1.6, 2.4, 3.2)), (15.5, (3.2, 3.2, 4.8, 6.4)))
PIECES = 8


def stages_of(bits):
    found = []
    for first in ORDERS:
        order = [(b,) for b in first if b < bits] + [(b,) for b in range(3, bits)]
        rows, stages = BLOCK[0], []
        for over in order:
            after = rows >> len(over)
            if after < MIN_ROWS:
                after = rows
            stages.append((over, rows, after))
            rows = after
        found.append(stages)
    return found


def sum_plan(bits):
    whole, delay, turn, depth = 5.7, 1.8, 0.12, 3
    steps = []
    for stages in stages_of(bits):
        places = stages + [stage for stage in reversed(stages) if stage[1] > stage[2]]
        steps.append([(over[0], whole * after / BLOCK[0]) for over, _, after in places] + [(None, 0.5)])
    steps.append([(None, 0.1)] + [(b, 0.4) for b in range(bits)])
    at = [0] * len(steps)
    free, queued, waiting, plan = {}, {}, [], []
    number = itertools.count()
    events, begun = [], set()
    for p in range(STREAMS):
        first = ORDERS[p][0]
        begin = QKV_AT if p in QKV else SUMS_AT[first] if first in begun else FIRST_AT[first]
        begun.add(first)
        events.append((begin, next(number), "ready", p))
    events.append((COEFF_AT, next(number), "ready", STREAMS))
    events += [(t, next(number), "rows", times) for t, times in ROW_LOADS]
    heapq.heapify(events)
    now = 0.0

    def able(t):
        return next((b for a, b in COMPUTES if a < t < b), t)

    while events:
        t, _, kind, p = heapq.heappop(events)
        if kind == "rows":
            for link, time in enumerate(p):
                free[link] = max(free.get(link, 0.0), t) + time
            continue
        if kind == "free":
            queued[p] -= 1
            kind = "look"
        if able(max(now, t)) > max(now, t):
            heapq.heappush(events, (able(max(now, t)), next(number), kind, p))
            continue
        now = max(now, t)
        if kind == "ready":
            waiting.append(p)
        elif kind == "end":
            now += turn
            plan.append((now, p))
            at[p] += 1
            if at[p] < len(steps[p]):
                waiting.append(p)
        for q in sorted(waiting, key=lambda q: (q < STREAMS, (q - QKV[0]) % STREAMS)):
            link, time = steps[q][at[q]]
            uses = {None: ()}.get(link, ((2, 1), (3, 2)) if bits == 4 and link == 3 else ((link, 1),))
            if any(queued.get(used, 0) >= depth for used, _ in uses):
                continue
            waiting.remove(q)
            now += 0.03
            plan.append((now, q))
            done = now if uses else now + time
            for used, share in uses:
                queued[used] = queued.get(used, 0) + 1
                free[used] = max(free.get(used, 0.0), now) + time * share
                heapq.heappush(events, (free[used], next(number), "free", used))
                done = max(done, free[used])
            heapq.heappush(events, (done + delay, next(number), "end", q))
    return plan


def scratch(z, nb):
    R, D, FF, PT, PS = z.R, z.D, z.FF, z.PT, z.PT + z.P
    stages = z.stages[0]
    halved = sum(before > after for _, before, after in stages)
    vm, dma = pltpu.VMEM, pltpu.SemaphoreType.DMA
    s = dict(
        dest_in=vm((1, R), I32),
        lists_in=vm((nb, R), I32),
        cond_in=vm((1, 32), F32),
        tok=vm((R, D), BF16),
        cot=vm((R, D), BF16),
        wqkv=vm((D, 3 * D), BF16),
        wout=vm((D, D), BF16),
        wup=vm((D, FF), BF16),
        wdown=vm((FF, D), BF16),
        ada1=vm((32, 2 * D), F32),
        ada2=vm((32, 2 * D), F32),
        c=vm((16, 2 * D), F32),
        pick=vm((R, PS), BF16),
        place=vm((PS, R), BF16),
        out_t=vm((PT, D), BF16),
        out_c=vm((PT, D), BF16),
        in_t=vm((PS, D), BF16),
        in_c=vm((PS, D), BF16),
        home_y=vm((PS, D), BF16),
        home_g=vm((PS, D), BF16),
        more_out=vm((4, z.P, 1, D + 128), F32),
        more_in=vm((4, z.P, 1, D + 128), F32),
        x=vm((R, D), F32),
        plain1=vm((R, D), F32),
        inv1=vm((R, 128), F32),
        plain2=vm((R, D), F32),
        inv2=vm((R, 128), F32),
        resid=vm((R, D), F32),
        gresid=vm((R, D), F32),
        tmp=vm((R, D), F32),
        ups=vm((2, R, D), BF16),
        normed=vm((3, R, D), BF16),
        normed_p=vm((R, D), BF16),
        qkv=vm((3, R, 3 * D), BF16),
        cols=vm((3, nb, R), F32),
        colq=vm((R, nb), F32),
        cq=vm((R, 3 * R), F32),
        ck=vm((3, R, R), F32),
        s=vm((R, 3 * R), F32),
        s2=vm((R, 3 * R), F32),
        w=vm((H, R, 3 * R), BF16),
        low=vm((R, 3 * R), BF16),
        low2=vm((R, 3 * R), BF16),
        o=vm((2, R, D), BF16),
        wide_o=vm((R, D), F32),
        u=vm((R, D), F32),
        ga=vm((R, D), F32),
        a=vm((R, FF), BF16),
        a_p=vm((R, FF // 2), BF16),
        gu=vm((R, FF), BF16),
        gu_p=vm((R, FF // 2), BF16),
        normed2=vm((2, R, D), BF16),
        gr=vm((R, D), BF16),
        gr_p=vm((R, D // 2), BF16),
        go=vm((3, R, D), BF16),
        stat=vm((R, 128), F32),
        stats=vm((3, 2 * H, R), F32),
        gqkv=vm((R, 3 * D), BF16),
        gqkv_p=vm((R, 3 * D // 2), BF16),
        acc=vm((STREAMS,) + BLOCK, BF16),
        **{f"rcv{k}": vm((STREAMS, (1 << len(b)) - 1, n, BLOCK[1]), BF16) for k, (b, _, n) in enumerate(stages)},
        gcs=vm((z.bits + 2, 8, D), F32),
        gcr=vm((z.bits + 1, 8, D), F32),
        load_sem=dma((11,)),
        row_ss=dma((2,)),
        row_rs=dma((4,)),
        own_sem=dma((2,)),
        more_ss=dma((2,)),
        more_rs=dma((4,)),
        more_own=dma((2,)),
        side_ss=dma((4, 2)),
        side_rs=dma((4, 2)),
        piece_rs=dma((2, PIECES)),
        pair_ss=dma((1,)),
        pair_rs=dma((8,)),
        sum_ss=dma((1,)),
        late_ss=dma((STREAMS, len(stages) - halved) if len(stages) > halved + 1 else (1, 1)),
        rs_rs=dma((STREAMS, len(stages))),
        ag_rs=dma((STREAMS,)),
        core_ss=dma((1,)),
        core_rs=dma((1,)),
        gc_ss=dma((1,)),
        gc_rs=dma((z.bits + 1,)),
    )
    return s


def marker():
    def phase(name):
        del name

    return phase


def layer(z, names, *refs):
    n = types.SimpleNamespace(**dict(zip(names, refs, strict=True)))
    Pn, R, D, FF, T, PT, PS = z.P, z.R, z.D, z.FF, z.T, z.PT, z.PT + z.P
    me = lax.axis_index("patch")
    rp = lax.axis_index("rep")
    mate = 1 - rp
    nxt = lax.rem(me + 1, Pn)
    prv = lax.rem(me + Pn - 1, Pn)
    started = []
    phase = marker()

    def tiles(total, fn, init=0, size=TILE, together=1):
        def some(i, carry):
            for j in range(together):
                carry = fn(pl.ds(pl.multiple_of((i * together + j) * size, size), size), carry)
            return carry

        return lax.fori_loop(0, total // (size * together), some, init)

    def load(i, src, dst):
        copy = pltpu.make_async_copy(src, dst, n.load_sem.at[i])
        copy.start()
        return copy

    phase("entry")
    barrier = pltpu.get_barrier_semaphore()

    def greet(i, carry):
        pl.semaphore_signal(barrier, inc=1, device_id=(lax.rem(me + i, Pn), rp), device_id_type=MESH)
        return carry

    lax.fori_loop(1, Pn, greet, 0)
    pl.semaphore_signal(barrier, inc=1, device_id=(me, mate), device_id_type=MESH)
    get_dest = load(8, n.dest, n.dest_in)
    get_tok = load(0, n.tokens, n.tok)
    get_lists = load(9, n.neighbours, n.lists_in)
    get_cond = load(10, n.cond, n.cond_in)
    get_cot = load(1, n.cotangent, n.cot)
    get_ada1 = load(2, n.ada_attn, n.ada1)
    get_ada2 = load(3, n.ada_mlp, n.ada2)
    get_wqkv = load(4, n.w_qkv, n.wqkv)
    get_wdown = load(5, n.w_down, n.wdown)
    get_wout = load(6, n.w_out, n.wout)
    get_wup = load(7, n.w_up, n.wup)

    def remote(src, dst, ss, rs, to, keep=False):
        copy = pltpu.make_async_remote_copy(
            src_ref=src, dst_ref=dst, send_sem=ss, recv_sem=rs, device_id=to, device_id_type=MESH
        )
        copy.start()
        if keep:
            started.append(copy)
        return copy

    def more(ref, i, at):
        return ref.at[i, at] if i == 0 else ref.at[i, at, :, pl.ds(0, D)]

    def send_rows(i, src, dst, odd=None):
        def one(j, carry):
            to = me ^ (Pn - j if odd is None else Pn + odd - 2 * j)
            pltpu.make_async_remote_copy(
                src_ref=src.at[pl.ds(pl.multiple_of(to * T, 16), T)],
                dst_ref=dst.at[pl.ds(pl.multiple_of(me * T, 16), T)],
                send_sem=n.row_ss.at[i % 2],
                recv_sem=n.row_rs.at[i],
                device_id=(to, rp),
                device_id_type=MESH,
            ).start()
            pltpu.make_async_remote_copy(
                src_ref=more(n.more_out, i, to),
                dst_ref=more(n.more_in, i, me),
                send_sem=n.more_ss.at[i % 2],
                recv_sem=n.more_rs.at[i],
                device_id=(to, rp),
                device_id_type=MESH,
            ).start()
            return carry

        lax.fori_loop(1, Pn if odd is None else Pn // 2 + odd, one, 0)
        if odd == 0:
            return
        mine = pl.ds(pl.multiple_of(me * T, 16), T)
        pltpu.make_async_copy(src.at[mine], dst.at[mine], n.own_sem.at[i // 3]).start()
        pltpu.make_async_copy(more(n.more_out, i, me), more(n.more_in, i, me), n.more_own.at[i // 3]).start()

    def waits_for(ref, sem):
        pltpu.make_async_copy(ref, ref, sem).wait()

    def rows_in(i, dst):
        waits_for(more(n.more_in, i, pl.ds(0, Pn - 1)), n.more_rs.at[i])
        waits_for(more(n.more_in, i, 0), n.more_own.at[i // 3])
        waits_for(dst.at[pl.ds(0, PT - T)], n.row_rs.at[i])
        waits_for(dst.at[pl.ds(0, T)], n.own_sem.at[i // 3])
        dst[PT:PS] = n.more_in[i, :, 0, :D].astype(BF16)

    def rows_gone(i, src):
        waits_for(src.at[pl.ds(0, PT - T)], n.row_ss.at[i % 2])
        waits_for(more(n.more_out, i, pl.ds(0, Pn - 1)), n.more_ss.at[i % 2])

    def set_rows(i, hot_rows, values, out):
        total = mm(hot_rows, values)
        out[...] = total[:PT].astype(BF16)
        n.more_out[i, :, 0, :D] = total[PT:]

    even = lax.rem(me, 2) == 0
    near = me ^ 1
    near_slot = jnp.where(even, 2, 0)
    far_slot = 2 - near_slot
    onward = lax.rem(jnp.where(even, me + 2, me + Pn - 2), Pn)

    def to_sides(i, ref):
        return (
            remote(ref.at[1], ref.at[0], n.side_ss.at[i, 0], n.side_rs.at[i, 0], (nxt, rp), True),
            remote(ref.at[1], ref.at[2], n.side_ss.at[i, 1], n.side_rs.at[i, 1], (prv, rp), True),
        )

    def to_near(i, ref, c):
        size = R // PIECES
        return remote(
            ref.at[1, pl.ds(c * size, size)],
            ref.at[far_slot, pl.ds(c * size, size)],
            n.side_ss.at[i, 0],
            n.piece_rs.at[i - 1, c],
            (near, rp),
        )

    def hand_on(i, ref, copies):
        size = R // PIECES
        for copy in copies:
            c = len(handed[i])
            copy.wait_recv()
            handed[i].append(
                remote(
                    ref.at[near_slot, pl.ds(c * size, size)],
                    ref.at[far_slot, pl.ds(c * size, size)],
                    n.side_ss.at[i, 1],
                    n.side_rs.at[i, 1],
                    (onward, rp),
                )
            )

    handed = {1: [], 2: []}

    def far_in(i, ref):
        waits_for(ref.at[far_slot], n.side_rs.at[i, 1])

    def to_mate(i, src, dst):
        return remote(src, dst, n.pair_ss.at[0], n.pair_rs.at[i], (me, mate))

    get_dest.wait()
    dest = n.dest_in[...].astype(F32)
    mine_hot = iota((Pn, R), 0) == dest
    before = hot(iota((R, R), 0) < iota((R, R), 1)).astype(BF16)
    earlier = mm(hot(mine_hot).astype(BF16), before)
    rank = jnp.sum(jnp.where(mine_hot, earlier, 0.0), axis=0, keepdims=True)
    code = jnp.where(rank < T, dest * T + rank, PT + dest)
    pick = hot(code == iota((PS, R), 0))
    pick_low = pick.astype(BF16)
    get_tok.wait()
    set_rows(0, pick_low, n.tok[...], n.out_t)
    n.more_out[0, :, 0, D:] = jnp.broadcast_to(jnp.sum(hot(mine_hot), axis=1, keepdims=True), (Pn, 128))
    get_lists.wait()
    n.cols[1] = lists_of(z, n.lists_in[...], me)
    phase("barrier")
    pl.semaphore_wait(barrier, Pn)
    phase("send tokens")
    side_lists = to_sides(0, n.cols)
    send_rows(0, n.out_t, n.in_t)
    get_cot.wait()
    set_rows(1, pick_low, n.cot[...], n.out_c)
    n.pick[...] = pick.T.astype(BF16)

    phase("counts")
    get_ada1.wait()
    get_ada2.wait()
    get_cond.wait()
    cond = jnp.broadcast_to(n.cond_in[...], (8, n.cond_in.shape[1]))
    n.c[0:8] = jnp.dot(cond, n.ada1[...], precision=lax.Precision.HIGHEST, preferred_element_type=F32)
    n.c[8:16] = jnp.dot(cond, n.ada2[...], precision=lax.Precision.HIGHEST, preferred_element_type=F32)
    n.colq[...] = n.cols[1].T
    lists = n.cols.shape[1]

    def count_q(t, carry):
        ids = iota((TILE, 3 * R), 1)
        col = n.colq[t, :]
        total = jnp.zeros((TILE, 3 * R), F32)
        for j in range(lists):
            total = total + hot(col[:, j : j + 1] == ids)
        n.cq[t, :] = jnp.where(total > 0.0, jnp.log2(total), NEVER)
        return carry

    tiles(R, count_q)

    def count_k(side, base):
        def one(t, carry):
            ids = iota((TILE, R), 0) + (t.start + base).astype(F32)
            total = jnp.zeros((TILE, R), F32)
            for j in range(lists):
                total = total + hot(n.cols[side, j : j + 1, :] == ids)
            n.ck[side, t, :] = jnp.where(total > 0.0, jnp.log2(total), NEVER)
            return carry

        tiles(R, one)

    count_k(1, R)
    phase("side counts")
    for lists_copy in side_lists:
        lists_copy.wait_recv()
    count_k(0, 2 * R)
    count_k(2, 0)

    phase("places")
    row = iota((PS, 1), 0)
    source = jnp.where(row < PT, jnp.floor((row + 0.5) * (1.0 / T)), row - PT)
    step = jnp.where(row < PT, row - source * T, T * 1.0)
    spread = hot(source == iota((PS, Pn), 1)).astype(BF16)
    earlier_sources = hot(iota((Pn, Pn), 0) > iota((Pn, Pn), 1)).astype(BF16)
    phase("wait tokens")
    rows_in(0, n.in_t)
    send_rows(1, n.out_c, n.in_c, 0)
    phase("place rows")
    count = n.more_in[0, :, 0, D:].astype(BF16)
    offset = mm(earlier_sources, count).astype(BF16)
    position = jnp.where(step < mm(spread, count)[:, 0:1], mm(spread, offset)[:, 0:1] + step, -1.0)
    place = hot(position == iota((PS, R), 1))
    n.place[...] = place.astype(BF16)
    place_t = place.T.astype(BF16)
    n.x[...] = mm(place_t, n.in_t[...])

    def norm(src, coeffs, plain_ref, inv_ref, out, after=None):
        def one(t, carry):
            v = src[t, :]
            centred = v - jnp.sum(v, axis=-1, keepdims=True) * (1.0 / D)
            inverse = lax.rsqrt(jnp.sum(centred * centred, axis=-1, keepdims=True) * (1.0 / D) + EPS)
            plain = centred * inverse
            plain_ref[t, :] = plain
            inv_ref[t, :] = jnp.broadcast_to(inverse, (TILE, 128))
            out[t, :] = (plain * (1.0 + n.c[coeffs : coeffs + 1, :D]) + n.c[coeffs : coeffs + 1, D:]).astype(BF16)
            return carry

        for c in range(PIECES):
            size = R // PIECES
            for j in range(size // TILE):
                one(pl.ds(c * size + j * TILE, TILE), 0)
            if after:
                after(c)

    def norm_back(grad, coeffs, plain_ref, inv_ref, finish):
        def one(t, carry):
            g = grad[t, :]
            plain = plain_ref[t, :]
            scaled = g * (1.0 + n.c[coeffs : coeffs + 1, :D])
            mean = jnp.sum(scaled, axis=-1, keepdims=True) * (1.0 / D)
            along = jnp.sum(scaled * plain, axis=-1, keepdims=True) * (1.0 / D)
            finish(t, inv_ref[t, 0:1] * (scaled - mean - plain * along))
            return (
                carry[0] + jnp.sum(g * plain, axis=0, keepdims=True),
                carry[1] + jnp.sum(g, axis=0, keepdims=True),
            )

        zero = jnp.zeros((1, D), F32)
        return tiles(R, one, (zero, zero), together=8)

    phase("norm")
    side_normed = []
    norm(n.x, 0, n.plain1, n.inv1, n.normed.at[1], lambda c: side_normed.append(to_near(1, n.normed, c)))
    mate_normed = to_mate(0, n.normed.at[1], n.normed_p)
    phase("project")
    get_wqkv.wait()

    def project(side):
        for j in range(3):
            c = slice(j * D, (j + 1) * D)
            n.qkv[side, :, c] = mm(n.normed[side], n.wqkv[:, c]).astype(BF16)

    project(1)
    phase("wait halo")
    hand_on(1, n.normed, side_normed)
    send_rows(1, n.out_c, n.in_c, 1)
    project(near_slot)
    phase("wait far")
    far_in(1, n.normed)
    project(far_slot)

    phase("attention")
    scale = 1.0 / HD**0.5

    def part(which, h):
        return slice(which * D + h * HD, which * D + (h + 1) * HD)

    for h in range(H):
        for side in range(3):
            n.s[:, side * R : (side + 1) * R] = mm(n.qkv[1, :, part(0, h)], n.qkv[side, :, part(1, h)], NT)

        def soft(t, carry, h=h):
            s = n.s[t, :] * (scale * LOG2E) + n.cq[t, :]
            top = jnp.max(s, axis=-1, keepdims=True)
            e = jnp.exp2(s - top)
            total = jnp.sum(e, axis=-1, keepdims=True)
            w = e * (1.0 / total)
            n.w[h, t, :] = w.astype(BF16)
            n.stat[t, h : h + 1] = top + jnp.log2(total)
            return carry

        tiles(R, soft, together=8)
        mixed = jnp.zeros((R, HD), F32)
        for side in range(3):
            mixed = mixed + mm(n.w[h, :, side * R : (side + 1) * R], n.qkv[side, :, part(2, h)])
        n.wide_o[:, h * HD : (h + 1) * HD] = mixed
        n.o[0, :, h * HD : (h + 1) * HD] = mixed.astype(BF16)
    mate_o = to_mate(2, n.o.at[0], n.o.at[1])

    phase("wait upstream")
    rows_in(1, n.in_c)
    n.ups[0] = mm(place_t, n.in_c[...]).astype(BF16)
    mate_ups = to_mate(1, n.ups.at[0], n.ups.at[1])
    phase("resid")
    get_wout.wait()
    n.resid[...] = n.x[...] + mm(n.o[0], n.wout[...])
    norm(n.resid, 8, n.plain2, n.inv2, n.normed2.at[0])
    mate_normed2 = to_mate(3, n.normed2.at[0], n.normed2.at[1])
    get_wup.wait()
    get_wdown.wait()
    phase("mlp")
    half = FF // 2
    for j in range(FF // D):
        c = slice(j * D, (j + 1) * D)
        n.u[...] = mm(n.normed2[0], n.wup[:, c])
        n.ga[...] = mm(n.ups[0], n.wdown[c, :], NT)

        def gate(t, carry, c=c):
            u = n.u[t, :]
            sig = 1.0 / (1.0 + jnp.exp(-u))
            n.a[t, c] = (u * sig).astype(BF16)
            n.gu[t, c] = (n.ga[t, :] * sig * (1.0 + u * (1.0 - sig))).astype(BF16)
            return carry

        tiles(R, gate, together=8)
    theirs = pl.ds(pl.multiple_of(mate * half, 128), half)
    ours = pl.ds(pl.multiple_of(rp * half, 128), half)
    mate_a = to_mate(4, n.a.at[:, theirs], n.a_p)
    mate_gu = to_mate(5, n.gu.at[:, theirs], n.gu_p)
    phase("mlp back")
    n.tmp[...] = mm(n.gu[...], n.wup[...], NT)

    def keep2(t, gw):
        total = n.ups[0, t, :].astype(F32) + gw
        n.gresid[t, :] = total
        n.gr[t, :] = total.astype(BF16)

    gc2 = norm_back(n.tmp, 8, n.plain2, n.inv2, keep2)
    phase("go")
    n.go[1] = mm(n.gr[...], n.wout[...], NT).astype(BF16)
    side_go = [to_near(2, n.go, c) for c in range(PIECES)]

    def against(t, carry):
        product = n.go[1, t, :].astype(F32) * n.wide_o[t, :]
        for h in range(H):
            n.stat[t, H + h : H + h + 1] = jnp.sum(product[:, h * HD : (h + 1) * HD], axis=-1, keepdims=True)
        return carry

    tiles(R, against, together=8)
    n.stats[1] = n.stat[...].T[0 : 2 * H]
    side_stats = to_sides(3, n.stats)
    quarter = D // 2
    mate_gr = to_mate(6, n.gr.at[:, pl.ds(pl.multiple_of(mate * quarter, 128), quarter)], n.gr_p)
    live = {}
    one_late = sum(rows == after for _, rows, after in z.stages[0]) == 1

    def place_in(p, k):
        return sum(((me >> b) & 1) << i for i, b in enumerate(z.stages[p][k][0]))

    def start_of(p, k):
        return sum(place_in(p, i) * z.stages[p][i][2] for i in range(k) if z.stages[p][i][1] > z.stages[p][i][2])

    def span(p, k):
        rows = z.stages[p][k - 1][2] if k else BLOCK[0]
        return pl.ds(pl.multiple_of(start_of(p, k), rows) if k else 0, rows)

    def partners(p, k):
        over = z.stages[p][k][0]
        for j in range(1, 1 << len(over)):
            yield j, (me ^ sum(1 << b for i, b in enumerate(over) if j >> i & 1), rp)

    def reduce_start(p, k):
        _, rows, after = z.stages[p][k]
        for j, to in partners(p, k):
            if after < rows:
                at = start_of(p, k) + (place_in(p, k) ^ j) * after
                src, ss = n.acc.at[p, pl.ds(pl.multiple_of(at, after), after)], n.sum_ss.at[0]
            else:
                src = n.acc.at[p, span(p, k)]
                ss = n.sum_ss.at[0] if one_late else n.late_ss.at[p, len(z.stages[p]) - 1 - k]
            live[p] = remote(src, getattr(n, f"rcv{k}").at[p, j - 1], ss, n.rs_rs.at[p, k], to)

    def reduce_end(p, k):
        _, rows, after = z.stages[p][k]
        got = getattr(n, f"rcv{k}")
        waits_for(got.at[p], n.rs_rs.at[p, k])
        if after == rows and not one_late:
            live[p].wait_send()
        kept = span(p, k + 1)
        total = n.acc[p, kept].astype(F32)
        for j in range(got.shape[1]):
            total = total + got[p, j].astype(F32)
        into = n.grads_out.at[rp, p, kept] if k + 1 == len(z.stages[p]) else n.acc.at[p, kept]
        into[...] = total.astype(BF16)

    def gather_start(p, k):
        ref = n.grads_out.at[rp, p, span(p, k + 1)]
        for _, to in partners(p, k):
            remote(ref, ref, n.sum_ss.at[0], n.ag_rs.at[p] if k == 0 else n.rs_rs.at[p, k - 1], to)
        if k == 0:
            remote(ref, ref, n.core_ss.at[0], n.core_rs.at[0], (me, mate))

    def gather_end(p, k):
        _, rows, after = z.stages[p][k]
        waits_for(n.grads_out.at[rp, p, pl.ds(0, rows - after)], n.ag_rs.at[p] if k == 0 else n.rs_rs.at[p, k - 1])

    def core_start(p):
        rows = z.stages[p][0][2]
        ref = n.grads_out.at[rp, p, pl.ds(pl.multiple_of((1 - place_in(p, 0)) * rows, rows), rows)]
        remote(ref, ref, n.core_ss.at[0], n.core_rs.at[0], (me, mate))

    steps_left = {}
    for p in range(STREAMS):
        steps = []
        kept = [k for k, stage in enumerate(z.stages[p]) if stage[1] > stage[2]]
        for k in range(len(z.stages[p])):
            steps += [functools.partial(reduce_start, p, k), functools.partial(reduce_end, p, k)]
        for k in reversed(kept):
            steps += [functools.partial(gather_start, p, k), functools.partial(gather_end, p, k)]
        steps += [functools.partial(core_start, p), lambda: None]
        steps_left[p] = steps

    def small_start(k):
        to = (me, mate) if k == 0 else (me ^ (1 << (k - 1)), rp)
        live["gc"] = remote(n.gcs.at[k], n.gcr.at[k], n.gc_ss.at[0], n.gc_rs.at[k], to)

    def small_end(k):
        live["gc"].wait_recv()
        n.gcs[k + 1] = n.gcs[k] + n.gcr[k]

    steps = []
    for k in range(z.bits + 1):
        steps += [functools.partial(small_start, k), functools.partial(small_end, k)]
    steps_left[STREAMS] = steps
    actions = sum_plan(z.bits)

    def service(until=None):
        while actions and (until is None or actions[0][0] <= until):
            phase(f"sums {2 * int(actions[0][0] / 2)}")
            steps_left[actions.pop(0)[1]].pop(0)()

    phase("y")
    y = (n.resid[...] + mm(n.a[...], n.wdown[...])).astype(BF16)
    rows_gone(0, n.out_t)
    set_rows(2, n.place[...], y, n.out_t)
    send_rows(2, n.out_t, n.home_y, 0)
    phase("grad down")
    mate_ups.wait_recv()
    mate_a.wait_recv()
    for j in range(2):
        r = pl.ds(pl.multiple_of(rp * half + j * BLOCK[0], 128), BLOCK[0])
        for i in range(2):
            c = slice(i * BLOCK[1], (i + 1) * BLOCK[1])
            total = mm(n.a[:, r], n.ups[0, :, c], TN) + mm(n.a_p[:, j * BLOCK[0] : (j + 1) * BLOCK[0]], n.ups[1, :, c], TN)
            n.acc[2 * j + i] = total.astype(BF16)
    phase("grad up")
    mate_normed2.wait_recv()
    mate_gu.wait_recv()
    for p in range(len(UP)):
        c = pl.ds(pl.multiple_of(rp * half + p * BLOCK[1], 128), BLOCK[1])
        d = slice(p * BLOCK[1], (p + 1) * BLOCK[1])
        n.acc[UP[p]] = (mm(n.normed2[0], n.gu[:, c], TN) + mm(n.normed2[1], n.gu_p[:, d], TN)).astype(BF16)
    mate_o.wait_recv()
    mate_gr.wait_recv()
    c = pl.ds(pl.multiple_of(rp * quarter, 128), quarter)
    n.acc[OUT[0]] = (mm(n.o[0], n.gr[:, c], TN) + mm(n.o[1], n.gr_p[...], TN)).astype(BF16)

    phase("query back")
    service(2.25)
    for h in range(H):
        head = slice(h * HD, (h + 1) * HD)
        for side in range(3):
            n.s[:, side * R : (side + 1) * R] = mm(n.go[1, :, head], n.qkv[side, :, part(2, h)], NT)

        def soft_back(t, carry, h=h):
            w = n.w[h, t, :].astype(F32)
            gp = n.s[t, :]
            n.low[t, :] = (w * (gp - n.stat[t, H + h : H + h + 1])).astype(BF16)
            return carry

        tiles(R, soft_back, together=8)
        total = jnp.zeros((R, HD), F32)
        for side in range(3):
            total = total + mm(n.low[:, side * R : (side + 1) * R], n.qkv[side, :, part(1, h)])
        n.gqkv[:, part(0, h)] = (total * scale).astype(BF16)
        if h < PIECES:
            hand_on(2, n.go, side_go[PIECES // H * h : PIECES // H * (h + 1)])
        service((3.05, 3.65, 5.15, 6.45)[h])
    service(10.3)

    phase("sums step")
    for copy in side_stats:
        copy.wait_recv()
    phase("far go")
    far_in(2, n.go)
    phase("send y")
    send_rows(2, n.out_t, n.home_y, 1)
    phase("key back")
    for h in range(H):
        head = slice(h * HD, (h + 1) * HD)
        for side in range(3):
            span_q = slice(side * R, (side + 1) * R)
            n.s[:, span_q] = mm(n.qkv[1, :, part(1, h)], n.qkv[side, :, part(0, h)], NT)
            n.s2[:, span_q] = mm(n.qkv[1, :, part(2, h)], n.go[side, :, head], NT)

        def key_back(t, carry, h=h):
            for side in range(3):
                span_q = slice(side * R, (side + 1) * R)
                s = n.s[t, span_q] * (scale * LOG2E) + n.ck[side, t, :]
                w = jnp.exp2(s - n.stats[side, h : h + 1, :])
                n.low[t, span_q] = w.astype(BF16)
                n.low2[t, span_q] = (w * (n.s2[t, span_q] - n.stats[side, H + h : H + h + 1, :])).astype(BF16)
            return carry

        tiles(R, key_back, together=8)
        total_k = jnp.zeros((R, HD), F32)
        total_v = jnp.zeros((R, HD), F32)
        for side in range(3):
            span_q = slice(side * R, (side + 1) * R)
            total_k = total_k + mm(n.low2[:, span_q], n.qkv[side, :, part(0, h)])
            total_v = total_v + mm(n.low[:, span_q], n.go[side, :, head])
        n.gqkv[:, part(1, h)] = (total_k * scale).astype(BF16)
        n.gqkv[:, part(2, h)] = total_v.astype(BF16)
        service(11.05 + 0.6 * h)
    phase("send gqkv")
    wide = 3 * D // 2
    mate_gqkv = to_mate(7, n.gqkv.at[:, pl.ds(pl.multiple_of(mate * wide, 128), wide)], n.gqkv_p)
    phase("gx")
    n.tmp[...] = mm(n.gqkv[...], n.wqkv[...], NT)
    gx_ref = n.tok

    def keep1(t, gw):
        gx_ref[t, :] = (n.gresid[t, :] + gw).astype(BF16)

    gc1 = norm_back(n.tmp, 0, n.plain1, n.inv1, keep1)
    row = lax.broadcasted_iota(I32, (8, D), 0)
    sums = jnp.zeros((8, D), F32)
    for i, value in enumerate((*gc1, *gc2)):
        sums = jnp.where(row == i, value, sums)
    n.gcs[0] = sums

    service(13.7)
    mate_gqkv.wait_recv()
    mate_normed.wait_recv()
    phase("grad qkv")
    for p in range(3):
        c = pl.ds(pl.multiple_of(rp * wide + p * BLOCK[1], 128), BLOCK[1])
        d = slice(p * BLOCK[1], (p + 1) * BLOCK[1])
        n.acc[QKV[p]] = (mm(n.normed[1], n.gqkv[:, c], TN) + mm(n.normed_p[...], n.gqkv_p[:, d], TN)).astype(BF16)
    phase("leave gx")
    service(14.95)
    rows_gone(1, n.out_c)
    set_rows(3, n.place[...], gx_ref[...], n.out_c)
    send_rows(3, n.out_c, n.home_g)
    phase("sums")
    service(50.0)
    phase("home")
    rows_in(2, n.home_y)
    n.y_out[...] = mm(n.pick[...], n.home_y[...]).astype(BF16)
    rows_in(3, n.home_g)
    n.g_out[...] = mm(n.pick[...], n.home_g[...]).astype(BF16)

    service()
    waits_for(n.grads_out.at[mate], n.core_rs.at[0])
    n.sums_out[...] = n.gcs[z.bits + 1]
    phase("end")
    rows_gone(2, n.out_t)
    rows_gone(3, n.out_c)
    for copy in started:
        copy.wait_send()
    blocks = R * (6 * D + FF) // (BLOCK[0] * BLOCK[1])
    waits_for(n.grads_out.at[0, pl.ds(0, blocks)], n.pair_ss.at[0])
    for i, ref in ((1, n.normed), (2, n.go)):
        for leg in range(2):
            waits_for(ref.at[1], n.side_ss.at[i, leg])
    last = z.stages[0][-1][2]
    waits_for(n.grads_out.at[:, :, pl.ds(0, BLOCK[0] - last + (last // 2 if one_late else 0))], n.sum_ss.at[0])
    waits_for(n.grads_out.at[rp], n.core_ss.at[0])
    waits_for(n.gcr, n.gc_ss.at[0])


def lists_of(z, neighbours, me):
    within = neighbours & (z.R - 1)
    shift = (2 * z.R).bit_length() - 1
    away = (neighbours >> shift) - me
    after = (away == 1) | (away == 1 - z.P)
    base = jnp.where(away == 0, z.R, jnp.where(after, 2 * z.R, 0))
    return (base + within).astype(F32)


def finish(z, g_ref, sums_ref, y_ref, gx_ref, ada1_ref, ada2_ref, cond_ref, *rest):
    y_out, gx_out, qkv_out, out_out, up_out, down_out, ga1_out, ga2_out, gcond_out, wide, ga1, ga2, gcond, wide_sem, row_sem = rest
    count = cond_ref.shape[1]
    eye = lax.broadcasted_iota(I32, (count, count), 0) == lax.broadcasted_iota(I32, (count, count), 1)
    cond = jnp.sum(jnp.where(eye, cond_ref[...], 0.0), axis=1, keepdims=True)
    d = z.D
    total = jnp.zeros((count, 1), F32)
    for row, ada, out in ((0, ada1_ref, ga1), (2, ada2_ref, ga2)):
        for j in range(2):
            c = slice(j * d, (j + 1) * d)
            sums = sums_ref[row + j : row + j + 1, :]
            out[:, c] = cond * sums
            total = total + jnp.sum(ada[:, c] * sums, axis=1, keepdims=True)
    gcond[...] = jnp.sum(jnp.where(eye, total, 0.0), axis=0, keepdims=True)
    pairs = ((y_ref, y_out), (gx_ref, gx_out), (ga1, ga1_out), (ga2, ga2_out), (gcond, gcond_out))
    rows = [pltpu.make_async_copy(a, b, row_sem.at[i]) for i, (a, b) in enumerate(pairs)]
    for copy in rows:
        copy.start()
    high, across = BLOCK
    copies = []
    for i in range(2):
        for p in range(STREAMS):
            if p in DOWN:
                r, c, out = 2 * i + p // 2, p % 2, down_out
            elif p in UP:
                r, c, out = 0, len(UP) * i + p - UP[0], up_out
            elif p in OUT:
                r, c, out = 0, i, out_out
            else:
                r, c, out = 0, len(QKV) * i + p - QKV[0], qkv_out
            wide[i, p] = g_ref[i, p].astype(F32)
            to = out.at[r * high : (r + 1) * high, c * across : (c + 1) * across]
            copies.append(pltpu.make_async_copy(wide.at[i, p], to, wide_sem.at[i, p]))
            copies[-1].start()
    for copy in (*copies, *rows):
        copy.wait()


def local(tokens, cotangent, dest, neighbours, w_qkv, w_out, w_up, w_down, ada_attn, ada_mlp, cond):
    rows, width = tokens.shape
    z = sizes(lax.axis_size("patch"), rows, width, w_up.shape[1])
    dest = dest.reshape(1, rows)
    neighbours = neighbours.T
    cond = cond.reshape(1, cond.shape[0])
    inputs = dict(
        tokens=tokens,
        cotangent=cotangent,
        dest=dest,
        neighbours=neighbours,
        w_qkv=w_qkv,
        w_out=w_out,
        w_up=w_up,
        w_down=w_down,
        ada_attn=ada_attn,
        ada_mlp=ada_mlp,
        cond=cond,
    )
    any_space = pl.BlockSpec(memory_space=pl.ANY)
    vmem = pl.BlockSpec(memory_space=pltpu.VMEM)
    shape = jax.ShapeDtypeStruct
    outs = dict(
        grads_out=pltpu.VMEM((2, STREAMS) + BLOCK, BF16),
        sums_out=pltpu.VMEM((8, width), F32),
        y_out=pltpu.VMEM((rows, width), BF16),
        g_out=pltpu.VMEM((rows, width), BF16),
    )
    held = scratch(z, neighbours.shape[0])
    held_out = pl.pallas_call(
        functools.partial(layer, z, [*inputs, *outs, *held]),
        out_shape=list(outs.values()),
        in_specs=[any_space] * len(inputs),
        out_specs=[vmem, vmem, vmem, vmem],
        scratch_shapes=list(held.values()),
        compiler_params=pltpu.CompilerParams(collective_id=0, has_side_effects=True, vmem_limit_bytes=56 << 20),
        name="layer",
    )(*inputs.values())

    held_out = [pltpu.with_memory_space_constraint(v, pltpu.VMEM) for v in held_out]
    y, gx, g_qkv, g_out, g_up, g_down, g_ada1, g_ada2, g_cond = pl.pallas_call(
        functools.partial(finish, z),
        in_specs=[vmem] * 7,
        out_specs=[any_space] * 9,
        scratch_shapes=[
            pltpu.VMEM((2, STREAMS) + BLOCK, F32),
            pltpu.VMEM(ada_attn.shape, F32),
            pltpu.VMEM(ada_mlp.shape, F32),
            pltpu.VMEM(cond.shape, F32),
            pltpu.SemaphoreType.DMA((2, STREAMS)),
            pltpu.SemaphoreType.DMA((5,)),
        ],
        out_shape=[
            shape((rows, width), BF16),
            shape((rows, width), BF16),
            shape(w_qkv.shape, F32),
            shape(w_out.shape, F32),
            shape(w_up.shape, F32),
            shape(w_down.shape, F32),
            shape(ada_attn.shape, F32),
            shape(ada_mlp.shape, F32),
            shape(cond.shape, F32),
        ],
        compiler_params=pltpu.CompilerParams(vmem_limit_bytes=32 << 20),
        name="finish",
    )(*held_out, ada_attn, ada_mlp, cond)
    return y, gx, g_qkv, g_out, g_up, g_down, g_ada1, g_ada2, g_cond.reshape(cond.shape[1])


def solution(mesh):
    row = P(("patch", "rep"), None)
    return jax.shard_map(
        local,
        mesh=mesh,
        in_specs=(row, row, P(("patch", "rep")), row) + (P(),) * 7,
        out_specs=(row, row) + (P(),) * 7,
        check_vma=False,
    )
```
